32 devices in a mesh: gx: 4 (over z), gy: 4 (over x, core), sa: 2 (over y).
Axes of the slice: x: 2, y: 2, z: 4, core: 2. Of those that a mesh axis runs over, the one named last changes fastest.
Arguments:
- field_now: float32 [160, 256, 512], P('sa', 'gy', 'gx'), may hold values from -1.5 to 1.5
- field_before: float32 [160, 256, 512], P('sa', 'gy', 'gx'), may hold values from -1.5 to 1.5
- source: float32 [160, 256, 512], P('sa', 'gy', 'gx'), may hold values from -0.06 to 0.06
- log_fields: float32 [9, 256, 512], P(None, ('gy', 'sa'), 'gx'), may hold values from -0.15 to 0.15
- weights: float32 [1500], replicated, may hold values from 0.0002 to 0.002
- mean_perm: float32 [], replicated, may hold values from 0.5 to 2
- node_index: int32 [1500, 8], replicated, may hold values from 0 to 6
- mode_index: int32 [160, 8], replicated, may hold values from 0 to 3, as said below
Outputs:
- fresh: float32 [160, 256, 512], P('sa', 'gy', 'gx')
- update: float32 [160, 256, 512], P('sa', 'gy', 'gx')
The draws below stay inside these ranges and needn't reach their ends.
Inputs may be any that keep to these rules, and one draw needn't show every extreme that they name: `node_index`: each entry numbers a point of the list in the first step. `mode_index`: the rows are distinct multi-indices of total degree at most 3.
All inputs are finite; a program needn't handle non-finite values.
Results may differ from the reference program's by a relative error of at most 0.0003.
Values sent between devices are 32-bit elements; how exact they have to be, the bound alone decides.
A program may use at most 128 MiB of HBM per device.

```python
import math
import jax
import jax.numpy as jnp
import numpy as np
from jax import lax

G = 8
P_SIZE = 160
Q = 1500
NX = 512
NY = 256


def multi_indices(germ_count, highest):
    listed = [[]]
    for column in range(germ_count):
        listed = [record + [degree] for record in listed for degree in range(highest + 1) if sum(record) + degree <= highest]
    return np.array(listed, dtype=np.int32)


def draw_mode_index(key, part):
    table = jnp.asarray(multi_indices(G, 3))
    shuffled = jax.random.permutation(jax.random.fold_in(key, 17), table.shape[0])
    return table[shuffled[:P_SIZE]]


def plant(result, rng, least, largest):
    longest = result.shape.index(max(result.shape))
    spots = []
    for shift in (0, 1):
        where = [jax.random.randint(jax.random.fold_in(rng, axis), (), 0, length) for axis, length in enumerate(result.shape)]
        where[longest] = (where[longest] + shift) % result.shape[longest]
        spots.append(tuple(where))
    return result.at[spots[0]].set(least).at[spots[1]].set(largest)


def level_of(rng, extent, cuts, low, top_value):
    gain = 1.0
    for position, parts in cuts:
        heights = jax.random.uniform(jax.random.fold_in(jax.random.fold_in(rng, 6), position), (parts,), jnp.float32, low / len(cuts), top_value / len(cuts))
        gain = gain * jnp.repeat(jnp.exp(heights), extent[position] // parts).reshape((-1,) + (1,) * (len(extent) - 1 - position))
    return gain


def scatter_about(key, extent, spread, reach, split=(), kind=jnp.bfloat16):
    values = jax.random.normal(key, extent, jnp.float32) * spread
    if len(split) > 0:
        values = level_of(key, extent, split, -0.22, 0.18) * values
    return jnp.clip(values, min=-reach, max=reach).astype(kind)


def setup_inputs(seed: int = 0) -> dict:
    streams_of = jax.random.split(jax.random.key(seed), 9)
    field_now = scatter_about(streams_of[0], (P_SIZE, NY, NX), 0.1, 1.5, ((0, 2), (1, 4), (2, 4)), jnp.float32)
    field_before = scatter_about(streams_of[1], (P_SIZE, NY, NX), 0.1, 1.5, ((0, 2), (1, 4), (2, 4)), jnp.float32)
    source = scatter_about(streams_of[2], (P_SIZE, NY, NX), 0.01, 0.06, ((0, 2), (1, 4), (2, 4)), jnp.float32)
    log_fields = jnp.clip(jax.random.uniform(streams_of[3], (G + 1, NY, NX), jnp.float32, -0.15, 0.15) * level_of(streams_of[3], (G + 1, NY, NX), ((1, 8), (2, 4)), -0.4, 0.0), -0.15, 0.15)
    weights = jnp.clip(jnp.exp(jax.random.uniform(streams_of[4], (Q,), jnp.float32, math.log(0.0002), math.log(0.002))), 0.0002, 0.002)
    mean_perm = jnp.clip(jnp.exp(jax.random.uniform(streams_of[5], (), jnp.float32, math.log(0.5), math.log(2.0))), 0.5, 2.0)
    node_index = plant(jax.random.randint(streams_of[6], (Q, G), 0, 7), jax.random.fold_in(streams_of[6], 1), 0, 6).astype(jnp.int32)
    mode_index = draw_mode_index(jax.random.fold_in(streams_of[8], 71), 0)
    return {"field_now": field_now, "field_before": field_before, "source": source, "log_fields": log_fields, "weights": weights, "mean_perm": mean_perm, "node_index": node_index, "mode_index": mode_index}


HIGHEST = lax.Precision.HIGHEST
hermite_points = (0.0, -1.7320508075688772, 1.7320508075688772, -1.355626179974266, 1.355626179974266, -2.8569700138728056, 2.8569700138728056)
storage_rate = 0.0004
relax_weight = 1.6
step_length = 0.3

def node_germs(node_index):
    levels = jnp.arange(len(hermite_points), dtype=jnp.int32)
    picked = (node_index[:, :, None] == levels).astype(jnp.float32)
    points = jnp.asarray(hermite_points, dtype=jnp.float32)
    return lax.optimization_barrier(jnp.sum(picked * points, axis=2))

def chaos_basis(node_index, mode_index):
    germ_values = node_germs(node_index)
    square = germ_values * germ_values
    hermite = jnp.stack([jnp.ones_like(germ_values), germ_values, (square - 1.0) / math.sqrt(2.0), (square * germ_values - 3.0 * germ_values) / math.sqrt(6.0)], axis=2)
    degrees = jnp.arange(4, dtype=jnp.int32)
    values = jnp.ones((node_index.shape[0], mode_index.shape[0]), jnp.float32)
    for column in range(mode_index.shape[1]):
        select = (mode_index[:, column][:, None] == degrees).astype(jnp.float32)
        values = values * jnp.dot(hermite[:, column, :], select.T, precision=HIGHEST)
    return (germ_values, values)

def with_mean(germ_values):
    return jnp.concatenate([jnp.ones((germ_values.shape[0], 1), germ_values.dtype), germ_values], axis=1)

def harmonic(later, earlier):
    return 2.0 * later * earlier / (later + earlier)

def apply_operator(values, log_perm):
    conduct = jnp.exp(log_perm)
    across = harmonic(conduct[:, :, 1:], conduct[:, :, :-1]) * (values[:, :, 1:] - values[:, :, :-1])
    along = harmonic(conduct[:, 1:, :], conduct[:, :-1, :]) * (values[:, 1:, :] - values[:, :-1, :])
    across_div = jnp.pad(across, ((0, 0), (0, 0), (0, 1))) - jnp.pad(across, ((0, 0), (0, 0), (1, 0)))
    along_div = jnp.pad(along, ((0, 0), (0, 1), (0, 0))) - jnp.pad(along, ((0, 0), (1, 0), (0, 0)))
    return storage_rate * values - across_div - along_div

def cosine_matrix(length):
    freq = jnp.arange(length, dtype=jnp.int32)[:, None]
    cells = jnp.arange(length, dtype=jnp.int32)[None, :]
    phase = freq * (2 * cells + 1) % (4 * length)
    angle = phase.astype(jnp.float32) * (math.pi / (2 * length))
    factor = jnp.where(freq == 0, math.sqrt(1.0 / length), math.sqrt(2.0 / length))
    return factor * jnp.cos(angle)

def eigen_values(first, count, length):
    freq = (first + jnp.arange(count, dtype=jnp.int32)).astype(jnp.float32)
    return 2.0 - 2.0 * jnp.cos(freq * (math.pi / length))

def reference(field_now, field_before, source, log_fields, weights, mean_perm, node_index, mode_index):
    germ_values, basis = chaos_basis(node_index, mode_index)
    germ_full = with_mean(germ_values)
    node_block = math.gcd(Q, 50)
    blocks = Q // node_block
    node_items = (basis.reshape(blocks, node_block, P_SIZE), germ_full.reshape(blocks, node_block, G + 1), weights.reshape(blocks, node_block))

    def accumulate(running, node_item):
        basis_part, germ_part, weight_part = node_item
        values = jnp.einsum('qp,pyx->qyx', basis_part, field_now, precision=HIGHEST)
        log_perm = jnp.einsum('qg,gyx->qyx', germ_part, log_fields, precision=HIGHEST)
        applied = apply_operator(values, log_perm)
        running = running + jnp.einsum('qp,qyx->pyx', basis_part * weight_part[:, None], applied, precision=HIGHEST)
        return (running, None)
    galerkin, unused = lax.scan(accumulate, jnp.zeros(field_now.shape, jnp.float32), node_items)
    residual = source - galerkin
    rows_matrix = cosine_matrix(NY)
    cols_matrix = cosine_matrix(NX)
    spectral = jnp.einsum('jy,pyx->pjx', rows_matrix, residual, precision=HIGHEST)
    spectral = jnp.einsum('pjx,kx->pjk', spectral, cols_matrix, precision=HIGHEST)
    spectral = spectral / (storage_rate + mean_perm * (eigen_values(0, NY, NY)[:, None] + eigen_values(0, NX, NX)[None, :]))
    spectral = jnp.einsum('pjk,kx->pjx', spectral, cols_matrix, precision=HIGHEST)
    update = jnp.einsum('jy,pjx->pyx', rows_matrix, spectral, precision=HIGHEST)
    fresh = field_before + relax_weight * (field_now - field_before + step_length * update)
    return (fresh, update)
```

```python
import math

import jax
import jax.numpy as jnp
import numpy as np
from jax import lax
from jax.experimental import pallas as pl
from jax.experimental.pallas import tpu as pltpu
from jax.sharding import PartitionSpec as P


HIGHEST = lax.Precision.HIGHEST
hermite_points = (
    0.0,
    -1.7320508075688772,
    1.7320508075688772,
    -1.355626179974266,
    1.355626179974266,
    -2.8569700138728056,
    2.8569700138728056,
)
storage_rate = 0.0004
relax_weight = 1.6
step_length = 0.3


LANES = 128
NODE_BLOCK = 512
BF16 = jnp.bfloat16


def round_up(value, step):
    return -(-value // step) * step


def split_high(block):
    high = lax.reduce_precision(block, exponent_bits=8, mantissa_bits=7)
    return (high.astype(BF16), (block - high).astype(BF16))


def stacked(block, dim, order, total):
    high, low = split_high(block)
    pieces = [low if kind else high for kind in order]
    joined = jnp.concatenate(pieces, axis=dim)
    widths = [(0, 0)] * joined.ndim
    widths[dim] = (0, total - joined.shape[dim])
    return jnp.pad(joined, widths)


def shifted(last, first, axes):
    count = lax.axis_size(axes)
    forward = [(i, i + 1) for i in range(count - 1)]
    backward = [(target, source) for source, target in forward]
    here = lax.axis_index(axes)
    before = jnp.where(here == 0, first, lax.ppermute(last, axes, forward))
    after = jnp.where(here == count - 1, last, lax.ppermute(first, axes, backward))
    return (before, after)


def dot(left, right):
    return jnp.dot(left, right, preferred_element_type=jnp.float32)


def node_kernel(
    group, basis_ref, germ_ref, weight_ref, field_ref, log_ref, edge_field_ref, edge_log_ref,
    out_ref, edge_ref, value_prev, half_prev, flux_prev,
):
    block, step = pl.program_id(0), pl.program_id(1)
    modes = out_ref.shape[0]

    def at_nodes(field, log_perm):
        return (dot(basis_ref[...], field), jnp.exp(dot(germ_ref[...], log_perm)))

    def flux(later, earlier, half_later, half_earlier):
        return (later - earlier) * pl.reciprocal(half_later + half_earlier)

    def project(applied):
        high = applied.astype(BF16)
        rest = applied - high.astype(jnp.float32)
        middle = rest.astype(BF16)
        low = (rest - middle.astype(jnp.float32)).astype(BF16)
        both = dot(weight_ref[...], high) + dot(weight_ref[...], middle)
        return both[:modes] + both[modes:] + dot(weight_ref[:modes, :], low)

    @pl.when(step == 0)
    def start():
        values, halves = at_nodes(field_ref[:, : 2 * LANES], log_ref[:, : 2 * LANES])
        value_prev[...] = values[:, LANES:]
        half_prev[...] = halves[:, LANES:]
        flux_prev[...] = flux(
            values[:, LANES:], values[:, :LANES], halves[:, LANES:], halves[:, :LANES]
        )
        width = edge_ref.shape[1]
        values, halves = at_nodes(edge_field_ref[...], edge_log_ref[...])
        edge = project(
            flux(values[:, width:], values[:, :width], halves[:, width:], halves[:, :width])
        )

        @pl.when(block == 0)
        def first():
            edge_ref[...] = edge
            out_ref[...] = jnp.zeros_like(out_ref)

        @pl.when(block > 0)
        def later():
            edge_ref[...] += edge

    value, half, flux_up = value_prev[...], half_prev[...], flux_prev[...]
    inside = lax.broadcasted_iota(jnp.int32, value.shape, 1) < LANES - 1
    for pair in range(group // 2):
        ahead = pl.ds(pl.multiple_of((step * group + 2 + 2 * pair) * LANES, LANES), 2 * LANES)
        values, halves = at_nodes(field_ref[:, ahead], log_ref[:, ahead])
        applied = []
        for row in range(2):
            value_next = values[:, row * LANES : (row + 1) * LANES]
            half_next = halves[:, row * LANES : (row + 1) * LANES]
            flux_down = flux(value_next, value, half_next, half)
            across = jnp.where(
                inside,
                flux(
                    pltpu.roll(value, LANES - 1, 1), value, pltpu.roll(half, LANES - 1, 1), half
                ),
                0.0,
            )
            applied.append(
                storage_rate * value - (across - pltpu.roll(across, 1, 1)) - (flux_down - flux_up)
            )
            value, half, flux_up = value_next, half_next, flux_down
        rows = pl.ds(pl.multiple_of((step * group + 2 * pair) * LANES, LANES), 2 * LANES)
        out_ref[:, rows] += project(jnp.concatenate(applied, axis=1))
    value_prev[...] = value
    half_prev[...] = half
    flux_prev[...] = flux_up


def galerkin_product(field, log_fields, germ_full, basis, weights):
    modes, rows, width = field.shape
    nodes = basis.shape[0]
    germs = germ_full.shape[1]
    padded_nodes = round_up(nodes, NODE_BLOCK)
    depth = round_up(3 * modes, LANES)
    log_depth = round_up(3 * (germs + 1), 16)

    both = lambda pick: jnp.concatenate([pick(field), pick(log_fields)], axis=0)
    first_row, last_row = both(lambda a: a[:, 0, :]), both(lambda a: a[:, -1, :])
    first_col, last_col = both(lambda a: a[:, :, 0]), both(lambda a: a[:, :, -1])
    above, below = shifted(last_row, first_row, ("gy", "sa"))
    before, after = shifted(last_col, first_col, "gx")
    edge_width = round_up(2 * rows, LANES)
    fill = jnp.zeros((modes + germs, edge_width - 2 * rows), jnp.float32)
    edges = jnp.concatenate([before, last_col, fill, first_col, after, fill], axis=1)

    def operands(block):
        cells = block.shape[1]
        ones = jnp.ones((1, cells), jnp.float32)
        return (
            stacked(block[:modes], 0, (0, 1, 0), depth),
            stacked(jnp.concatenate([block[modes:], ones]), 0, (0, 1, 0), log_depth),
        )

    def tall(block, lo, hi):
        return jnp.concatenate(
            [above[lo:hi], block.reshape(hi - lo, rows * width), below[lo:hi]], axis=1
        )

    cells = jnp.concatenate(
        [tall(field, 0, modes), tall(log_fields, modes, modes + germs)], axis=0
    )
    field_op, log_op = operands(cells)
    edge_field_op, edge_log_op = operands(edges)
    extend = lambda a: jnp.pad(a, ((0, padded_nodes - nodes), (0, 0)))
    basis_op = stacked(extend(basis), 1, (0, 0, 1), depth)
    log_half = jnp.full((nodes, 1), -math.log(2.0), jnp.float32)
    germ_op = stacked(
        extend(jnp.concatenate([-germ_full, log_half], axis=1)), 1, (0, 0, 1), log_depth
    )
    weight_op = stacked(extend(basis * weights[:, None]).T, 0, (0, 1), 2 * modes)

    group = math.gcd(rows, 8)
    whole = lambda a: pl.BlockSpec(a.shape, lambda q, g: (0, 0))
    carry = pltpu.VMEM((NODE_BLOCK, LANES), jnp.float32)
    galerkin, edge = pl.pallas_call(
        lambda *refs: node_kernel(group, *refs),
        grid=(padded_nodes // NODE_BLOCK, rows // group),
        in_specs=[
            pl.BlockSpec((NODE_BLOCK, depth), lambda q, g: (q, 0)),
            pl.BlockSpec((NODE_BLOCK, log_depth), lambda q, g: (q, 0)),
            pl.BlockSpec((2 * modes, NODE_BLOCK), lambda q, g: (0, q)),
            whole(field_op),
            whole(log_op),
            whole(edge_field_op),
            whole(edge_log_op),
        ],
        out_specs=[
            pl.BlockSpec((modes, rows * width), lambda q, g: (0, 0)),
            pl.BlockSpec((modes, edge_width), lambda q, g: (0, 0)),
        ],
        out_shape=[
            jax.ShapeDtypeStruct((modes, rows * width), jnp.float32),
            jax.ShapeDtypeStruct((modes, edge_width), jnp.float32),
        ],
        scratch_shapes=[carry, carry, carry],
        compiler_params=pltpu.CompilerParams(
            dimension_semantics=("arbitrary", "arbitrary"), vmem_limit_bytes=56 * 1024 * 1024
        ),
    )(basis_op, germ_op, weight_op, field_op, log_op, edge_field_op, edge_log_op)
    place = jnp.arange(width, dtype=jnp.int32)
    return (
        galerkin.reshape(modes, rows, width)
        + jnp.where(place == 0, edge[:, :rows, None], 0.0)
        - jnp.where(place == width - 1, edge[:, rows : 2 * rows, None], 0.0)
    )


def node_germs(node_index):
    levels = jnp.arange(len(hermite_points), dtype=jnp.int32)
    picked = (node_index[:, :, None] == levels).astype(jnp.float32)
    points = jnp.asarray(hermite_points, dtype=jnp.float32)
    return jnp.sum(picked * points, axis=2)


def chaos_basis(node_index, mode_index):
    germ_values = node_germs(node_index)
    square = germ_values * germ_values
    hermite = jnp.stack(
        [
            jnp.ones_like(germ_values),
            germ_values,
            (square - 1.0) / math.sqrt(2.0),
            (square * germ_values - 3.0 * germ_values) / math.sqrt(6.0),
        ],
        axis=2,
    )
    degrees = jnp.arange(4, dtype=jnp.int32)
    values = jnp.ones((node_index.shape[0], mode_index.shape[0]), jnp.float32)
    for column in range(mode_index.shape[1]):
        select = (mode_index[:, column][:, None] == degrees).astype(jnp.float32)
        values = values * jnp.dot(hermite[:, column, :], select.T, precision=HIGHEST)
    return (germ_values, values)


def with_mean(germ_values):
    return jnp.concatenate(
        [jnp.ones((germ_values.shape[0], 1), germ_values.dtype), germ_values], axis=1
    )


def on_device(
    field_now, field_before, source, log_fields, weights, mean_perm, node_index, mode_index
):
    germ_values, basis = chaos_basis(node_index, mode_index)
    germ_full = with_mean(germ_values)
    moved_field = lax.all_to_all(field_now, "sa", split_axis=1, concat_axis=0, tiled=True)
    galerkin = galerkin_product(moved_field, log_fields, germ_full, basis, weights)
    galerkin = lax.all_to_all(galerkin, "sa", split_axis=0, concat_axis=1, tiled=True)
    update = precondition(source - galerkin, mean_perm)
    fresh = field_before + relax_weight * (field_now - field_before + step_length * update)
    return (fresh, update)


def cosine_table(length):
    freq, cells = np.arange(length)[:, None], np.arange(length)[None, :]
    factor = np.where(freq == 0, math.sqrt(1.0 / length), math.sqrt(2.0 / length))
    return factor * np.cos((freq * (2 * cells + 1) % (4 * length)) * (math.pi / (2 * length)))


def flux_table(count, mean_perm, inverse, ends):
    same = jnp.sum(inverse * ends[0] * ends[0], axis=0)
    cross = jnp.sum(inverse * ends[0] * ends[1], axis=0)
    number = np.arange(1, count)
    sines = np.sin((number[:, None] * number[None, :]) % (2 * count) * (math.pi / count))
    pairs = (2.0 / count) * sines[:, :, None] * sines[:, None, :]
    turns = np.cos(number * (math.pi / count))
    shrink = 1.0 / (1.0 / mean_perm + 2.0 * same - 2.0 * cross * turns[:, None].astype(np.float32))
    table = jnp.sum(pairs[:, :, :, None].astype(np.float32) * shrink[:, None, None, :], axis=0)
    return jnp.pad(table, ((1, 1), (0, 0), (0, 0)))


def precondition(residual, mean_perm):
    gy, gx = (lax.axis_size(axis) for axis in ("gy", "gx"))
    modes, rows, width = residual.shape
    f32 = lambda a: jnp.asarray(a.astype(np.float32))
    row_table, col_table, whole_table = (cosine_table(n) for n in (rows, width, gx * width))
    rows_matrix, cols_matrix = f32(row_table), f32(col_table)
    row_ends, col_ends = f32(row_table[:, [0, -1]].T), f32(col_table[:, [0, -1]].T)
    join = f32(np.einsum("kix,lx->kil", whole_table.reshape(-1, gx, width), col_table))
    eigen = lambda count: 2.0 - 2.0 * np.cos(np.arange(count) * (math.pi / count))
    denominator = lambda cols: storage_rate + mean_perm * f32(eigen(rows)[:, None] + cols[None, :])
    inverse = 1.0 / denominator(eigen(width))
    col_flux = flux_table(gx, mean_perm, inverse.T, col_ends[:, :, None])
    row_flux = flux_table(gy, mean_perm, 1.0 / denominator(eigen(gx * width)), row_ends[:, :, None])
    product = lambda spec, *args: jnp.einsum(spec, *args, precision=HIGHEST)

    spectral = product("jy,myx->mjx", rows_matrix, residual)
    spectral = product("mjx,kx->mjk", spectral, cols_matrix)
    alone = spectral * inverse
    at_cols = product("mjk,ck->mcj", alone, col_ends)
    at_rows = product("mjk,cj->mck", alone, row_ends)
    sides = jnp.concatenate([at_cols.reshape(modes, -1), at_rows.reshape(modes, -1)], axis=1)
    part = -(-modes // (gx * gy))
    sides = jnp.pad(sides, ((0, gx * gy * part - modes), (0, 0)))
    swap = lambda a: lax.all_to_all(a, ("gx", "gy"), split_axis=0, concat_axis=0, tiled=True)
    every = swap(sides).reshape(gx, gy, part, -1)

    def col_fluxes(ends):
        jump = ends[1:, :, :, 0] - ends[:-1, :, :, 1]
        return jnp.sum(col_flux[:, :, None, None, :] * jump[None], axis=1)

    at_cols = every[..., : 2 * rows].reshape(gx, gy, part, 2, rows)
    at_rows = every[..., 2 * rows :].reshape(gx, gy, part, 2, width)
    through_cols = col_fluxes(at_cols)
    by_row = inverse * row_ends[:, :, None]
    by_col = inverse * col_ends[:, None, :]
    at_rows = (
        at_rows
        + product("iymj,cjk->iymck", through_cols[1:], by_row) * col_ends[1]
        - product("iymj,cjk->iymck", through_cols[:-1], by_row) * col_ends[0]
    )
    jump = at_rows[:, 1:, :, 0] - at_rows[:, :-1, :, 1]
    jump = product("kil,iyml->ymk", join, jump)
    through_rows = jnp.sum(row_flux[:, :, None, :] * jump[None], axis=1)
    through_rows = product("kil,ymk->iyml", join, through_rows)
    back = product("iymk,cjk->iymcj", through_rows, by_col)
    through_cols = through_cols + col_fluxes(
        back[:, 1:] * row_ends[1] - back[:, :-1] * row_ends[0]
    )
    through = jnp.concatenate(
        [through_cols[:-1], through_cols[1:], through_rows[:, :-1], through_rows[:, 1:]], axis=-1
    )
    through = swap(through.reshape(gx * gy * part, -1))[:modes, None, :]
    left, right = through[..., :rows], through[..., rows : 2 * rows]
    top, bottom = through[..., 2 * rows : -width], through[..., -width:]
    upright = lambda a: jnp.swapaxes(a, 1, 2)
    spectral = spectral + (upright(right) * col_ends[1] - upright(left) * col_ends[0])
    spectral = spectral + (bottom * row_ends[1][:, None] - top * row_ends[0][:, None])
    spectral = spectral * inverse
    columns = product("mjk,kx->mjx", spectral, cols_matrix)
    return product("jy,mjx->myx", rows_matrix, columns)


def solution(mesh):
    return jax.shard_map(
        on_device,
        mesh=mesh,
        in_specs=(
            P("sa", "gy", "gx"),
            P("sa", "gy", "gx"),
            P("sa", "gy", "gx"),
            P(None, ("gy", "sa"), "gx"),
            P(),
            P(),
            P(),
            P(),
        ),
        out_specs=(P("sa", "gy", "gx"), P("sa", "gy", "gx")),
        check_vma=False,
    )
```

```python
import functools
import math

import jax
import jax.numpy as jnp
import numpy as np
from jax import lax
from jax.experimental import pallas as pl
from jax.experimental.pallas import tpu as pltpu
from jax.sharding import PartitionSpec as P


HIGHEST = lax.Precision.HIGHEST
hermite_points = (
    0.0,
    -1.7320508075688772,
    1.7320508075688772,
    -1.355626179974266,
    1.355626179974266,
    -2.8569700138728056,
    2.8569700138728056,
)
storage_rate = 0.0004
relax_weight = 1.6
step_length = 0.3


LANES = 128
NODE_BLOCK = 512
LOG_DEPTH = 16
BF16 = jnp.bfloat16


def round_up(value, step):
    return -(-value // step) * step


def product(left, right):
    return jnp.dot(left, right, preferred_element_type=jnp.float32)


def split_two(block):
    high = block.astype(BF16)
    return (high, (block - high.astype(jnp.float32)).astype(BF16))


def stacked(parts, depth):
    missing = depth - sum(part.shape[0] for part in parts)
    if missing:
        parts = parts + [jnp.zeros((missing,) + parts[0].shape[1:], parts[0].dtype)]
    return jnp.concatenate(parts, axis=0)


def node_kernel(
    sizes, field_ref, log_ref, field_cols_ref, log_cols_ref, germ_ref, degree_ref, weight_ref,
    out_ref,
    lines, log_lines, log_sides, sides, total, line_op, log_op, basis_op, germ_op, weight_op,
    edge, value_prev, half_prev, flux_prev,
    line_send, line_recv, halo_send, side_send, side_recv, log_send, log_recv, out_send, out_recv,
):
    count_x, count_y, shares, group = sizes
    modes, rows, width = field_ref.shape
    own_rows = rows // shares
    every = shares * modes
    below, above = own_rows, own_rows + 1
    blocks = basis_op.shape[0] // NODE_BLOCK
    x, y, share = (lax.axis_index(axis) for axis in ("gx", "gy", "sa"))
    first_y = jnp.logical_and(y == 0, share == 0)
    last_y = jnp.logical_and(y == count_y - 1, share == shares - 1)
    not_first, not_last = jnp.logical_not(first_y), jnp.logical_not(last_y)
    peer = lambda step: lax.rem(share + step, shares)

    def remote(source, target, send, recv, **place):
        return pltpu.make_async_remote_copy(
            src_ref=source, dst_ref=target, send_sem=send, recv_sem=recv,
            device_id=place, device_id_type=pl.DeviceIdType.MESH,
        )

    def arrived(target, recv):
        pltpu.make_async_copy(target, target, recv).wait()

    barrier = pltpu.get_barrier_semaphore()
    greet = lambda **place: pl.semaphore_signal(
        barrier, inc=1, device_id=place, device_id_type=pl.DeviceIdType.MESH
    )
    for step in range(1, shares):
        greet(sa=peer(step))
    conditions = (
        (x > 0, dict(gx=x - 1)), (x < count_x - 1, dict(gx=x + 1)),
        (y > 0, dict(gy=y - 1)), (y < count_y - 1, dict(gy=y + 1)),
    )
    for condition, place in conditions:
        @pl.when(condition)
        def _():
            for step in range(shares):
                greet(sa=peer(step), **place)
    sides_met = sum(condition.astype(jnp.int32) for condition, _ in conditions)
    pl.semaphore_wait(barrier, shares - 1 + shares * sides_met)

    remote_copies = []

    def start(condition, copy):
        remote_copies.append((condition, copy))
        if condition is None:
            copy.start()
        else:
            pl.when(condition)(copy.start)

    row_of = lambda row: field_ref.at[:, row, :]
    flat_next = jnp.where(share == shares - 1, y + 1, y), lax.rem(share + 1, shares)
    flat_last = jnp.where(share == 0, y - 1, y), lax.rem(share + shares - 1, shares)
    log_copies = (
        (not_last, log_ref.at[:, own_rows - 1, :], log_lines.at[1], 0,
         dict(gy=flat_next[0], sa=flat_next[1])),
        (not_first, log_ref.at[:, 0, :], log_lines.at[0], 1,
         dict(gy=flat_last[0], sa=flat_last[1])),
        (x < count_x - 1, log_cols_ref.at[1], log_sides.at[0], 2, dict(gx=x + 1)),
        (x > 0, log_cols_ref.at[0], log_sides.at[1], 3, dict(gx=x - 1)),
    )
    for condition, source, target, slot, place in log_copies:
        start(condition, remote(source, target, log_send.at[slot], log_recv.at[slot], **place))
    start(y > 0, remote(
        row_of(0), lines.at[below, share], halo_send.at[0], line_recv.at[below, share],
        gy=y - 1, sa=jnp.int32(shares - 1),
    ))
    start(y < count_y - 1, remote(
        row_of(rows - 1), lines.at[above, share], halo_send.at[1], line_recv.at[above, share],
        gy=y + 1, sa=jnp.int32(0),
    ))
    for step in range(1, shares):
        to = peer(step)
        start(to > 0, remote(
            row_of(jnp.maximum(to * own_rows - 1, 0)), lines.at[above, share],
            halo_send.at[2 * step], line_recv.at[above, share], sa=to,
        ))
        start(to < shares - 1, remote(
            row_of(jnp.minimum((to + 1) * own_rows, rows - 1)), lines.at[below, share],
            halo_send.at[2 * step + 1], line_recv.at[below, share], sa=to,
        ))
    own_above = pltpu.make_async_copy(
        row_of(jnp.maximum(share * own_rows - 1, 0)), lines.at[above, share],
        line_recv.at[above, share],
    )
    own_below = pltpu.make_async_copy(
        row_of(jnp.minimum((share + 1) * own_rows, rows - 1)), lines.at[below, share],
        line_recv.at[below, share],
    )
    pl.when(share > 0)(own_above.start)
    pl.when(share < shares - 1)(own_below.start)
    for step in range(shares):
        to = peer(step)
        for kind in range(2):
            source = field_cols_ref.at[to, kind]
            if step:
                start(None, remote(
                    source, sides.at[kind, share], side_send.at[step, kind],
                    side_recv.at[kind, share], sa=to,
                ))
            else:
                pltpu.make_async_copy(
                    source, sides.at[kind, share], side_recv.at[kind, share]
                ).start()
        start(x > 0, remote(
            field_cols_ref.at[to, 0], sides.at[2, share], side_send.at[step, 2],
            side_recv.at[2, share], gx=x - 1, sa=to,
        ))
        start(x < count_x - 1, remote(
            field_cols_ref.at[to, 1], sides.at[3, share], side_send.at[step, 3],
            side_recv.at[3, share], gx=x + 1, sa=to,
        ))

    def line_copy(row, step):
        to = peer(step)
        return remote(
            row_of(to * own_rows + row), lines.at[row, share], line_send.at[row, step],
            line_recv.at[row, share], sa=to,
        )

    def send_lines(row, carry):
        for step in range(1, shares):
            line_copy(row, step).start()
        pltpu.make_async_copy(
            row_of(share * own_rows + row), lines.at[row, share], line_recv.at[row, share]
        ).start()
        return carry

    lax.fori_loop(0, own_rows, send_lines, 0)

    weight_op[...] = jnp.zeros_like(weight_op)
    total[...] = jnp.zeros_like(total)

    def make_basis(block, carry):
        lanes = pl.ds(pl.multiple_of(block * LANES, LANES), LANES)
        germs = germ_ref[:, lanes]
        square = germs * germs
        second = (square - 1.0) / math.sqrt(2.0)
        third = (square * germs - 3.0 * germs) / math.sqrt(6.0)
        values = jnp.ones((every, LANES), jnp.float32)
        for germ in range(germs.shape[0]):
            degree = jnp.broadcast_to(degree_ref[:, germ : germ + 1], (every, LANES))
            at = lambda table: jnp.broadcast_to(table[germ : germ + 1, :], (every, LANES))
            values = values * jnp.where(
                degree == 0, 1.0,
                jnp.where(degree == 1, at(germs), jnp.where(degree == 2, at(second), at(third))),
            )
        high, low = split_two(values)
        wide = lambda a: a.astype(jnp.float32)
        stack = stacked([wide(high), wide(high), wide(low)], basis_op.shape[1])
        basis_op[lanes, :] = jnp.transpose(stack).astype(BF16)
        high, low = split_two(values * (2.0 * weight_ref[:, lanes]))
        weight_op[:every, lanes] = high
        weight_op[every:, lanes] = low
        spread = stacked([-jnp.ones((1, LANES), jnp.float32), -germs], LOG_DEPTH)
        high, low = split_two(spread)
        stack = stacked([wide(high), wide(high), wide(low)], LANES)
        germ_op[lanes, :] = jnp.transpose(stack).astype(BF16)
        return carry

    lax.fori_loop(0, basis_op.shape[0] // LANES, make_basis, 0)

    def log_stack(block):
        high, low = split_two(stacked([block], LOG_DEPTH))
        return stacked([high, low, high], LANES)

    def field_stack(block):
        high, low = split_two(block)
        return stacked([high, low, high], line_op.shape[1])

    for condition, _, target, slot, _ in (
        (not_first, None, log_lines.at[1], 0, None), (not_last, None, log_lines.at[0], 1, None),
        (x > 0, None, log_sides.at[0], 2, None), (x < count_x - 1, None, log_sides.at[1], 3, None),
    ):
        @pl.when(condition)
        def _():
            arrived(target, log_recv.at[slot])

    def make_log(row, carry):
        log_op[row] = log_stack(log_ref[:, row, :])
        return carry

    lax.fori_loop(0, own_rows, make_log, 0)
    log_op[below] = log_stack(
        jnp.where(last_y, log_ref[:, own_rows - 1, :], log_lines[0])
    )
    log_op[above] = log_stack(jnp.where(first_y, log_ref[:, 0, :], log_lines[1]))

    def at_nodes(nodes, field, logs):
        return (product(basis_op[nodes, :], field), jnp.exp(product(germ_op[nodes, :], logs)))

    def flux(later, earlier, half_later, half_earlier):
        return (later - earlier) * pl.reciprocal(half_later + half_earlier)

    def project(nodes, applied):
        high = applied.astype(BF16)
        rest = applied - high.astype(jnp.float32)
        middle = rest.astype(BF16)
        low = (rest - middle.astype(jnp.float32)).astype(BF16)
        both = product(weight_op[:, nodes], high) + product(weight_op[:, nodes], middle)
        return both[:every] + both[every:] + product(weight_op[:every, nodes], low)

    node_slice = lambda block: pl.ds(pl.multiple_of(block * NODE_BLOCK, NODE_BLOCK), NODE_BLOCK)

    for kind in range(4):
        condition = (None, None, x < count_x - 1, x > 0)[kind]
        for source in range(shares):
            wait = lambda: arrived(sides.at[kind, source], side_recv.at[kind, source])
            wait() if condition is None else pl.when(condition)(wait)
    flat = lambda ref: ref.reshape(every, LANES)
    side = [flat(sides[kind]) for kind in range(4)]
    log_first, log_last = log_cols_ref[0], log_cols_ref[1]
    before = jnp.where(x == 0, side[0], side[3])
    after = jnp.where(x == count_x - 1, side[1], side[2])
    log_before = jnp.where(x == 0, log_first, log_sides[0])
    log_after = jnp.where(x == count_x - 1, log_last, log_sides[1])

    def beside(low_part, high_part):
        lane = lax.broadcasted_iota(jnp.int32, low_part.shape, 1)
        return jnp.where(lane < own_rows, low_part, pltpu.roll(high_part, own_rows, 1))

    line_op[0, :, :LANES] = field_stack(beside(before, side[1]))
    line_op[0, :, LANES:] = field_stack(beside(side[0], after))
    log_edge = jnp.concatenate(
        [log_stack(beside(log_before, log_last)), log_stack(beside(log_first, log_after))], axis=1
    )
    edge[...] = jnp.zeros_like(edge)

    def make_edge(block, carry):
        nodes = node_slice(block)
        values, halves = at_nodes(nodes, line_op[0], log_edge)
        edge[...] += project(nodes, flux(
            values[:, LANES:], values[:, :LANES], halves[:, LANES:], halves[:, :LANES]
        ))
        return carry

    lax.fori_loop(0, blocks, make_edge, 0)

    def wait_line(row):
        for source in range(shares):
            arrived(lines.at[row, source], line_recv.at[row, source])

    wait_line(0)
    pl.when(not_first)(lambda: wait_line(above))
    line = flat(lines[0])
    line_op[0, :, :LANES] = field_stack(jnp.where(first_y, line, flat(lines[above])))
    line_op[0, :, LANES:] = field_stack(line)

    def begin(block, carry):
        nodes = node_slice(block)
        logs = jnp.concatenate([log_op[above], log_op[0]], axis=1)
        values, halves = at_nodes(nodes, line_op[0], logs)
        value_prev[nodes, :] = values[:, LANES:]
        half_prev[nodes, :] = halves[:, LANES:]
        flux_prev[nodes, :] = flux(
            values[:, LANES:], values[:, :LANES], halves[:, LANES:], halves[:, :LANES]
        )
        return carry

    lax.fori_loop(0, blocks, begin, 0)

    def out_copy(row, step):
        to = peer(step)
        return remote(
            total.at[row, to], out_ref.at[:, share * own_rows + row, :], out_send.at[row, step],
            out_recv.at[row, share], sa=to,
        )

    def own_copy(row):
        return pltpu.make_async_copy(
            total.at[row, share], out_ref.at[:, share * own_rows + row, :],
            out_recv.at[row, share],
        )

    def take_group(index, carry):
        base = index * group
        for ahead in range(1, group + 1):
            row = base + ahead
            if ahead < group:
                wait_line(row)
            else:
                pl.when(jnp.logical_or(row < own_rows, not_last))(lambda: wait_line(row))
            line = flat(lines[row])
            if ahead == group:
                line = jnp.where(
                    jnp.logical_and(row == own_rows, last_y), flat(lines[row - 1]), line
                )
            place = pl.ds((ahead - 1) % 2 * LANES, LANES)
            line_op[(ahead - 1) // 2, :, place] = field_stack(line)

        def take_nodes(block, carry):
            nodes = node_slice(block)
            value, half, flux_up = value_prev[nodes, :], half_prev[nodes, :], flux_prev[nodes, :]
            inside = lax.broadcasted_iota(jnp.int32, value.shape, 1) < LANES - 1
            for pair in range(group // 2):
                row = base + 2 * pair
                logs = jnp.concatenate([log_op[row + 1], log_op[row + 2]], axis=1)
                values, halves = at_nodes(nodes, line_op[pair], logs)
                applied = []
                for here in range(2):
                    value_next = values[:, here * LANES : (here + 1) * LANES]
                    half_next = halves[:, here * LANES : (here + 1) * LANES]
                    flux_down = flux(value_next, value, half_next, half)
                    across = jnp.where(
                        inside,
                        flux(
                            pltpu.roll(value, LANES - 1, 1), value,
                            pltpu.roll(half, LANES - 1, 1), half,
                        ),
                        0.0,
                    )
                    applied.append(
                        (0.5 * storage_rate) * value
                        - (across - pltpu.roll(across, 1, 1)) - (flux_down - flux_up)
                    )
                    value, half, flux_up = value_next, half_next, flux_down
                sums = project(nodes, jnp.concatenate(applied, axis=1))
                parts = sums.reshape(shares, modes, 2 * LANES)
                total[row] += parts[:, :, :LANES]
                total[row + 1] += parts[:, :, LANES:]
            value_prev[nodes, :] = value
            half_prev[nodes, :] = half
            flux_prev[nodes, :] = flux_up
            return carry

        lax.fori_loop(0, blocks, take_nodes, 0)
        lane = lax.broadcasted_iota(jnp.int32, (every, LANES), 1)
        for step in range(group):
            row = base + step
            left = pltpu.roll(edge[...], lax.rem(LANES - row, LANES), 1)
            right = pltpu.roll(edge[...], LANES - 1 - own_rows - row, 1)
            change = jnp.where(lane == 0, left, 0.0) - jnp.where(lane == LANES - 1, right, 0.0)
            total[row] += change.reshape(shares, modes, LANES)
        for step in range(group):
            row = base + step
            for to in range(1, shares):
                out_copy(row, to).start()
            own_copy(row).start()
        return carry

    lax.fori_loop(0, own_rows // group, take_group, 0)

    def finish(row, carry):
        for step in range(1, shares):
            line_copy(row, step).wait_send()
            out_copy(row, step).wait_send()
            source = peer(step)
            arrived(out_ref.at[:, source * own_rows + row, :], out_recv.at[row, source])
        own_copy(row).wait()
        return carry

    lax.fori_loop(0, own_rows, finish, 0)
    for condition, copy in remote_copies:
        if condition is None:
            copy.wait_send()
        else:
            pl.when(condition)(copy.wait_send)


def galerkin_product(field, log_fields, weights, node_index, mode_index):
    modes, rows, width = field.shape
    count_x, count_y, shares = (lax.axis_size(axis) for axis in ("gx", "gy", "sa"))
    padded = round_up(modes, 16)
    grow = lambda a, size, dim: jnp.pad(
        a, [(0, size - a.shape[d] if d == dim else 0) for d in range(a.ndim)]
    )
    field = grow(field, padded, 0)
    own_rows = rows // shares
    nodes = node_index.shape[0]
    all_nodes = round_up(nodes, NODE_BLOCK)
    germs = grow(node_germs(node_index).T, all_nodes, 1)
    degrees = grow(mode_index.reshape(shares, modes, -1), padded, 1).reshape(shares * padded, -1)
    cols = jnp.stack([field[:, :, 0], field[:, :, -1]]).reshape(2, padded, shares, own_rows)
    cols = grow(cols.transpose(2, 0, 1, 3), LANES, 3)
    log_cols = grow(jnp.stack([log_fields[:, :, 0], log_fields[:, :, -1]]), LANES, 2)
    levels = log_fields.shape[0]
    group = math.gcd(own_rows, 8)
    every = shares * padded
    depth = round_up(3 * every, LANES)
    slots = own_rows + 2
    vmem = lambda shape, kind=jnp.float32: pltpu.VMEM(shape, kind)
    dma = lambda *shape: pltpu.SemaphoreType.DMA(shape)
    place = pl.BlockSpec(memory_space=pl.ANY)
    whole = pl.BlockSpec(memory_space=pltpu.VMEM)
    result = pl.pallas_call(
        functools.partial(node_kernel, (count_x, count_y, shares, group)),
        in_specs=[place, whole, place, whole, whole, whole, whole],
        out_specs=place,
        out_shape=jax.ShapeDtypeStruct((padded, rows, width), jnp.float32),
        scratch_shapes=[
            vmem((slots, shares, padded, LANES)),
            vmem((2, levels, LANES)),
            vmem((2, levels, LANES)),
            vmem((4, shares, padded, LANES)),
            vmem((own_rows, shares, padded, LANES)),
            vmem((group // 2, depth, 2 * LANES), BF16),
            vmem((slots, LANES, LANES), BF16),
            vmem((all_nodes, depth), BF16),
            vmem((all_nodes, LANES), BF16),
            vmem((2 * every, all_nodes), BF16),
            vmem((every, LANES)),
            vmem((all_nodes, LANES)),
            vmem((all_nodes, LANES)),
            vmem((all_nodes, LANES)),
            dma(own_rows, shares), dma(slots, shares), dma(2 * shares), dma(shares, 4),
            dma(4, shares), dma(4), dma(4), dma(own_rows, shares), dma(own_rows, shares),
        ],
        compiler_params=pltpu.CompilerParams(
            collective_id=0, has_side_effects=True, vmem_limit_bytes=56 * 1024 * 1024
        ),
    )(
        field, log_fields, cols, log_cols, germs, degrees,
        grow(weights[None, :], all_nodes, 1),
    )
    return result[:modes]


def node_germs(node_index):
    levels = jnp.arange(len(hermite_points), dtype=jnp.int32)
    picked = (node_index[:, :, None] == levels).astype(jnp.float32)
    points = jnp.asarray(hermite_points, dtype=jnp.float32)
    return jnp.sum(picked * points, axis=2)


def on_device(
    field_now, field_before, source, log_fields, weights, mean_perm, node_index, mode_index
):
    galerkin = galerkin_product(field_now, log_fields, weights, node_index, mode_index)
    update = precondition(source - galerkin, mean_perm)
    fresh = field_before + relax_weight * (field_now - field_before + step_length * update)
    return (fresh, update)


def cosine_table(length):
    freq, cells = np.arange(length)[:, None], np.arange(length)[None, :]
    factor = np.where(freq == 0, math.sqrt(1.0 / length), math.sqrt(2.0 / length))
    return factor * np.cos((freq * (2 * cells + 1) % (4 * length)) * (math.pi / (2 * length)))


def flux_table(count, mean_perm, inverse, ends):
    same = jnp.sum(inverse * ends[0] * ends[0], axis=0)
    cross = jnp.sum(inverse * ends[0] * ends[1], axis=0)
    number = np.arange(1, count)
    sines = np.sin((number[:, None] * number[None, :]) % (2 * count) * (math.pi / count))
    pairs = (2.0 / count) * sines[:, :, None] * sines[:, None, :]
    turns = np.cos(number * (math.pi / count))
    shrink = 1.0 / (1.0 / mean_perm + 2.0 * same - 2.0 * cross * turns[:, None].astype(np.float32))
    table = jnp.sum(pairs[:, :, :, None].astype(np.float32) * shrink[:, None, None, :], axis=0)
    return jnp.pad(table, ((1, 1), (0, 0), (0, 0)))


def precondition(residual, mean_perm):
    gy, gx = (lax.axis_size(axis) for axis in ("gy", "gx"))
    modes, rows, width = residual.shape
    f32 = lambda a: jnp.asarray(a.astype(np.float32))
    row_table, col_table, whole_table = (cosine_table(n) for n in (rows, width, gx * width))
    rows_matrix, cols_matrix = f32(row_table), f32(col_table)
    row_ends, col_ends = f32(row_table[:, [0, -1]].T), f32(col_table[:, [0, -1]].T)
    join = f32(np.einsum("kix,lx->kil", whole_table.reshape(-1, gx, width), col_table))
    eigen = lambda count: 2.0 - 2.0 * np.cos(np.arange(count) * (math.pi / count))
    denominator = lambda cols: storage_rate + mean_perm * f32(eigen(rows)[:, None] + cols[None, :])
    inverse = 1.0 / denominator(eigen(width))
    col_flux = flux_table(gx, mean_perm, inverse.T, col_ends[:, :, None])
    row_flux = flux_table(gy, mean_perm, 1.0 / denominator(eigen(gx * width)), row_ends[:, :, None])
    mix = lambda spec, *args: jnp.einsum(spec, *args, precision=HIGHEST)

    spectral = mix("jy,myx->mjx", rows_matrix, residual)
    spectral = mix("mjx,kx->mjk", spectral, cols_matrix)
    alone = spectral * inverse
    at_cols = mix("mjk,ck->mcj", alone, col_ends)
    at_rows = mix("mjk,cj->mck", alone, row_ends)
    sides = jnp.concatenate([at_cols.reshape(modes, -1), at_rows.reshape(modes, -1)], axis=1)
    part = -(-modes // (gx * gy))
    sides = jnp.pad(sides, ((0, gx * gy * part - modes), (0, 0)))
    swap = lambda a: lax.all_to_all(a, ("gx", "gy"), split_axis=0, concat_axis=0, tiled=True)
    every = swap(sides).reshape(gx, gy, part, -1)

    def col_fluxes(ends):
        jump = ends[1:, :, :, 0] - ends[:-1, :, :, 1]
        return jnp.sum(col_flux[:, :, None, None, :] * jump[None], axis=1)

    at_cols = every[..., : 2 * rows].reshape(gx, gy, part, 2, rows)
    at_rows = every[..., 2 * rows :].reshape(gx, gy, part, 2, width)
    through_cols = col_fluxes(at_cols)
    by_row = inverse * row_ends[:, :, None]
    by_col = inverse * col_ends[:, None, :]
    at_rows = (
        at_rows
        + mix("iymj,cjk->iymck", through_cols[1:], by_row) * col_ends[1]
        - mix("iymj,cjk->iymck", through_cols[:-1], by_row) * col_ends[0]
    )
    jump = at_rows[:, 1:, :, 0] - at_rows[:, :-1, :, 1]
    jump = mix("kil,iyml->ymk", join, jump)
    through_rows = jnp.sum(row_flux[:, :, None, :] * jump[None], axis=1)
    through_rows = mix("kil,ymk->iyml", join, through_rows)
    back = mix("iymk,cjk->iymcj", through_rows, by_col)
    through_cols = through_cols + col_fluxes(
        back[:, 1:] * row_ends[1] - back[:, :-1] * row_ends[0]
    )
    through = jnp.concatenate(
        [through_cols[:-1], through_cols[1:], through_rows[:, :-1], through_rows[:, 1:]], axis=-1
    )
    through = swap(through.reshape(gx * gy * part, -1))[:modes, None, :]
    left, right = through[..., :rows], through[..., rows : 2 * rows]
    top, bottom = through[..., 2 * rows : -width], through[..., -width:]
    upright = lambda a: jnp.swapaxes(a, 1, 2)
    spectral = spectral + (upright(right) * col_ends[1] - upright(left) * col_ends[0])
    spectral = spectral + (bottom * row_ends[1][:, None] - top * row_ends[0][:, None])
    spectral = spectral * inverse
    columns = mix("mjk,kx->mjx", spectral, cols_matrix)
    return mix("jy,mjx->myx", rows_matrix, columns)


def solution(mesh):
    return jax.shard_map(
        on_device,
        mesh=mesh,
        in_specs=(
            P("sa", "gy", "gx"),
            P("sa", "gy", "gx"),
            P("sa", "gy", "gx"),
            P(None, ("gy", "sa"), "gx"),
            P(),
            P(),
            P(),
            P(),
        ),
        out_specs=(P("sa", "gy", "gx"), P("sa", "gy", "gx")),
        check_vma=False,
    )
```

```python
import functools
import math

import jax
import jax.numpy as jnp
import numpy as np
from jax import lax
from jax.experimental import pallas as pl
from jax.experimental.pallas import tpu as pltpu
from jax.sharding import PartitionSpec as P


HIGHEST = lax.Precision.HIGHEST
hermite_points = (
    0.0,
    -1.7320508075688772,
    1.7320508075688772,
    -1.355626179974266,
    1.355626179974266,
    -2.8569700138728056,
    2.8569700138728056,
)
storage_rate = 0.0004
relax_weight = 1.6
step_length = 0.3


LANES = 128
NODE_BLOCK = 512
LOG_DEPTH = 16
BF16 = jnp.bfloat16


def round_up(value, step):
    return -(-value // step) * step


def product(left, right):
    return jnp.dot(left, right, preferred_element_type=jnp.float32)


def split_two(block):
    high = block.astype(BF16)
    return (high, (block - high.astype(jnp.float32)).astype(BF16))


def split_three(block):
    high = block.astype(BF16)
    rest = block - high.astype(jnp.float32)
    middle = rest.astype(BF16)
    return (high, middle, (rest - middle.astype(jnp.float32)).astype(BF16))


def exact(left, right):
    return jnp.dot(left, right, precision=HIGHEST, preferred_element_type=jnp.float32)


def row_transform(block, pair_ref, rest_ref):
    high, middle, low = split_three(block)
    both = product(jnp.concatenate([high, middle], axis=1), pair_ref[...])
    both = both[:, :LANES] + both[:, LANES:]
    return both + product(jnp.concatenate([low, high], axis=1), rest_ref[...])


def col_transform(block, all_ref):
    high, middle, low = split_three(block)
    stack = jnp.concatenate([high, middle, high, middle, low, high], axis=0)
    return product(all_ref[...], stack)


def make_tables(sizes, per, mean, lane_ref, column_ref, far_ref, inverse, by_row, by_col, col_table, row_table):
    count_x, count_y = sizes
    half = LANES // 2
    column = lambda k, rows=LANES: jnp.broadcast_to(column_ref[:rows, k : k + 1], (rows, LANES))
    lanes = lambda k: lane_ref[k : k + 1, :]
    upright = 1.0 / (storage_rate + mean * (column(0) + lanes(5)))
    flat = 1.0 / (storage_rate + mean * (column(3) + lanes(2)))
    inverse[:, :LANES] = flat[:half]
    inverse[:, LANES:] = flat[:half]
    lane = lax.broadcasted_iota(jnp.int32, (LANES, LANES), 1)
    row = lax.broadcasted_iota(jnp.int32, (LANES, LANES), 0)
    for end in range(2):
        part = upright * column(1 + end)
        by_col[:LANES, end * LANES : (end + 1) * LANES] = jnp.where(lane < half, part, 0.0)
        by_col[LANES:, end * LANES : (end + 1) * LANES] = jnp.where(lane < half, 0.0, part)
        part = flat * column(4 + end)
        by_row[:, 2 * end * LANES : (2 * end + 1) * LANES] = jnp.where(row < half, part, 0.0)
        by_row[:, (2 * end + 1) * LANES : (2 * end + 2) * LANES] = jnp.where(row < half, 0.0, part)

    def tables(count, same, cross):
        shrink = [
            1.0 / (1.0 / mean + 2.0 * same - 2.0 * math.cos(n * math.pi / count) * cross)
            for n in range(1, count)
        ]
        sine = lambda a, b: math.sin(a * b % (2 * count) * math.pi / count)
        return [
            [
                sum((2.0 / count) * sine(n, a) * sine(n, b) * shrink[n - 1] for n in range(1, count))
                for b in range(1, count)
            ]
            for a in range(1, count)
        ]

    total = lambda a: jnp.sum(a, axis=0, keepdims=True)
    ends = column(1), column(2)
    found = tables(
        count_x, total(upright * ends[0] * ends[0]), total(upright * ends[0] * ends[1])
    )
    for a in range(count_x - 1):
        for b in range(count_x - 1):
            col_table[a, b : b + 1, :] = found[a][b]
    far = far_ref[0:1, :]
    wide = lambda k: jnp.broadcast_to(column_ref[:half, k : k + 1], (half, far.shape[1]))
    deep = 1.0 / (storage_rate + mean * (wide(3) + far))
    found = tables(
        count_y, total(deep * wide(4) * wide(4)), total(deep * wide(4) * wide(5))
    )
    depth = row_table.shape[1]
    where_row = lax.broadcasted_iota(jnp.int32, (depth, far.shape[1]), 0) // per
    for shift in range(-(count_y - 2), count_y - 1):
        table = jnp.zeros((depth, far.shape[1]), jnp.float32)
        for a in range(count_y - 1):
            if 0 <= a + shift < count_y - 1:
                table = jnp.where(where_row == a, found[a][a + shift], table)
        row_table[shift + count_y - 2] = table


def solve_fluxes(sizes, per, got, back, lane_ref, join_ref, by_row, by_col, col_table, row_table):
    count_x, count_y = sizes
    depth = row_table.shape[1]
    rows = count_y * per
    lanes = lambda k: lane_ref[k : k + 1, :]
    take = lambda block, kind: got[pl.ds(block * rows * 8 + kind, depth, stride=8), :]
    row = lax.broadcasted_iota(jnp.int32, (depth, LANES), 0)
    up = lambda a, by=1: pltpu.roll(a, (-by * per) % depth, 0)
    down = lambda a: jnp.where(row < per, 0.0, pltpu.roll(a, per, 0))
    blocks, cuts = range(count_x), range(1, count_x)

    def through_cols(first, last):
        jump = [first[cut] - last[cut - 1] for cut in cuts]
        return [
            sum(col_table[a, b : b + 1, :] * jump[b] for b in range(count_x - 1))
            for a in range(count_x - 1)
        ]

    fluxes = through_cols([take(b, 0) for b in blocks], [take(b, 1) for b in blocks])
    spread = [exact(flux, by_row[...]) for flux in fluxes]

    def at_row(block, end, half):
        part = slice((2 * end + half) * LANES, (2 * end + half + 1) * LANES)
        value = take(block, 2 + 2 * end + half)
        if block < count_x - 1:
            value = value + spread[block][:, part] * lanes(1)
        if block > 0:
            value = value - spread[block - 1][:, part] * lanes(0)
        return value

    jump = jnp.concatenate(
        [
            jnp.concatenate([up(at_row(b, 0, half)) - at_row(b, 1, half) for b in blocks], axis=1)
            for half in range(2)
        ],
        axis=0,
    )
    far = lax.dot_general(
        jump, join_ref[...], (((1,), (1,)), ((), ())), precision=HIGHEST,
        preferred_element_type=jnp.float32,
    )
    mixed = []
    for half in range(2):
        part = far[half * depth : (half + 1) * depth]
        mixed.append(sum(
            row_table[shift + count_y - 2] * (up(part, shift) if shift else part)
            for shift in range(-(count_y - 2), count_y - 1)
        ))
    near = exact(jnp.concatenate(mixed, axis=0), join_ref[...])
    through_rows = [
        [near[half * depth : (half + 1) * depth, b * LANES : (b + 1) * LANES] for half in range(2)]
        for b in blocks
    ]
    ends = []
    for b in blocks:
        reach = exact(jnp.concatenate(through_rows[b], axis=1), by_col[...])
        ends.append([
            lanes(4) * reach[:, end * LANES : (end + 1) * LANES]
            - lanes(3) * down(reach[:, end * LANES : (end + 1) * LANES])
            for end in range(2)
        ])
    more = through_cols([end[0] for end in ends], [end[1] for end in ends])
    fluxes = [a + b for a, b in zip(fluxes, more)]
    nothing = jnp.zeros((depth, LANES), jnp.float32)
    for b in blocks:
        left = fluxes[b - 1] if b > 0 else nothing
        right = fluxes[b] if b < count_x - 1 else nothing
        top = [down(part) for part in through_rows[b]]
        for kind, value in enumerate([left, right] + top + through_rows[b]):
            back[pl.ds(b * rows * 8 + kind, depth, stride=8), :] = value


def stacked(parts, depth):
    missing = depth - sum(part.shape[0] for part in parts)
    if missing:
        parts = parts + [jnp.zeros((missing,) + parts[0].shape[1:], parts[0].dtype)]
    return jnp.concatenate(parts, axis=0)


def node_kernel(
    sizes, field_ref, log_ref, field_cols_ref, log_cols_ref, germ_ref, degree_ref, weight_ref,
    source_ref, mean_ref, pair_ref, rest_ref, all_ref, lane_ref, column_ref, far_ref, join_ref,
    spec_ref, flux_ref,
    lines, log_lines, log_sides, sides, total, line_op, log_op, basis_op, germ_op, weight_op,
    edge, value_prev, half_prev, flux_prev,
    home, spectrum, origin, traces, got, back, tall, join,
    inverse, by_row, by_col, col_table, row_table,
    load_sem, spec_sem, trace_send, trace_recv, flux_send, flux_recv,
    line_send, line_recv, halo_send, side_send, side_recv, log_send, log_recv, out_send, out_recv,
):
    count_x, count_y, shares, group = sizes
    modes, rows, width = field_ref.shape
    own_rows = rows // shares
    every = shares * modes
    below, above = own_rows, own_rows + 1
    blocks = basis_op.shape[0] // NODE_BLOCK
    x, y, share = (lax.axis_index(axis) for axis in ("gx", "gy", "sa"))
    first_y = jnp.logical_and(y == 0, share == 0)
    last_y = jnp.logical_and(y == count_y - 1, share == shares - 1)
    not_first, not_last = jnp.logical_not(first_y), jnp.logical_not(last_y)
    peer = lambda step: lax.rem(share + step, shares)

    def remote(source, target, send, recv, **place):
        return pltpu.make_async_remote_copy(
            src_ref=source, dst_ref=target, send_sem=send, recv_sem=recv,
            device_id=place, device_id_type=pl.DeviceIdType.MESH,
        )

    def arrived(target, recv):
        pltpu.make_async_copy(target, target, recv).wait()

    barrier = pltpu.get_barrier_semaphore()
    greet = lambda **place: pl.semaphore_signal(
        barrier, inc=1, device_id=place, device_id_type=pl.DeviceIdType.MESH
    )
    for step in range(1, shares):
        greet(sa=peer(step))
    owners = count_x * count_y
    me = x * count_y + y
    other = lambda step: lax.rem(me + step, owners)
    at_owner = lambda owner: dict(gx=lax.div(owner, count_y), gy=lax.rem(owner, count_y))
    for step in range(1, owners):
        greet(**at_owner(other(step)))
    conditions = (
        (x > 0, dict(gx=x - 1)), (x < count_x - 1, dict(gx=x + 1)),
        (y > 0, dict(gy=y - 1)), (y < count_y - 1, dict(gy=y + 1)),
    )
    for condition, place in conditions:
        @pl.when(condition)
        def _():
            for step in range(1, shares):
                greet(sa=peer(step), **place)
    sides_met = sum(condition.astype(jnp.int32) for condition, _ in conditions)
    pl.semaphore_wait(barrier, owners - 1 + (shares - 1) * (1 + sides_met))

    remote_copies = []

    def start(condition, copy):
        remote_copies.append((condition, copy))
        if condition is None:
            copy.start()
        else:
            pl.when(condition)(copy.start)

    row_of = lambda row: field_ref.at[:, row, :]
    flat_next = jnp.where(share == shares - 1, y + 1, y), lax.rem(share + 1, shares)
    flat_last = jnp.where(share == 0, y - 1, y), lax.rem(share + shares - 1, shares)
    log_copies = (
        (not_last, log_ref.at[:, own_rows - 1, :], log_lines.at[1], 0,
         dict(gy=flat_next[0], sa=flat_next[1])),
        (not_first, log_ref.at[:, 0, :], log_lines.at[0], 1,
         dict(gy=flat_last[0], sa=flat_last[1])),
        (x < count_x - 1, log_cols_ref.at[1], log_sides.at[0], 2, dict(gx=x + 1)),
        (x > 0, log_cols_ref.at[0], log_sides.at[1], 3, dict(gx=x - 1)),
    )
    for condition, source, target, slot, place in log_copies:
        start(condition, remote(source, target, log_send.at[slot], log_recv.at[slot], **place))
    start(y > 0, remote(
        row_of(0), lines.at[below, share], halo_send.at[0], line_recv.at[below, share],
        gy=y - 1, sa=jnp.int32(shares - 1),
    ))
    start(y < count_y - 1, remote(
        row_of(rows - 1), lines.at[above, share], halo_send.at[1], line_recv.at[above, share],
        gy=y + 1, sa=jnp.int32(0),
    ))
    for step in range(1, shares):
        to = peer(step)
        start(to > 0, remote(
            row_of(jnp.maximum(to * own_rows - 1, 0)), lines.at[above, share],
            halo_send.at[2 * step], line_recv.at[above, share], sa=to,
        ))
        start(to < shares - 1, remote(
            row_of(jnp.minimum((to + 1) * own_rows, rows - 1)), lines.at[below, share],
            halo_send.at[2 * step + 1], line_recv.at[below, share], sa=to,
        ))
    own_above = pltpu.make_async_copy(
        row_of(jnp.maximum(share * own_rows - 1, 0)), lines.at[above, share],
        line_recv.at[above, share],
    )
    own_below = pltpu.make_async_copy(
        row_of(jnp.minimum((share + 1) * own_rows, rows - 1)), lines.at[below, share],
        line_recv.at[below, share],
    )
    pl.when(share > 0)(own_above.start)
    pl.when(share < shares - 1)(own_below.start)
    for step in range(shares):
        to = peer(step)
        for kind in range(2):
            source = field_cols_ref.at[to, kind]
            if step:
                start(None, remote(
                    source, sides.at[kind, share], side_send.at[step, kind],
                    side_recv.at[kind, share], sa=to,
                ))
            else:
                pltpu.make_async_copy(
                    source, sides.at[kind, share], side_recv.at[kind, share]
                ).start()
        start(x > 0, remote(
            field_cols_ref.at[to, 0], sides.at[2, share], side_send.at[step, 2],
            side_recv.at[2, share], gx=x - 1, sa=to,
        ))
        start(x < count_x - 1, remote(
            field_cols_ref.at[to, 1], sides.at[3, share], side_send.at[step, 3],
            side_recv.at[3, share], gx=x + 1, sa=to,
        ))

    def line_copy(row, step):
        to = peer(step)
        return remote(
            row_of(to * own_rows + row), lines.at[row, share], line_send.at[row, step],
            line_recv.at[row, share], sa=to,
        )

    def send_lines(row, carry):
        for step in range(1, shares):
            line_copy(row, step).start()
        pltpu.make_async_copy(
            row_of(share * own_rows + row), lines.at[row, share], line_recv.at[row, share]
        ).start()
        return carry

    lax.fori_loop(0, own_rows, send_lines, 0)
    load_origin = pltpu.make_async_copy(source_ref, origin, load_sem.at[0])
    load_origin.start()
    load_join = pltpu.make_async_copy(join_ref, join, load_sem.at[1])
    load_join.start()
    pairs = modes // 2
    per = traces.shape[0] // 8 // owners
    plane = (count_x, count_y)
    beyond = got.shape[0] - traces.shape[0]
    if beyond:
        got[traces.shape[0] :, :] = jnp.zeros((beyond, LANES), jnp.float32)
    traces[...] = jnp.zeros_like(traces)
    make_tables(
        plane, per, mean_ref[0], lane_ref, column_ref, far_ref,
        inverse, by_row, by_col, col_table, row_table,
    )

    weight_op[...] = jnp.zeros_like(weight_op)
    total[...] = jnp.zeros_like(total)

    def make_basis(block, carry):
        lanes = pl.ds(pl.multiple_of(block * LANES, LANES), LANES)
        germs = germ_ref[:, lanes]
        square = germs * germs
        second = (square - 1.0) / math.sqrt(2.0)
        third = (square * germs - 3.0 * germs) / math.sqrt(6.0)
        values = jnp.ones((every, LANES), jnp.float32)
        for germ in range(germs.shape[0]):
            degree = jnp.broadcast_to(degree_ref[:, germ : germ + 1], (every, LANES))
            at = lambda table: jnp.broadcast_to(table[germ : germ + 1, :], (every, LANES))
            values = values * jnp.where(
                degree == 0, 1.0,
                jnp.where(degree == 1, at(germs), jnp.where(degree == 2, at(second), at(third))),
            )
        high, low = split_two(values)
        wide = lambda a: a.astype(jnp.float32)
        stack = stacked([wide(high), wide(high), wide(low)], basis_op.shape[1])
        basis_op[lanes, :] = jnp.transpose(stack).astype(BF16)
        high, low = split_two(values * (2.0 * weight_ref[:, lanes]))
        weight_op[:every, lanes] = high
        weight_op[every:, lanes] = low
        spread = stacked([-jnp.ones((1, LANES), jnp.float32), -germs], LOG_DEPTH)
        high, low = split_two(spread)
        stack = stacked([wide(high), wide(high), wide(low)], LANES)
        germ_op[lanes, :] = jnp.transpose(stack).astype(BF16)
        return carry

    lax.fori_loop(0, basis_op.shape[0] // LANES, make_basis, 0)

    def log_stack(block):
        high, low = split_two(stacked([block], LOG_DEPTH))
        return stacked([high, low, high], LANES)

    def field_stack(block):
        high, low = split_two(block)
        return stacked([high, low, high], line_op.shape[1])

    for condition, _, target, slot, _ in (
        (not_first, None, log_lines.at[1], 0, None), (not_last, None, log_lines.at[0], 1, None),
        (x > 0, None, log_sides.at[0], 2, None), (x < count_x - 1, None, log_sides.at[1], 3, None),
    ):
        @pl.when(condition)
        def _():
            arrived(target, log_recv.at[slot])

    def make_log(row, carry):
        log_op[row] = log_stack(log_ref[:, row, :])
        return carry

    lax.fori_loop(0, own_rows, make_log, 0)
    log_op[below] = log_stack(
        jnp.where(last_y, log_ref[:, own_rows - 1, :], log_lines[0])
    )
    log_op[above] = log_stack(jnp.where(first_y, log_ref[:, 0, :], log_lines[1]))

    def at_nodes(nodes, field, logs):
        return (product(basis_op[nodes, :], field), jnp.exp(product(germ_op[nodes, :], logs)))

    def flux(later, earlier, half_later, half_earlier):
        return (later - earlier) * pl.reciprocal(half_later + half_earlier)

    def project(nodes, applied):
        high = applied.astype(BF16)
        rest = applied - high.astype(jnp.float32)
        middle = rest.astype(BF16)
        low = (rest - middle.astype(jnp.float32)).astype(BF16)
        both = product(weight_op[:, nodes], high) + product(weight_op[:, nodes], middle)
        return both[:every] + both[every:] + product(weight_op[:every, nodes], low)

    node_slice = lambda block: pl.ds(pl.multiple_of(block * NODE_BLOCK, NODE_BLOCK), NODE_BLOCK)

    for kind in range(4):
        condition = (None, None, x < count_x - 1, x > 0)[kind]
        for source in range(shares):
            wait = lambda: arrived(sides.at[kind, source], side_recv.at[kind, source])
            wait() if condition is None else pl.when(condition)(wait)
    flat = lambda ref: ref.reshape(every, LANES)
    side = [flat(sides[kind]) for kind in range(4)]
    log_first, log_last = log_cols_ref[0], log_cols_ref[1]
    before = jnp.where(x == 0, side[0], side[3])
    after = jnp.where(x == count_x - 1, side[1], side[2])
    log_before = jnp.where(x == 0, log_first, log_sides[0])
    log_after = jnp.where(x == count_x - 1, log_last, log_sides[1])

    def beside(low_part, high_part):
        lane = lax.broadcasted_iota(jnp.int32, low_part.shape, 1)
        return jnp.where(lane < own_rows, low_part, pltpu.roll(high_part, own_rows, 1))

    line_op[0, :, :LANES] = field_stack(beside(before, side[1]))
    line_op[0, :, LANES:] = field_stack(beside(side[0], after))
    log_edge = jnp.concatenate(
        [log_stack(beside(log_before, log_last)), log_stack(beside(log_first, log_after))], axis=1
    )
    edge[...] = jnp.zeros_like(edge)

    def make_edge(block, carry):
        nodes = node_slice(block)
        values, halves = at_nodes(nodes, line_op[0], log_edge)
        edge[...] += project(nodes, flux(
            values[:, LANES:], values[:, :LANES], halves[:, LANES:], halves[:, :LANES]
        ))
        return carry

    lax.fori_loop(0, blocks, make_edge, 0)

    def wait_line(row):
        for source in range(shares):
            arrived(lines.at[row, source], line_recv.at[row, source])

    wait_line(0)
    pl.when(not_first)(lambda: wait_line(above))
    line = flat(lines[0])
    line_op[0, :, :LANES] = field_stack(jnp.where(first_y, line, flat(lines[above])))
    line_op[0, :, LANES:] = field_stack(line)

    def begin(block, carry):
        nodes = node_slice(block)
        logs = jnp.concatenate([log_op[above], log_op[0]], axis=1)
        values, halves = at_nodes(nodes, line_op[0], logs)
        value_prev[nodes, :] = values[:, LANES:]
        half_prev[nodes, :] = halves[:, LANES:]
        flux_prev[nodes, :] = flux(
            values[:, LANES:], values[:, :LANES], halves[:, LANES:], halves[:, :LANES]
        )
        return carry

    lax.fori_loop(0, blocks, begin, 0)

    home_row = lambda row: home.at[pl.ds(row * modes, modes), :]

    def out_copy(row, step):
        to = peer(step)
        return remote(
            total.at[row, to], home_row(share * own_rows + row), out_send.at[row, step],
            out_recv.at[row, share], sa=to,
        )

    def own_copy(row):
        return pltpu.make_async_copy(
            total.at[row, share], home_row(share * own_rows + row), out_recv.at[row, share]
        )

    def take_origin(pair, carry):
        block = origin[pl.ds(2 * pair, 2)].reshape(2 * rows, LANES)
        block = row_transform(block, pair_ref, rest_ref)
        spectrum[pair] = col_transform(
            jnp.concatenate([block[:rows], block[rows:]], axis=1), all_ref
        )
        return carry

    groups = own_rows // group
    load_origin.wait()

    def take_group(index, carry):
        base = index * group
        lax.fori_loop(
            lax.div(index * pairs, groups), lax.div((index + 1) * pairs, groups), take_origin, 0
        )
        for ahead in range(1, group + 1):
            row = base + ahead
            if ahead < group:
                wait_line(row)
            else:
                pl.when(jnp.logical_or(row < own_rows, not_last))(lambda: wait_line(row))
            line = flat(lines[row])
            if ahead == group:
                line = jnp.where(
                    jnp.logical_and(row == own_rows, last_y), flat(lines[row - 1]), line
                )
            place = pl.ds((ahead - 1) % 2 * LANES, LANES)
            line_op[(ahead - 1) // 2, :, place] = field_stack(line)

        def take_nodes(block, carry):
            nodes = node_slice(block)
            value, half, flux_up = value_prev[nodes, :], half_prev[nodes, :], flux_prev[nodes, :]
            inside = lax.broadcasted_iota(jnp.int32, value.shape, 1) < LANES - 1
            for pair in range(group // 2):
                row = base + 2 * pair
                logs = jnp.concatenate([log_op[row + 1], log_op[row + 2]], axis=1)
                values, halves = at_nodes(nodes, line_op[pair], logs)
                applied = []
                for here in range(2):
                    value_next = values[:, here * LANES : (here + 1) * LANES]
                    half_next = halves[:, here * LANES : (here + 1) * LANES]
                    flux_down = flux(value_next, value, half_next, half)
                    across = jnp.where(
                        inside,
                        flux(
                            pltpu.roll(value, LANES - 1, 1), value,
                            pltpu.roll(half, LANES - 1, 1), half,
                        ),
                        0.0,
                    )
                    applied.append(
                        (0.5 * storage_rate) * value
                        - (across - pltpu.roll(across, 1, 1)) - (flux_down - flux_up)
                    )
                    value, half, flux_up = value_next, half_next, flux_down
                sums = project(nodes, jnp.concatenate(applied, axis=1))
                parts = sums.reshape(shares, modes, 2 * LANES)
                total[row] += parts[:, :, :LANES]
                total[row + 1] += parts[:, :, LANES:]
            value_prev[nodes, :] = value
            half_prev[nodes, :] = half
            flux_prev[nodes, :] = flux_up
            return carry

        lax.fori_loop(0, blocks, take_nodes, 0)
        lane = lax.broadcasted_iota(jnp.int32, (every, LANES), 1)
        for step in range(group):
            row = base + step
            left = pltpu.roll(edge[...], lax.rem(LANES - row, LANES), 1)
            right = pltpu.roll(edge[...], LANES - 1 - own_rows - row, 1)
            change = jnp.where(lane == 0, left, 0.0) - jnp.where(lane == LANES - 1, right, 0.0)
            line = row_transform(flat(total[row]) + change, pair_ref, rest_ref)
            total[row] = line.reshape(shares, modes, LANES)
        for step in range(group):
            row = base + step
            for to in range(1, shares):
                out_copy(row, to).start()
            own_copy(row).start()
        return carry

    lax.fori_loop(0, own_rows // group, take_group, 0)

    def arrive(row, carry):
        for step in range(1, shares):
            source = peer(step)
            arrived(home_row(source * own_rows + row), out_recv.at[row, source])
        own_copy(row).wait()
        return carry

    lax.fori_loop(0, own_rows, arrive, 0)

    def take_pair(pair, columns):
        line = [home[pl.ds(2 * pair + half, rows, stride=modes), :] for half in range(2)]
        line = col_transform(jnp.concatenate(line, axis=1), all_ref)
        line = spectrum[pair] - line
        spectrum[pair] = line
        alone = line * inverse[...]
        trace = pl.ds(8 * pair, 8)
        lane = lax.broadcasted_iota(jnp.int32, (LANES, LANES), 1)
        result = []
        for end in range(2):
            ends = jnp.broadcast_to(column_ref[:rows, 4 + end : 5 + end], (rows, 2 * LANES))
            result.append(jnp.sum(alone * ends, axis=0, keepdims=True))
            upright = jnp.concatenate([alone[:, :LANES], alone[:, LANES:]], axis=0)
            upright = jnp.sum(upright * lane_ref[end : end + 1, :], axis=1, keepdims=True)
            columns = jnp.where(lane == end * (LANES // 2) + pair, upright, columns)
        blank = jnp.zeros((2, LANES), jnp.float32)
        traces[trace, :] = jnp.concatenate(
            [blank, result[0][:, :LANES], result[0][:, LANES:],
             result[1][:, :LANES], result[1][:, LANES:], blank], axis=0
        )
        return columns

    columns = lax.fori_loop(0, pairs, take_pair, jnp.zeros((LANES, LANES), jnp.float32))
    tall[...] = jnp.transpose(columns)
    for end in range(2):
        traces[pl.ds(end, pairs, stride=8), :] = tall[pl.ds(end * (LANES // 2), pairs), :]
    save = pltpu.make_async_copy(spectrum, spec_ref, spec_sem)
    save.start()

    piece = lambda owner: pl.ds(owner * per * 8, per * 8)

    def trace_copy(step):
        to = other(step)
        return remote(
            traces.at[piece(to), :], got.at[piece(me), :], trace_send.at[step],
            trace_recv.at[me], **at_owner(to),
        )

    def flux_copy(step):
        to = other(step)
        return remote(
            back.at[piece(to), :], flux_ref.at[piece(me), :], flux_send.at[step],
            flux_recv.at[me], **at_owner(to),
        )

    for step in range(1, owners):
        trace_copy(step).start()
    got[piece(me), :] = traces[piece(me), :]
    load_join.wait()
    for step in range(1, owners):
        arrived(got.at[piece(other(step)), :], trace_recv.at[other(step)])
    solve_fluxes(plane, per, got, back, lane_ref, join, by_row, by_col, col_table, row_table)
    for step in range(1, owners):
        flux_copy(step).start()
    own_flux = pltpu.make_async_copy(
        back.at[piece(me), :], flux_ref.at[piece(me), :], flux_recv.at[me]
    )
    own_flux.start()

    def sent(row, carry):
        for step in range(1, shares):
            line_copy(row, step).wait_send()
            out_copy(row, step).wait_send()
        return carry

    lax.fori_loop(0, own_rows, sent, 0)
    for condition, copy in remote_copies:
        if condition is None:
            copy.wait_send()
        else:
            pl.when(condition)(copy.wait_send)
    save.wait()
    own_flux.wait()
    for step in range(1, owners):
        trace_copy(step).wait_send()
        flux_copy(step).wait_send()
        arrived(flux_ref.at[piece(other(step)), :], flux_recv.at[other(step)])


def finish_kernel(
    spec_ref, flux_ref, now_ref, before_ref, mean_ref, lane_ref, column_ref, rows_ref, cols_ref,
    fresh_ref, update_ref, inverse,
):
    rows = spec_ref.shape[1]
    column = lambda k: jnp.broadcast_to(column_ref[:rows, k : k + 1], (rows, LANES))

    @pl.when(pl.program_id(0) == 0)
    def start():
        inverse[...] = 1.0 / (storage_rate + mean_ref[0] * (column(3) + lane_ref[2:3, :]))

    upright = jnp.transpose(flux_ref[...])
    for pair in range(spec_ref.shape[0]):
        parts = []
        for half in range(2):
            beside = lambda kind: jnp.broadcast_to(
                upright[half * rows : (half + 1) * rows, 8 * pair + kind : 8 * pair + kind + 1],
                (rows, LANES),
            )
            over = lambda kind: flux_ref[8 * pair + kind : 8 * pair + kind + 1, :]
            part = spec_ref[pair, :, half * LANES : (half + 1) * LANES]
            part = part + (beside(1) * lane_ref[1:2, :] - beside(0) * lane_ref[0:1, :])
            part = part + (column(5) * over(4 + half) - column(4) * over(2 + half))
            parts.append(part * inverse[...])
        high, low = split_two(jnp.concatenate(parts, axis=1))
        part = product(rows_ref[...], jnp.concatenate([high, low, high], axis=0))
        high, low = split_two(jnp.concatenate([part[:, :LANES], part[:, LANES:]], axis=0))
        part = product(jnp.concatenate([high, low], axis=1), cols_ref[...])
        part = (part[:, :LANES] + part[:, LANES:]).reshape(2, rows, LANES)
        mode = slice(2 * pair, 2 * pair + 2)
        update_ref[mode] = part
        before = before_ref[mode]
        fresh_ref[mode] = before + relax_weight * (now_ref[mode] - before + step_length * part)


def cosine_table(length):
    freq, cells = np.arange(length)[:, None], np.arange(length)[None, :]
    factor = np.where(freq == 0, math.sqrt(1.0 / length), math.sqrt(2.0 / length))
    return factor * np.cos((freq * (2 * cells + 1) % (4 * length)) * (math.pi / (2 * length)))


def pieces(table):
    found, rest = [], table.astype(np.float32)
    for _ in range(3):
        found.append(rest.astype(BF16))
        rest = rest - found[-1].astype(np.float32)
    return found


def constant_tables(count_x, rows, width):
    eigen = lambda count: 2.0 - 2.0 * np.cos(np.arange(count) * (math.pi / count))
    row_table, col_table = cosine_table(rows), cosine_table(width)
    far_table = cosine_table(count_x * width)
    join = np.einsum("kix,lx->kil", far_table.reshape(-1, count_x, width), col_table)
    twice = lambda a: np.concatenate([a, a])
    lanes = [
        col_table[:, 0], col_table[:, -1], eigen(width),
        twice(row_table[:, 0]), twice(row_table[:, -1]), twice(eigen(rows)),
    ]
    columns = [lanes[2], lanes[0], lanes[1], lanes[5], lanes[3], lanes[4]]
    grow = lambda a: np.pad(np.stack(a), ((0, 8 - len(a)), (0, 0))).astype(np.float32)
    high, middle, low = pieces(col_table.T)
    front = pieces(col_table)
    pair = np.block([[high, middle], [high, middle]])
    rest = np.concatenate([high, low])
    back = np.block([[front[0], front[1]], [front[0], np.zeros_like(high)]])
    high, middle, low = pieces(row_table)
    every = np.concatenate([high, high, middle, middle, high, low], axis=1)
    high, low, _ = pieces(row_table.T)
    rows_back = np.concatenate([high, high, low], axis=1)
    return dict(
        pair=pair, rest=rest, every=every, lanes=grow(lanes), columns=grow(columns).T.copy(),
        far=grow([eigen(count_x * width)]), join=join.reshape(len(far_table), -1).astype(np.float32),
        rows=rows_back, cols=back,
    )


def chebyshev_step(
    field, field_before, source, log_fields, weights, mean_perm, node_index, mode_index
):
    modes, rows, width = field.shape
    count_x, count_y, shares = (lax.axis_size(axis) for axis in ("gx", "gy", "sa"))
    padded = round_up(modes, 16)
    grow = lambda a, size, dim: jnp.pad(
        a, [(0, size - a.shape[d] if d == dim else 0) for d in range(a.ndim)]
    )
    field, field_before, source = (grow(a, padded, 0) for a in (field, field_before, source))
    mean = mean_perm.reshape(1)
    tables = constant_tables(count_x, rows, width)
    pairs, owners = padded // 2, count_x * count_y
    per = -(-pairs // owners)
    depth_solve = round_up(count_y * per, 8)
    extra = 8 * (depth_solve - count_y * per)
    own_rows = rows // shares
    nodes = node_index.shape[0]
    all_nodes = round_up(nodes, NODE_BLOCK)
    germs = grow(node_germs(node_index).T, all_nodes, 1)
    degrees = grow(mode_index.reshape(shares, modes, -1), padded, 1).reshape(shares * padded, -1)
    cols = jnp.stack([field[:, :, 0], field[:, :, -1]]).reshape(2, padded, shares, own_rows)
    cols = grow(cols.transpose(2, 0, 1, 3), LANES, 3)
    log_cols = grow(jnp.stack([log_fields[:, :, 0], log_fields[:, :, -1]]), LANES, 2)
    levels = log_fields.shape[0]
    group = math.gcd(own_rows, 8)
    every = shares * padded
    depth = round_up(3 * every, LANES)
    slots = own_rows + 2
    vmem = lambda shape, kind=jnp.float32: pltpu.VMEM(shape, kind)
    dma = lambda *shape: pltpu.SemaphoreType.DMA(shape)
    place = pl.BlockSpec(memory_space=pl.ANY)
    whole = pl.BlockSpec(memory_space=pltpu.VMEM)
    numbers = pl.BlockSpec(memory_space=pltpu.SMEM)
    spectrum, fluxes = pl.pallas_call(
        functools.partial(node_kernel, (count_x, count_y, shares, group)),
        in_specs=[place, whole, place, whole, whole, whole, whole]
        + [place, numbers] + [whole] * 6 + [place],
        out_specs=[place, place],
        out_shape=[
            jax.ShapeDtypeStruct((pairs, rows, 2 * width), jnp.float32),
            jax.ShapeDtypeStruct((owners * per * 8, LANES), jnp.float32),
        ],
        scratch_shapes=[
            vmem((slots, shares, padded, LANES)),
            vmem((2, levels, LANES)),
            vmem((2, levels, LANES)),
            vmem((4, shares, padded, LANES)),
            vmem((own_rows, shares, padded, LANES)),
            vmem((group // 2, depth, 2 * LANES), BF16),
            vmem((slots, LANES, LANES), BF16),
            vmem((all_nodes, depth), BF16),
            vmem((all_nodes, LANES), BF16),
            vmem((2 * every, all_nodes), BF16),
            vmem((every, LANES)),
            vmem((all_nodes, LANES)),
            vmem((all_nodes, LANES)),
            vmem((all_nodes, LANES)),
            vmem((rows * padded, LANES)),
            vmem((pairs, rows, 2 * LANES)),
            vmem((padded, rows, LANES)),
            vmem((owners * per * 8, LANES)),
            vmem((owners * per * 8 + extra, LANES)),
            vmem((owners * per * 8 + extra, LANES)),
            vmem((LANES, LANES)),
            vmem(tables["join"].shape),
            vmem((rows, 2 * LANES)),
            vmem((LANES, 4 * LANES)),
            vmem((2 * LANES, 2 * LANES)),
            vmem((count_x - 1, round_up(count_x - 1, 8), LANES)),
            vmem((2 * count_y - 3, depth_solve, count_x * width)),
            dma(2), pltpu.SemaphoreType.DMA, dma(owners), dma(owners), dma(owners), dma(owners),
            dma(own_rows, shares), dma(slots, shares), dma(2 * shares), dma(shares, 4),
            dma(4, shares), dma(4), dma(4), dma(own_rows, shares), dma(own_rows, shares),
        ],
        compiler_params=pltpu.CompilerParams(
            collective_id=0, has_side_effects=True, vmem_limit_bytes=56 * 1024 * 1024
        ),
    )(
        field, log_fields, cols, log_cols, germs, degrees,
        grow(weights[None, :], all_nodes, 1), source, mean,
        *(tables[name] for name in ("pair", "rest", "every", "lanes", "columns", "far", "join")),
    )
    step = math.gcd(pairs, 8)
    block = pl.BlockSpec((2 * step, rows, width), lambda n: (n, 0, 0))
    still = lambda a: pl.BlockSpec(a.shape, lambda n: (0,) * a.ndim)
    shape = jax.ShapeDtypeStruct(field.shape, jnp.float32)
    fresh, update = pl.pallas_call(
        finish_kernel,
        grid=(pairs // step,),
        in_specs=[
            pl.BlockSpec((step, rows, 2 * width), lambda n: (n, 0, 0)),
            pl.BlockSpec((8 * step, LANES), lambda n: (n, 0)),
            block, block, numbers,
        ] + [still(tables[name]) for name in ("lanes", "columns", "rows", "cols")],
        out_specs=[block, block],
        out_shape=[shape, shape],
        scratch_shapes=[vmem((rows, LANES))],
        compiler_params=pltpu.CompilerParams(dimension_semantics=("arbitrary",)),
    )(
        spectrum, fluxes, field, field_before, mean,
        *(tables[name] for name in ("lanes", "columns", "rows", "cols")),
    )
    return (fresh[:modes], update[:modes])


def node_germs(node_index):
    levels = jnp.arange(len(hermite_points), dtype=jnp.int32)
    picked = (node_index[:, :, None] == levels).astype(jnp.float32)
    points = jnp.asarray(hermite_points, dtype=jnp.float32)
    return jnp.sum(picked * points, axis=2)


def solution(mesh):
    return jax.shard_map(
        chebyshev_step,
        mesh=mesh,
        in_specs=(
            P("sa", "gy", "gx"),
            P("sa", "gy", "gx"),
            P("sa", "gy", "gx"),
            P(None, ("gy", "sa"), "gx"),
            P(),
            P(),
            P(),
            P(),
        ),
        out_specs=(P("sa", "gy", "gx"), P("sa", "gy", "gx")),
        check_vma=False,
    )
```

```python
import functools
import math

import jax
import jax.numpy as jnp
import numpy as np
from jax import lax
from jax.experimental import pallas as pl
from jax.experimental.pallas import tpu as pltpu
from jax.sharding import PartitionSpec as P


HIGHEST = lax.Precision.HIGHEST
hermite_points = (
    0.0,
    -1.7320508075688772,
    1.7320508075688772,
    -1.355626179974266,
    1.355626179974266,
    -2.8569700138728056,
    2.8569700138728056,
)
storage_rate = 0.0004
relax_weight = 1.6
step_length = 0.3


LANES = 128
NODE_BLOCK = 512
LOG_DEPTH = 16
BF16 = jnp.bfloat16


def round_up(value, step):
    return -(-value // step) * step


def product(left, right):
    return jnp.dot(left, right, preferred_element_type=jnp.float32)


def split_two(block):
    high = block.astype(BF16)
    return (high, (block - high.astype(jnp.float32)).astype(BF16))


def split_three(block):
    high = block.astype(BF16)
    rest = block - high.astype(jnp.float32)
    middle = rest.astype(BF16)
    return (high, middle, (rest - middle.astype(jnp.float32)).astype(BF16))


def exact(left, right):
    return jnp.dot(left, right, precision=HIGHEST, preferred_element_type=jnp.float32)


def row_transform(block, pair_ref, rest_ref):
    high, middle, low = split_three(block)
    both = product(jnp.concatenate([high, middle], axis=1), pair_ref[...])
    both = both[:, :LANES] + both[:, LANES:]
    return both + product(jnp.concatenate([low, high], axis=1), rest_ref[...])


def col_transform(block, all_ref):
    high, middle, low = split_three(block)
    stack = jnp.concatenate([high, middle, high, middle, low, high], axis=0)
    return product(all_ref[...], stack)


def make_tables(sizes, per, mean, lane_ref, column_ref, far_ref, inverse, by_row, by_col, col_table, row_table):
    count_x, count_y = sizes
    half = LANES // 2
    column = lambda k, rows=LANES: jnp.broadcast_to(column_ref[:rows, k : k + 1], (rows, LANES))
    lanes = lambda k: lane_ref[k : k + 1, :]
    upright = 1.0 / (storage_rate + mean * (column(0) + lanes(5)))
    flat = 1.0 / (storage_rate + mean * (column(3) + lanes(2)))
    inverse[:, :LANES] = flat[:half]
    inverse[:, LANES:] = flat[:half]
    lane = lax.broadcasted_iota(jnp.int32, (LANES, LANES), 1)
    row = lax.broadcasted_iota(jnp.int32, (LANES, LANES), 0)
    for end in range(2):
        part = upright * column(1 + end)
        by_col[:LANES, end * LANES : (end + 1) * LANES] = jnp.where(lane < half, part, 0.0)
        by_col[LANES:, end * LANES : (end + 1) * LANES] = jnp.where(lane < half, 0.0, part)
        part = flat * column(4 + end)
        by_row[:, 2 * end * LANES : (2 * end + 1) * LANES] = jnp.where(row < half, part, 0.0)
        by_row[:, (2 * end + 1) * LANES : (2 * end + 2) * LANES] = jnp.where(row < half, 0.0, part)

    def tables(count, same, cross):
        shrink = [
            1.0 / (1.0 / mean + 2.0 * same - 2.0 * math.cos(n * math.pi / count) * cross)
            for n in range(1, count)
        ]
        sine = lambda a, b: math.sin(a * b % (2 * count) * math.pi / count)
        return [
            [
                sum((2.0 / count) * sine(n, a) * sine(n, b) * shrink[n - 1] for n in range(1, count))
                for b in range(1, count)
            ]
            for a in range(1, count)
        ]

    total = lambda a: jnp.sum(a, axis=0, keepdims=True)
    ends = column(1), column(2)
    found = tables(
        count_x, total(upright * ends[0] * ends[0]), total(upright * ends[0] * ends[1])
    )
    for a in range(count_x - 1):
        for b in range(count_x - 1):
            col_table[a, b : b + 1, :] = found[a][b]
    far = far_ref[0:1, :]
    wide = lambda k: jnp.broadcast_to(column_ref[:half, k : k + 1], (half, far.shape[1]))
    deep = 1.0 / (storage_rate + mean * (wide(3) + far))
    found = tables(
        count_y, total(deep * wide(4) * wide(4)), total(deep * wide(4) * wide(5))
    )
    depth = row_table.shape[1]
    where_row = lax.broadcasted_iota(jnp.int32, (depth, far.shape[1]), 0) // per
    for shift in range(-(count_y - 2), count_y - 1):
        table = jnp.zeros((depth, far.shape[1]), jnp.float32)
        for a in range(count_y - 1):
            if 0 <= a + shift < count_y - 1:
                table = jnp.where(where_row == a, found[a][a + shift], table)
        row_table[shift + count_y - 2] = table


def solve_fluxes(sizes, per, got, back, lane_ref, join_ref, by_row, by_col, col_table, row_table):
    count_x, count_y = sizes
    depth = row_table.shape[1]
    rows = count_y * per
    lanes = lambda k: lane_ref[k : k + 1, :]
    take = lambda block, kind: got[pl.ds(block * rows * 8 + kind, depth, stride=8), :]
    row = lax.broadcasted_iota(jnp.int32, (depth, LANES), 0)
    up = lambda a, by=1: pltpu.roll(a, (-by * per) % depth, 0)
    down = lambda a: jnp.where(row < per, 0.0, pltpu.roll(a, per, 0))
    blocks, cuts = range(count_x), range(1, count_x)

    def through_cols(first, last):
        jump = [first[cut] - last[cut - 1] for cut in cuts]
        return [
            sum(col_table[a, b : b + 1, :] * jump[b] for b in range(count_x - 1))
            for a in range(count_x - 1)
        ]

    fluxes = through_cols([take(b, 0) for b in blocks], [take(b, 1) for b in blocks])
    spread = [exact(flux, by_row[...]) for flux in fluxes]

    def at_row(block, end, half):
        part = slice((2 * end + half) * LANES, (2 * end + half + 1) * LANES)
        value = take(block, 2 + 2 * end + half)
        if block < count_x - 1:
            value = value + spread[block][:, part] * lanes(1)
        if block > 0:
            value = value - spread[block - 1][:, part] * lanes(0)
        return value

    jump = jnp.concatenate(
        [
            jnp.concatenate([up(at_row(b, 0, half)) - at_row(b, 1, half) for b in blocks], axis=1)
            for half in range(2)
        ],
        axis=0,
    )
    far = lax.dot_general(
        jump, join_ref[...], (((1,), (1,)), ((), ())), precision=HIGHEST,
        preferred_element_type=jnp.float32,
    )
    mixed = []
    for half in range(2):
        part = far[half * depth : (half + 1) * depth]
        mixed.append(sum(
            row_table[shift + count_y - 2] * (up(part, shift) if shift else part)
            for shift in range(-(count_y - 2), count_y - 1)
        ))
    near = exact(jnp.concatenate(mixed, axis=0), join_ref[...])
    through_rows = [
        [near[half * depth : (half + 1) * depth, b * LANES : (b + 1) * LANES] for half in range(2)]
        for b in blocks
    ]
    ends = []
    for b in blocks:
        reach = exact(jnp.concatenate(through_rows[b], axis=1), by_col[...])
        ends.append([
            lanes(4) * reach[:, end * LANES : (end + 1) * LANES]
            - lanes(3) * down(reach[:, end * LANES : (end + 1) * LANES])
            for end in range(2)
        ])
    more = through_cols([end[0] for end in ends], [end[1] for end in ends])
    fluxes = [a + b for a, b in zip(fluxes, more)]
    nothing = jnp.zeros((depth, LANES), jnp.float32)
    for b in blocks:
        left = fluxes[b - 1] if b > 0 else nothing
        right = fluxes[b] if b < count_x - 1 else nothing
        top = [down(part) for part in through_rows[b]]
        for kind, value in enumerate([left, right] + top + through_rows[b]):
            back[pl.ds(b * rows * 8 + kind, depth, stride=8), :] = value


def stacked(parts, depth):
    missing = depth - sum(part.shape[0] for part in parts)
    if missing:
        parts = parts + [jnp.zeros((missing,) + parts[0].shape[1:], parts[0].dtype)]
    return jnp.concatenate(parts, axis=0)


def node_kernel(
    sizes, field_ref, log_ref, node_ref, mode_ref, weight_ref,
    source_ref, mean_ref, pair_ref, rest_ref, all_ref, lane_ref, column_ref, far_ref, join_ref,
    spec_ref, flux_ref,
    lines, log_lines, log_sides, sides, total, line_op, log_op, basis_op, germ_op, weight_op,
    edge, value_prev, half_prev, flux_prev,
    home, spectrum, origin, traces, got, back, tall, join,
    inverse, by_row, by_col, col_table, row_table,
    block_field, field_cols, log_cols, picks, shares_of, degrees,
    load_sem, spec_sem, trace_send, trace_recv, flux_send, flux_recv,
    line_send, line_recv, halo_send, side_send, side_recv, log_send, log_recv, out_send, out_recv,
):
    count_x, count_y, shares, group = sizes
    modes, rows, width = field_ref.shape
    own_rows = rows // shares
    every = shares * modes
    below, above = own_rows, own_rows + 1
    blocks = basis_op.shape[0] // NODE_BLOCK
    x, y, share = (lax.axis_index(axis) for axis in ("gx", "gy", "sa"))
    first_y = jnp.logical_and(y == 0, share == 0)
    last_y = jnp.logical_and(y == count_y - 1, share == shares - 1)
    not_first, not_last = jnp.logical_not(first_y), jnp.logical_not(last_y)
    peer = lambda step: lax.rem(share + step, shares)

    def remote(source, target, send, recv, **place):
        return pltpu.make_async_remote_copy(
            src_ref=source, dst_ref=target, send_sem=send, recv_sem=recv,
            device_id=place, device_id_type=pl.DeviceIdType.MESH,
        )

    def arrived(target, recv):
        pltpu.make_async_copy(target, target, recv).wait()

    load_field = pltpu.make_async_copy(field_ref, block_field, load_sem.at[2])
    load_field.start()
    load_origin = pltpu.make_async_copy(source_ref, origin, load_sem.at[0])
    load_origin.start()
    load_join = pltpu.make_async_copy(join_ref, join, load_sem.at[1])
    load_join.start()

    barrier = pltpu.get_barrier_semaphore()
    greet = lambda **place: pl.semaphore_signal(
        barrier, inc=1, device_id=place, device_id_type=pl.DeviceIdType.MESH
    )
    for step in range(1, shares):
        greet(sa=peer(step))
    owners = count_x * count_y
    me = x * count_y + y
    other = lambda step: lax.rem(me + step, owners)
    at_owner = lambda owner: dict(gx=lax.div(owner, count_y), gy=lax.rem(owner, count_y))
    for step in range(1, owners):
        greet(**at_owner(other(step)))
    conditions = (
        (x > 0, dict(gx=x - 1)), (x < count_x - 1, dict(gx=x + 1)),
        (y > 0, dict(gy=y - 1)), (y < count_y - 1, dict(gy=y + 1)),
    )
    for condition, place in conditions:
        @pl.when(condition)
        def _():
            for step in range(1, shares):
                greet(sa=peer(step), **place)
    pairs = modes // 2
    unroll = max(n for n in range(1, 6) if pairs % n == 0)
    pick_row = lax.broadcasted_iota(jnp.int32, (16, 2 * LANES), 0)
    pick_lane = lax.broadcasted_iota(jnp.int32, (16, 2 * LANES), 1) % LANES
    first_pick = jnp.logical_and(pick_row == 0, pick_lane == 0)
    last_pick = jnp.logical_and(pick_row == 1, pick_lane == LANES - 1)
    pick = jnp.where(jnp.logical_or(first_pick, last_pick), 1.0, 0.0).astype(BF16)

    def columns_of(block):
        return lax.dot_general(
            pick, jnp.concatenate(split_two(block), axis=1), (((1,), (1,)), ((), ())),
            preferred_element_type=jnp.float32,
        )

    log_cols[...] = jnp.zeros_like(log_cols)
    for level in range(log_ref.shape[0]):
        found = columns_of(log_ref[level])
        for end in range(2):
            log_cols[end, level : level + 1, :own_rows] = found[end : end + 1, :]
    load_field.wait()

    def take_columns(index, carry):
        for pair in range(unroll):
            mode = 2 * (index * unroll + pair)
            found = columns_of(block_field[pl.ds(mode, 2)].reshape(2 * rows, LANES))
            for half in range(2):
                part = pltpu.roll(found, LANES - rows, 1) if half else found
                for end in range(2):
                    field_cols[end, pl.ds(mode + half, 1), :] = part[end : end + 1, :]
        return carry

    lax.fori_loop(0, pairs // unroll, take_columns, 0)
    sides_met = sum(condition.astype(jnp.int32) for condition, _ in conditions)
    pl.semaphore_wait(barrier, owners - 1 + (shares - 1) * (1 + sides_met))

    remote_copies = []

    def start(condition, copy):
        remote_copies.append((condition, copy))
        if condition is None:
            copy.start()
        else:
            pl.when(condition)(copy.start)

    row_of = lambda row: field_ref.at[:, row, :]
    flat_next = jnp.where(share == shares - 1, y + 1, y), lax.rem(share + 1, shares)
    flat_last = jnp.where(share == 0, y - 1, y), lax.rem(share + shares - 1, shares)
    log_copies = (
        (not_last, log_ref.at[:, own_rows - 1, :], log_lines.at[1], 0,
         dict(gy=flat_next[0], sa=flat_next[1])),
        (not_first, log_ref.at[:, 0, :], log_lines.at[0], 1,
         dict(gy=flat_last[0], sa=flat_last[1])),
        (x < count_x - 1, log_cols.at[1], log_sides.at[0], 2, dict(gx=x + 1)),
        (x > 0, log_cols.at[0], log_sides.at[1], 3, dict(gx=x - 1)),
    )
    for condition, source, target, slot, place in log_copies:
        start(condition, remote(source, target, log_send.at[slot], log_recv.at[slot], **place))
    start(y > 0, remote(
        row_of(0), lines.at[below, share], halo_send.at[0], line_recv.at[below, share],
        gy=y - 1, sa=jnp.int32(shares - 1),
    ))
    start(y < count_y - 1, remote(
        row_of(rows - 1), lines.at[above, share], halo_send.at[1], line_recv.at[above, share],
        gy=y + 1, sa=jnp.int32(0),
    ))
    for step in range(1, shares):
        to = peer(step)
        start(to > 0, remote(
            row_of(jnp.maximum(to * own_rows - 1, 0)), lines.at[above, share],
            halo_send.at[2 * step], line_recv.at[above, share], sa=to,
        ))
        start(to < shares - 1, remote(
            row_of(jnp.minimum((to + 1) * own_rows, rows - 1)), lines.at[below, share],
            halo_send.at[2 * step + 1], line_recv.at[below, share], sa=to,
        ))
    own_above = pltpu.make_async_copy(
        row_of(jnp.maximum(share * own_rows - 1, 0)), lines.at[above, share],
        line_recv.at[above, share],
    )
    own_below = pltpu.make_async_copy(
        row_of(jnp.minimum((share + 1) * own_rows, rows - 1)), lines.at[below, share],
        line_recv.at[below, share],
    )
    pl.when(share > 0)(own_above.start)
    pl.when(share < shares - 1)(own_below.start)
    for step in range(shares):
        to = peer(step)
        for kind in range(2):
            source = field_cols.at[kind]
            if step:
                start(None, remote(
                    source, sides.at[kind, share], side_send.at[step, kind],
                    side_recv.at[kind, share], sa=to,
                ))
            else:
                pltpu.make_async_copy(
                    source, sides.at[kind, share], side_recv.at[kind, share]
                ).start()
        start(x > 0, remote(
            field_cols.at[0], sides.at[2, share], side_send.at[step, 2],
            side_recv.at[2, share], gx=x - 1, sa=to,
        ))
        start(x < count_x - 1, remote(
            field_cols.at[1], sides.at[3, share], side_send.at[step, 3],
            side_recv.at[3, share], gx=x + 1, sa=to,
        ))

    def line_copy(row, step):
        to = peer(step)
        return remote(
            row_of(to * own_rows + row), lines.at[row, share], line_send.at[row, step],
            line_recv.at[row, share], sa=to,
        )

    def send_lines(row, carry):
        for step in range(1, shares):
            line_copy(row, step).start()
        pltpu.make_async_copy(
            row_of(share * own_rows + row), lines.at[row, share], line_recv.at[row, share]
        ).start()
        return carry

    lax.fori_loop(0, own_rows, send_lines, 0)
    per = traces.shape[0] // 8 // owners
    plane = (count_x, count_y)
    beyond = got.shape[0] - traces.shape[0]
    if beyond:
        got[traces.shape[0] :, :] = jnp.zeros((beyond, LANES), jnp.float32)
    traces[...] = jnp.zeros_like(traces)
    make_tables(
        plane, per, mean_ref[0], lane_ref, column_ref, far_ref,
        inverse, by_row, by_col, col_table, row_table,
    )

    weight_op[...] = jnp.zeros_like(weight_op)
    total[...] = jnp.zeros_like(total)

    nodes_given = node_ref.shape[1]
    picks[...] = jnp.zeros_like(picks)
    picks[:, :nodes_given] = node_ref[...]
    shares_of[...] = jnp.zeros_like(shares_of)
    shares_of[:, :nodes_given] = weight_ref[...]
    degrees[...] = jnp.zeros_like(degrees)
    for start_at in range(0, every, LANES):
        width_at = min(LANES, every - start_at)
        degrees[start_at : start_at + mode_ref.shape[0], :width_at] = mode_ref[
            :, start_at : start_at + width_at
        ].astype(jnp.float32)
        here = slice(start_at, start_at + LANES)
        degrees[here, :] = jnp.transpose(degrees[here, :])

    def make_basis(block, carry):
        lanes = pl.ds(pl.multiple_of(block * LANES, LANES), LANES)
        picked = picks[:, lanes]
        germs = jnp.zeros(picked.shape, jnp.float32)
        for level, point in enumerate(hermite_points):
            germs = jnp.where(picked == level, point, germs)
        square = germs * germs
        second = (square - 1.0) / math.sqrt(2.0)
        third = (square * germs - 3.0 * germs) / math.sqrt(6.0)
        values = jnp.ones((every, LANES), jnp.float32)
        for germ in range(germs.shape[0]):
            degree = jnp.broadcast_to(degrees[:every, germ : germ + 1], (every, LANES))
            at = lambda table: jnp.broadcast_to(table[germ : germ + 1, :], (every, LANES))
            values = values * jnp.where(
                degree == 0, 1.0,
                jnp.where(degree == 1, at(germs), jnp.where(degree == 2, at(second), at(third))),
            )
        high, low = split_two(values)
        wide = lambda a: a.astype(jnp.float32)
        stack = stacked([wide(high), wide(high), wide(low)], basis_op.shape[1])
        basis_op[lanes, :] = jnp.transpose(stack).astype(BF16)
        high, low = split_two(values * (2.0 * shares_of[:, lanes]))
        weight_op[:every, lanes] = high
        weight_op[every:, lanes] = low
        spread = stacked([-jnp.ones((1, LANES), jnp.float32), -germs], LOG_DEPTH)
        high, low = split_two(spread)
        stack = stacked([wide(high), wide(high), wide(low)], LANES)
        germ_op[lanes, :] = jnp.transpose(stack).astype(BF16)
        return carry

    lax.fori_loop(0, basis_op.shape[0] // LANES, make_basis, 0)

    def log_stack(block):
        high, low = split_two(stacked([block], LOG_DEPTH))
        return stacked([high, low, high], LANES)

    def field_stack(block):
        high, low = split_two(block)
        return stacked([high, low, high], line_op.shape[1])

    for condition, _, target, slot, _ in (
        (not_first, None, log_lines.at[1], 0, None), (not_last, None, log_lines.at[0], 1, None),
        (x > 0, None, log_sides.at[0], 2, None), (x < count_x - 1, None, log_sides.at[1], 3, None),
    ):
        @pl.when(condition)
        def _():
            arrived(target, log_recv.at[slot])

    def make_log(row, carry):
        log_op[row] = log_stack(log_ref[:, row, :])
        return carry

    lax.fori_loop(0, own_rows, make_log, 0)
    log_op[below] = log_stack(
        jnp.where(last_y, log_ref[:, own_rows - 1, :], log_lines[0])
    )
    log_op[above] = log_stack(jnp.where(first_y, log_ref[:, 0, :], log_lines[1]))

    def at_nodes(nodes, field, logs):
        return (product(basis_op[nodes, :], field), jnp.exp(product(germ_op[nodes, :], logs)))

    def flux(later, earlier, half_later, half_earlier):
        return (later - earlier) * pl.reciprocal(half_later + half_earlier)

    def project(nodes, applied):
        high = applied.astype(BF16)
        rest = applied - high.astype(jnp.float32)
        middle = rest.astype(BF16)
        low = (rest - middle.astype(jnp.float32)).astype(BF16)
        both = product(weight_op[:, nodes], high) + product(weight_op[:, nodes], middle)
        return both[:every] + both[every:] + product(weight_op[:every, nodes], low)

    node_slice = lambda block: pl.ds(pl.multiple_of(block * NODE_BLOCK, NODE_BLOCK), NODE_BLOCK)

    for kind in range(4):
        condition = (None, None, x < count_x - 1, x > 0)[kind]
        for source in range(shares):
            wait = lambda: arrived(sides.at[kind, source], side_recv.at[kind, source])
            wait() if condition is None else pl.when(condition)(wait)
    flat = lambda ref: ref.reshape(every, LANES)
    turn = lax.rem(LANES - share * own_rows, LANES)
    side = [pltpu.roll(flat(sides[kind]), turn, 1) for kind in range(4)]
    log_first, log_last = log_cols[0], log_cols[1]
    before = jnp.where(x == 0, side[0], side[3])
    after = jnp.where(x == count_x - 1, side[1], side[2])
    log_before = jnp.where(x == 0, log_first, log_sides[0])
    log_after = jnp.where(x == count_x - 1, log_last, log_sides[1])

    def beside(low_part, high_part):
        lane = lax.broadcasted_iota(jnp.int32, low_part.shape, 1)
        return jnp.where(lane < own_rows, low_part, pltpu.roll(high_part, own_rows, 1))

    line_op[0, :, :LANES] = field_stack(beside(before, side[1]))
    line_op[0, :, LANES:] = field_stack(beside(side[0], after))
    log_edge = jnp.concatenate(
        [log_stack(beside(log_before, log_last)), log_stack(beside(log_first, log_after))], axis=1
    )
    edge[...] = jnp.zeros_like(edge)

    def make_edge(block, carry):
        nodes = node_slice(block)
        values, halves = at_nodes(nodes, line_op[0], log_edge)
        edge[...] += project(nodes, flux(
            values[:, LANES:], values[:, :LANES], halves[:, LANES:], halves[:, :LANES]
        ))
        return carry

    lax.fori_loop(0, blocks, make_edge, 0)

    def wait_line(row):
        for source in range(shares):
            arrived(lines.at[row, source], line_recv.at[row, source])

    wait_line(0)
    pl.when(not_first)(lambda: wait_line(above))
    line = flat(lines[0])
    line_op[0, :, :LANES] = field_stack(jnp.where(first_y, line, flat(lines[above])))
    line_op[0, :, LANES:] = field_stack(line)

    def begin(block, carry):
        nodes = node_slice(block)
        logs = jnp.concatenate([log_op[above], log_op[0]], axis=1)
        values, halves = at_nodes(nodes, line_op[0], logs)
        value_prev[nodes, :] = values[:, LANES:]
        half_prev[nodes, :] = halves[:, LANES:]
        flux_prev[nodes, :] = flux(
            values[:, LANES:], values[:, :LANES], halves[:, LANES:], halves[:, :LANES]
        )
        return carry

    lax.fori_loop(0, blocks, begin, 0)

    home_row = lambda row: home.at[pl.ds(row * modes, modes), :]

    def out_copy(row, step):
        to = peer(step)
        return remote(
            total.at[row, to], home_row(share * own_rows + row), out_send.at[row, step],
            out_recv.at[row, share], sa=to,
        )

    def own_copy(row):
        return pltpu.make_async_copy(
            total.at[row, share], home_row(share * own_rows + row), out_recv.at[row, share]
        )

    def take_origin(index, carry):
        for pair in range(unroll):
            one_origin(index * unroll + pair)
        return carry

    def one_origin(pair):
        block = origin[pl.ds(2 * pair, 2)].reshape(2 * rows, LANES)
        block = row_transform(block, pair_ref, rest_ref)
        spectrum[pair] = col_transform(
            jnp.concatenate([block[:rows], block[rows:]], axis=1), all_ref
        )

    groups = own_rows // group
    load_origin.wait()

    def take_group(index, carry):
        base = index * group
        lax.fori_loop(
            lax.div(index * (pairs // unroll), groups),
            lax.div((index + 1) * (pairs // unroll), groups), take_origin, 0,
        )
        for ahead in range(1, group + 1):
            row = base + ahead
            if ahead < group:
                wait_line(row)
            else:
                pl.when(jnp.logical_or(row < own_rows, not_last))(lambda: wait_line(row))
            line = flat(lines[row])
            if ahead == group:
                line = jnp.where(
                    jnp.logical_and(row == own_rows, last_y), flat(lines[row - 1]), line
                )
            place = pl.ds((ahead - 1) % 2 * LANES, LANES)
            line_op[(ahead - 1) // 2, :, place] = field_stack(line)

        def take_nodes(block, carry):
            nodes = node_slice(block)
            value, half, flux_up = value_prev[nodes, :], half_prev[nodes, :], flux_prev[nodes, :]
            inside = lax.broadcasted_iota(jnp.int32, value.shape, 1) < LANES - 1
            for pair in range(group // 2):
                row = base + 2 * pair
                logs = jnp.concatenate([log_op[row + 1], log_op[row + 2]], axis=1)
                values, halves = at_nodes(nodes, line_op[pair], logs)
                applied = []
                for here in range(2):
                    value_next = values[:, here * LANES : (here + 1) * LANES]
                    half_next = halves[:, here * LANES : (here + 1) * LANES]
                    flux_down = flux(value_next, value, half_next, half)
                    across = jnp.where(
                        inside,
                        flux(
                            pltpu.roll(value, LANES - 1, 1), value,
                            pltpu.roll(half, LANES - 1, 1), half,
                        ),
                        0.0,
                    )
                    applied.append(
                        (0.5 * storage_rate) * value
                        - (across - pltpu.roll(across, 1, 1)) - (flux_down - flux_up)
                    )
                    value, half, flux_up = value_next, half_next, flux_down
                sums = project(nodes, jnp.concatenate(applied, axis=1))
                parts = sums.reshape(shares, modes, 2 * LANES)
                total[row] += parts[:, :, :LANES]
                total[row + 1] += parts[:, :, LANES:]
            value_prev[nodes, :] = value
            half_prev[nodes, :] = half
            flux_prev[nodes, :] = flux_up
            return carry

        lax.fori_loop(0, blocks, take_nodes, 0)
        lane = lax.broadcasted_iota(jnp.int32, (every, LANES), 1)
        for step in range(group):
            row = base + step
            left = pltpu.roll(edge[...], lax.rem(LANES - row, LANES), 1)
            right = pltpu.roll(edge[...], LANES - 1 - own_rows - row, 1)
            change = jnp.where(lane == 0, left, 0.0) - jnp.where(lane == LANES - 1, right, 0.0)
            line = row_transform(flat(total[row]) + change, pair_ref, rest_ref)
            total[row] = line.reshape(shares, modes, LANES)
        for step in range(group):
            row = base + step
            for to in range(1, shares):
                out_copy(row, to).start()
            own_copy(row).start()
        return carry

    lax.fori_loop(0, own_rows // group, take_group, 0)

    def arrive(row, carry):
        for step in range(1, shares):
            source = peer(step)
            arrived(home_row(source * own_rows + row), out_recv.at[row, source])
        own_copy(row).wait()
        return carry

    lax.fori_loop(0, own_rows, arrive, 0)

    def take_pair(pair, columns):
        line = [home[pl.ds(2 * pair + half, rows, stride=modes), :] for half in range(2)]
        line = col_transform(jnp.concatenate(line, axis=1), all_ref)
        line = spectrum[pair] - line
        spectrum[pair] = line
        alone = line * inverse[...]
        trace = pl.ds(8 * pair, 8)
        lane = lax.broadcasted_iota(jnp.int32, (LANES, LANES), 1)
        result = []
        for end in range(2):
            ends = jnp.broadcast_to(column_ref[:rows, 4 + end : 5 + end], (rows, 2 * LANES))
            result.append(jnp.sum(alone * ends, axis=0, keepdims=True))
            upright = jnp.concatenate([alone[:, :LANES], alone[:, LANES:]], axis=0)
            upright = jnp.sum(upright * lane_ref[end : end + 1, :], axis=1, keepdims=True)
            columns = jnp.where(lane == end * (LANES // 2) + pair, upright, columns)
        blank = jnp.zeros((2, LANES), jnp.float32)
        traces[trace, :] = jnp.concatenate(
            [blank, result[0][:, :LANES], result[0][:, LANES:],
             result[1][:, :LANES], result[1][:, LANES:], blank], axis=0
        )
        return columns

    def take_pairs(index, columns):
        for pair in range(unroll):
            columns = take_pair(index * unroll + pair, columns)
        return columns

    columns = lax.fori_loop(
        0, pairs // unroll, take_pairs, jnp.zeros((LANES, LANES), jnp.float32)
    )
    tall[...] = jnp.transpose(columns)
    for end in range(2):
        traces[pl.ds(end, pairs, stride=8), :] = tall[pl.ds(end * (LANES // 2), pairs), :]
    save = pltpu.make_async_copy(spectrum, spec_ref, spec_sem)
    save.start()

    piece = lambda owner: pl.ds(owner * per * 8, per * 8)

    def trace_copy(step):
        to = other(step)
        return remote(
            traces.at[piece(to), :], got.at[piece(me), :], trace_send.at[step],
            trace_recv.at[me], **at_owner(to),
        )

    def flux_copy(step):
        to = other(step)
        return remote(
            back.at[piece(to), :], flux_ref.at[piece(me), :], flux_send.at[step],
            flux_recv.at[me], **at_owner(to),
        )

    for step in range(1, owners):
        trace_copy(step).start()
    got[piece(me), :] = traces[piece(me), :]
    load_join.wait()
    for step in range(1, owners):
        arrived(got.at[piece(other(step)), :], trace_recv.at[other(step)])
    solve_fluxes(plane, per, got, back, lane_ref, join, by_row, by_col, col_table, row_table)
    for step in range(1, owners):
        flux_copy(step).start()
    own_flux = pltpu.make_async_copy(
        back.at[piece(me), :], flux_ref.at[piece(me), :], flux_recv.at[me]
    )
    own_flux.start()

    def sent(row, carry):
        for step in range(1, shares):
            line_copy(row, step).wait_send()
            out_copy(row, step).wait_send()
        return carry

    lax.fori_loop(0, own_rows, sent, 0)
    for condition, copy in remote_copies:
        if condition is None:
            copy.wait_send()
        else:
            pl.when(condition)(copy.wait_send)
    save.wait()
    own_flux.wait()
    for step in range(1, owners):
        trace_copy(step).wait_send()
        flux_copy(step).wait_send()
        arrived(flux_ref.at[piece(other(step)), :], flux_recv.at[other(step)])


def finish_kernel(
    spec_ref, flux_ref, now_ref, before_ref, mean_ref, lane_ref, column_ref, rows_ref, cols_ref,
    fresh_ref, update_ref, inverse,
):
    rows = spec_ref.shape[1]
    column = lambda k: jnp.broadcast_to(column_ref[:rows, k : k + 1], (rows, LANES))

    @pl.when(pl.program_id(0) == 0)
    def start():
        inverse[...] = 1.0 / (storage_rate + mean_ref[0] * (column(3) + lane_ref[2:3, :]))

    upright = jnp.transpose(flux_ref[...])
    for pair in range(spec_ref.shape[0]):
        parts = []
        for half in range(2):
            beside = lambda kind: jnp.broadcast_to(
                upright[half * rows : (half + 1) * rows, 8 * pair + kind : 8 * pair + kind + 1],
                (rows, LANES),
            )
            over = lambda kind: flux_ref[8 * pair + kind : 8 * pair + kind + 1, :]
            part = spec_ref[pair, :, half * LANES : (half + 1) * LANES]
            part = part + (beside(1) * lane_ref[1:2, :] - beside(0) * lane_ref[0:1, :])
            part = part + (column(5) * over(4 + half) - column(4) * over(2 + half))
            parts.append(part * inverse[...])
        high, low = split_two(jnp.concatenate(parts, axis=1))
        part = product(rows_ref[...], jnp.concatenate([high, low, high], axis=0))
        high, low = split_two(jnp.concatenate([part[:, :LANES], part[:, LANES:]], axis=0))
        part = product(jnp.concatenate([high, low], axis=1), cols_ref[...])
        part = (part[:, :LANES] + part[:, LANES:]).reshape(2, rows, LANES)
        mode = slice(2 * pair, 2 * pair + 2)
        update_ref[mode] = part
        before = before_ref[mode]
        fresh_ref[mode] = before + relax_weight * (now_ref[mode] - before + step_length * part)


def cosine_table(length):
    freq, cells = np.arange(length)[:, None], np.arange(length)[None, :]
    factor = np.where(freq == 0, math.sqrt(1.0 / length), math.sqrt(2.0 / length))
    return factor * np.cos((freq * (2 * cells + 1) % (4 * length)) * (math.pi / (2 * length)))


def pieces(table):
    found, rest = [], table.astype(np.float32)
    for _ in range(3):
        found.append(rest.astype(BF16))
        rest = rest - found[-1].astype(np.float32)
    return found


def constant_tables(count_x, rows, width):
    eigen = lambda count: 2.0 - 2.0 * np.cos(np.arange(count) * (math.pi / count))
    row_table, col_table = cosine_table(rows), cosine_table(width)
    far_table = cosine_table(count_x * width)
    join = np.einsum("kix,lx->kil", far_table.reshape(-1, count_x, width), col_table)
    twice = lambda a: np.concatenate([a, a])
    lanes = [
        col_table[:, 0], col_table[:, -1], eigen(width),
        twice(row_table[:, 0]), twice(row_table[:, -1]), twice(eigen(rows)),
    ]
    columns = [lanes[2], lanes[0], lanes[1], lanes[5], lanes[3], lanes[4]]
    grow = lambda a: np.pad(np.stack(a), ((0, 8 - len(a)), (0, 0))).astype(np.float32)
    high, middle, low = pieces(col_table.T)
    front = pieces(col_table)
    pair = np.block([[high, middle], [high, middle]])
    rest = np.concatenate([high, low])
    back = np.block([[front[0], front[1]], [front[0], np.zeros_like(high)]])
    high, middle, low = pieces(row_table)
    every = np.concatenate([high, high, middle, middle, high, low], axis=1)
    high, low, _ = pieces(row_table.T)
    rows_back = np.concatenate([high, high, low], axis=1)
    return dict(
        pair=pair, rest=rest, every=every, lanes=grow(lanes), columns=grow(columns).T.copy(),
        far=grow([eigen(count_x * width)]), join=join.reshape(len(far_table), -1).astype(np.float32),
        rows=rows_back, cols=back,
    )


def chebyshev_step(
    field, field_before, source, log_fields, weights, mean_perm, node_index, mode_index
):
    modes, rows, width = field.shape
    count_x, count_y, shares = (lax.axis_size(axis) for axis in ("gx", "gy", "sa"))
    padded = round_up(modes, 16)
    grow = lambda a, size, dim: jnp.pad(
        a, [(0, size - a.shape[d] if d == dim else 0) for d in range(a.ndim)]
    )
    field, field_before, source = (grow(a, padded, 0) for a in (field, field_before, source))
    mean = mean_perm.reshape(1)
    tables = constant_tables(count_x, rows, width)
    pairs, owners = padded // 2, count_x * count_y
    per = -(-pairs // owners)
    depth_solve = round_up(count_y * per, 8)
    extra = 8 * (depth_solve - count_y * per)
    own_rows = rows // shares
    nodes = node_index.shape[0]
    all_nodes = round_up(nodes, NODE_BLOCK)
    modes_of = grow(mode_index.reshape(shares, modes, -1), padded, 1).reshape(shares * padded, -1)
    levels = log_fields.shape[0]
    group = math.gcd(own_rows, 8)
    every = shares * padded
    depth = round_up(3 * every, LANES)
    slots = own_rows + 2
    vmem = lambda shape, kind=jnp.float32: pltpu.VMEM(shape, kind)
    dma = lambda *shape: pltpu.SemaphoreType.DMA(shape)
    place = pl.BlockSpec(memory_space=pl.ANY)
    whole = pl.BlockSpec(memory_space=pltpu.VMEM)
    numbers = pl.BlockSpec(memory_space=pltpu.SMEM)
    spectrum, fluxes = pl.pallas_call(
        functools.partial(node_kernel, (count_x, count_y, shares, group)),
        in_specs=[place, whole, whole, whole, whole]
        + [place, numbers] + [whole] * 6 + [place],
        out_specs=[place, place],
        out_shape=[
            jax.ShapeDtypeStruct((pairs, rows, 2 * width), jnp.float32),
            jax.ShapeDtypeStruct((owners * per * 8, LANES), jnp.float32),
        ],
        scratch_shapes=[
            vmem((slots, shares, padded, LANES)),
            vmem((2, levels, LANES)),
            vmem((2, levels, LANES)),
            vmem((4, shares, padded, LANES)),
            vmem((own_rows, shares, padded, LANES)),
            vmem((group // 2, depth, 2 * LANES), BF16),
            vmem((slots, LANES, LANES), BF16),
            vmem((all_nodes, depth), BF16),
            vmem((all_nodes, LANES), BF16),
            vmem((2 * every, all_nodes), BF16),
            vmem((every, LANES)),
            vmem((all_nodes, LANES)),
            vmem((all_nodes, LANES)),
            vmem((all_nodes, LANES)),
            vmem((rows * padded, LANES)),
            vmem((pairs, rows, 2 * LANES)),
            vmem((padded, rows, LANES)),
            vmem((owners * per * 8, LANES)),
            vmem((owners * per * 8 + extra, LANES)),
            vmem((owners * per * 8 + extra, LANES)),
            vmem((LANES, LANES)),
            vmem(tables["join"].shape),
            vmem((rows, 2 * LANES)),
            vmem((LANES, 4 * LANES)),
            vmem((2 * LANES, 2 * LANES)),
            vmem((count_x - 1, round_up(count_x - 1, 8), LANES)),
            vmem((2 * count_y - 3, depth_solve, count_x * width)),
            vmem((padded, rows, LANES)),
            vmem((2, padded, LANES)),
            vmem((2, levels, LANES)),
            vmem((node_index.shape[1], all_nodes), jnp.int32),
            vmem((1, all_nodes)),
            vmem((round_up(every, LANES), LANES)),
            dma(3), pltpu.SemaphoreType.DMA, dma(owners), dma(owners), dma(owners), dma(owners),
            dma(own_rows, shares), dma(slots, shares), dma(2 * shares), dma(shares, 4),
            dma(4, shares), dma(4), dma(4), dma(own_rows, shares), dma(own_rows, shares),
        ],
        compiler_params=pltpu.CompilerParams(
            collective_id=0, has_side_effects=True, vmem_limit_bytes=56 * 1024 * 1024
        ),
    )(
        field, log_fields, node_index.T, modes_of.T, weights[None, :], source, mean,
        *(tables[name] for name in ("pair", "rest", "every", "lanes", "columns", "far", "join")),
    )
    step = math.gcd(pairs, 8)
    block = pl.BlockSpec((2 * step, rows, width), lambda n: (n, 0, 0))
    still = lambda a: pl.BlockSpec(a.shape, lambda n: (0,) * a.ndim)
    shape = jax.ShapeDtypeStruct(field.shape, jnp.float32)
    fresh, update = pl.pallas_call(
        finish_kernel,
        grid=(pairs // step,),
        in_specs=[
            pl.BlockSpec((step, rows, 2 * width), lambda n: (n, 0, 0)),
            pl.BlockSpec((8 * step, LANES), lambda n: (n, 0)),
            block, block, numbers,
        ] + [still(tables[name]) for name in ("lanes", "columns", "rows", "cols")],
        out_specs=[block, block],
        out_shape=[shape, shape],
        scratch_shapes=[vmem((rows, LANES))],
        compiler_params=pltpu.CompilerParams(dimension_semantics=("arbitrary",)),
    )(
        spectrum, fluxes, field, field_before, mean,
        *(tables[name] for name in ("lanes", "columns", "rows", "cols")),
    )
    return (fresh[:modes], update[:modes])


def solution(mesh):
    return jax.shard_map(
        chebyshev_step,
        mesh=mesh,
        in_specs=(
            P("sa", "gy", "gx"),
            P("sa", "gy", "gx"),
            P("sa", "gy", "gx"),
            P(None, ("gy", "sa"), "gx"),
            P(),
            P(),
            P(),
            P(),
        ),
        out_specs=(P("sa", "gy", "gx"), P("sa", "gy", "gx")),
        check_vma=False,
    )
```

```python
import functools
import math

import jax
import jax.numpy as jnp
import numpy as np
from jax import lax
from jax.experimental import pallas as pl
from jax.experimental.pallas import tpu as pltpu
from jax.sharding import PartitionSpec as P


HIGHEST = lax.Precision.HIGHEST
hermite_points = (
    0.0,
    -1.7320508075688772,
    1.7320508075688772,
    -1.355626179974266,
    1.355626179974266,
    -2.8569700138728056,
    2.8569700138728056,
)
storage_rate = 0.0004
relax_weight = 1.6
step_length = 0.3


LANES = 128
NODE_BLOCK = 512
LOG_DEPTH = 16
EARLY = 4
BF16 = jnp.bfloat16


def round_up(value, step):
    return -(-value // step) * step


def product(left, right):
    return jnp.dot(left, right, preferred_element_type=jnp.float32)


def split_two(block):
    high = block.astype(BF16)
    return (high, (block - high.astype(jnp.float32)).astype(BF16))


def split_three(block):
    high = block.astype(BF16)
    rest = block - high.astype(jnp.float32)
    middle = rest.astype(BF16)
    return (high, middle, (rest - middle.astype(jnp.float32)).astype(BF16))


def exact(left, right):
    return jnp.dot(left, right, precision=HIGHEST, preferred_element_type=jnp.float32)


def row_transform(block, pair_ref, rest_ref):
    high, middle, low = split_three(block)
    both = product(jnp.concatenate([high, middle], axis=1), pair_ref[...])
    both = both[:, :LANES] + both[:, LANES:]
    return both + product(jnp.concatenate([low, high], axis=1), rest_ref[...])


def col_transform(block, all_ref):
    high, middle, low = split_three(block)
    stack = jnp.concatenate([high, middle, high, middle, low, high], axis=0)
    return product(all_ref[...], stack)


def make_tables(sizes, per, mean, lane_ref, column_ref, far_ref, inverse, by_row, by_col, col_table, row_table):
    count_x, count_y = sizes
    half = LANES // 2
    column = lambda k, rows=LANES: jnp.broadcast_to(column_ref[:rows, k : k + 1], (rows, LANES))
    lanes = lambda k: lane_ref[k : k + 1, :]
    upright = 1.0 / (storage_rate + mean * (column(0) + lanes(5)))
    flat = 1.0 / (storage_rate + mean * (column(3) + lanes(2)))
    inverse[:, :LANES] = flat[:half]
    inverse[:, LANES:] = flat[:half]
    lane = lax.broadcasted_iota(jnp.int32, (LANES, LANES), 1)
    row = lax.broadcasted_iota(jnp.int32, (LANES, LANES), 0)
    for end in range(2):
        part = upright * column(1 + end)
        by_col[:LANES, end * LANES : (end + 1) * LANES] = jnp.where(lane < half, part, 0.0)
        by_col[LANES:, end * LANES : (end + 1) * LANES] = jnp.where(lane < half, 0.0, part)
        part = flat * column(4 + end)
        by_row[:, 2 * end * LANES : (2 * end + 1) * LANES] = jnp.where(row < half, part, 0.0)
        by_row[:, (2 * end + 1) * LANES : (2 * end + 2) * LANES] = jnp.where(row < half, 0.0, part)

    def tables(count, same, cross):
        shrink = [
            1.0 / (1.0 / mean + 2.0 * same - 2.0 * math.cos(n * math.pi / count) * cross)
            for n in range(1, count)
        ]
        sine = lambda a, b: math.sin(a * b % (2 * count) * math.pi / count)
        return [
            [
                sum((2.0 / count) * sine(n, a) * sine(n, b) * shrink[n - 1] for n in range(1, count))
                for b in range(1, count)
            ]
            for a in range(1, count)
        ]

    total = lambda a: jnp.sum(a, axis=0, keepdims=True)
    ends = column(1), column(2)
    found = tables(
        count_x, total(upright * ends[0] * ends[0]), total(upright * ends[0] * ends[1])
    )
    for a in range(count_x - 1):
        for b in range(count_x - 1):
            col_table[a, b : b + 1, :] = found[a][b]
    far = far_ref[0:1, :]
    wide = lambda k: jnp.broadcast_to(column_ref[:half, k : k + 1], (half, far.shape[1]))
    deep = 1.0 / (storage_rate + mean * (wide(3) + far))
    found = tables(
        count_y, total(deep * wide(4) * wide(4)), total(deep * wide(4) * wide(5))
    )
    depth = row_table.shape[1]
    where_row = lax.broadcasted_iota(jnp.int32, (depth, far.shape[1]), 0) // per
    for shift in range(-(count_y - 2), count_y - 1):
        table = jnp.zeros((depth, far.shape[1]), jnp.float32)
        for a in range(count_y - 1):
            if 0 <= a + shift < count_y - 1:
                table = jnp.where(where_row == a, found[a][a + shift], table)
        row_table[shift + count_y - 2] = table


def solve_fluxes(sizes, per, got, back, lane_ref, join_ref, by_row, by_col, col_table, row_table):
    count_x, count_y = sizes
    depth = row_table.shape[1]
    rows = count_y * per
    lanes = lambda k: lane_ref[k : k + 1, :]
    take = lambda block, kind: got[pl.ds(block * rows * 8 + kind, depth, stride=8), :]
    row = lax.broadcasted_iota(jnp.int32, (depth, LANES), 0)
    up = lambda a, by=1: pltpu.roll(a, (-by * per) % depth, 0)
    down = lambda a: jnp.where(row < per, 0.0, pltpu.roll(a, per, 0))
    blocks, cuts = range(count_x), range(1, count_x)

    def through_cols(first, last):
        jump = [first[cut] - last[cut - 1] for cut in cuts]
        return [
            sum(col_table[a, b : b + 1, :] * jump[b] for b in range(count_x - 1))
            for a in range(count_x - 1)
        ]

    fluxes = through_cols([take(b, 0) for b in blocks], [take(b, 1) for b in blocks])
    spread = [exact(flux, by_row[...]) for flux in fluxes]

    def at_row(block, end, half):
        part = slice((2 * end + half) * LANES, (2 * end + half + 1) * LANES)
        value = take(block, 2 + 2 * end + half)
        if block < count_x - 1:
            value = value + spread[block][:, part] * lanes(1)
        if block > 0:
            value = value - spread[block - 1][:, part] * lanes(0)
        return value

    jump = jnp.concatenate(
        [
            jnp.concatenate([up(at_row(b, 0, half)) - at_row(b, 1, half) for b in blocks], axis=1)
            for half in range(2)
        ],
        axis=0,
    )
    far = lax.dot_general(
        jump, join_ref[...], (((1,), (1,)), ((), ())), precision=HIGHEST,
        preferred_element_type=jnp.float32,
    )
    mixed = []
    for half in range(2):
        part = far[half * depth : (half + 1) * depth]
        mixed.append(sum(
            row_table[shift + count_y - 2] * (up(part, shift) if shift else part)
            for shift in range(-(count_y - 2), count_y - 1)
        ))
    near = exact(jnp.concatenate(mixed, axis=0), join_ref[...])
    through_rows = [
        [near[half * depth : (half + 1) * depth, b * LANES : (b + 1) * LANES] for half in range(2)]
        for b in blocks
    ]
    ends = []
    for b in blocks:
        reach = exact(jnp.concatenate(through_rows[b], axis=1), by_col[...])
        ends.append([
            lanes(4) * reach[:, end * LANES : (end + 1) * LANES]
            - lanes(3) * down(reach[:, end * LANES : (end + 1) * LANES])
            for end in range(2)
        ])
    more = through_cols([end[0] for end in ends], [end[1] for end in ends])
    fluxes = [a + b for a, b in zip(fluxes, more)]
    nothing = jnp.zeros((depth, LANES), jnp.float32)
    for b in blocks:
        left = fluxes[b - 1] if b > 0 else nothing
        right = fluxes[b] if b < count_x - 1 else nothing
        top = [down(part) for part in through_rows[b]]
        for kind, value in enumerate([left, right] + top + through_rows[b]):
            back[pl.ds(b * rows * 8 + kind, depth, stride=8), :] = value


def stacked(parts, depth):
    missing = depth - sum(part.shape[0] for part in parts)
    if missing:
        parts = parts + [jnp.zeros((missing,) + parts[0].shape[1:], parts[0].dtype)]
    return jnp.concatenate(parts, axis=0)


def node_kernel(
    sizes, field_ref, log_ref, node_ref, mode_ref, weight_ref,
    source_ref, mean_ref, pair_ref, rest_ref, all_ref, lane_ref, column_ref, far_ref, join_ref,
    spec_ref, flux_ref,
    lines, log_lines, log_sides, sides, total, line_op, log_op, basis_op, germ_op, weight_op,
    edge, value_prev, half_prev, flux_prev,
    home, spectrum, origin, traces, got, back, tall, join,
    inverse, by_row, by_col, col_table, row_table,
    block_field, field_cols, log_cols, picks, shares_of, degrees,
    load_sem, spec_sem, trace_send, trace_recv, flux_send, flux_recv,
    line_send, line_recv, halo_send, side_send, side_recv, log_send, log_recv, out_send, out_recv,
):
    count_x, count_y, shares, group = sizes
    modes, rows, width = field_ref.shape
    own_rows = rows // shares
    every = shares * modes
    below, above = own_rows, own_rows + 1
    blocks = basis_op.shape[0] // NODE_BLOCK
    x, y, share = (lax.axis_index(axis) for axis in ("gx", "gy", "sa"))
    first_y = jnp.logical_and(y == 0, share == 0)
    last_y = jnp.logical_and(y == count_y - 1, share == shares - 1)
    not_first, not_last = jnp.logical_not(first_y), jnp.logical_not(last_y)
    peer = lambda step: lax.rem(share + step, shares)

    def remote(source, target, send, recv, **place):
        return pltpu.make_async_remote_copy(
            src_ref=source, dst_ref=target, send_sem=send, recv_sem=recv,
            device_id=place, device_id_type=pl.DeviceIdType.MESH,
        )

    def arrived(target, recv):
        pltpu.make_async_copy(target, target, recv).wait()

    load_field = pltpu.make_async_copy(field_ref, block_field, load_sem.at[2])
    load_field.start()
    load_origin = pltpu.make_async_copy(source_ref, origin, load_sem.at[0])
    load_origin.start()
    load_join = pltpu.make_async_copy(join_ref, join, load_sem.at[1])
    load_join.start()

    barrier = pltpu.get_barrier_semaphore()
    greet = lambda **place: pl.semaphore_signal(
        barrier, inc=1, device_id=place, device_id_type=pl.DeviceIdType.MESH
    )
    for step in range(1, shares):
        greet(sa=peer(step))
    owners = count_x * count_y
    me = x * count_y + y
    other = lambda step: lax.rem(me + step, owners)
    at_owner = lambda owner: dict(gx=lax.div(owner, count_y), gy=lax.rem(owner, count_y))
    for step in range(1, owners):
        greet(**at_owner(other(step)))
    conditions = (
        (x > 0, dict(gx=x - 1)), (x < count_x - 1, dict(gx=x + 1)),
        (y > 0, dict(gy=y - 1)), (y < count_y - 1, dict(gy=y + 1)),
    )
    for condition, place in conditions:
        @pl.when(condition)
        def _():
            for step in range(1, shares):
                greet(sa=peer(step), **place)
    sides_met = sum(condition.astype(jnp.int32) for condition, _ in conditions)
    pl.semaphore_wait(barrier, owners - 1 + (shares - 1) * (1 + sides_met))

    remote_copies = []

    def start(condition, copy):
        remote_copies.append((condition, copy))
        if condition is None:
            copy.start()
        else:
            pl.when(condition)(copy.start)

    row_of = lambda row: field_ref.at[:, row, :]
    flat_next = jnp.where(share == shares - 1, y + 1, y), lax.rem(share + 1, shares)
    flat_last = jnp.where(share == 0, y - 1, y), lax.rem(share + shares - 1, shares)
    start(y > 0, remote(
        row_of(0), lines.at[below, share], halo_send.at[0], line_recv.at[below, share],
        gy=y - 1, sa=jnp.int32(shares - 1),
    ))
    start(y < count_y - 1, remote(
        row_of(rows - 1), lines.at[above, share], halo_send.at[1], line_recv.at[above, share],
        gy=y + 1, sa=jnp.int32(0),
    ))
    for step in range(1, shares):
        to = peer(step)
        start(to > 0, remote(
            row_of(jnp.maximum(to * own_rows - 1, 0)), lines.at[above, share],
            halo_send.at[2 * step], line_recv.at[above, share], sa=to,
        ))
        start(to < shares - 1, remote(
            row_of(jnp.minimum((to + 1) * own_rows, rows - 1)), lines.at[below, share],
            halo_send.at[2 * step + 1], line_recv.at[below, share], sa=to,
        ))
    own_above = pltpu.make_async_copy(
        row_of(jnp.maximum(share * own_rows - 1, 0)), lines.at[above, share],
        line_recv.at[above, share],
    )
    own_below = pltpu.make_async_copy(
        row_of(jnp.minimum((share + 1) * own_rows, rows - 1)), lines.at[below, share],
        line_recv.at[below, share],
    )
    pl.when(share > 0)(own_above.start)
    pl.when(share < shares - 1)(own_below.start)
    def line_copy(row, step):
        to = peer(step)
        return remote(
            row_of(to * own_rows + row), lines.at[row, share], line_send.at[row, step],
            line_recv.at[row, share], sa=to,
        )

    def send_lines(row, carry):
        for step in range(1, shares):
            line_copy(row, step).start()
        pltpu.make_async_copy(
            row_of(share * own_rows + row), lines.at[row, share], line_recv.at[row, share]
        ).start()
        return carry

    early = min(EARLY, own_rows)
    lax.fori_loop(0, early, send_lines, 0)
    pairs = modes // 2
    unroll = max(n for n in range(1, 6) if pairs % n == 0)
    pick_row = lax.broadcasted_iota(jnp.int32, (16, 2 * LANES), 0)
    pick_lane = lax.broadcasted_iota(jnp.int32, (16, 2 * LANES), 1) % LANES
    first_pick = jnp.logical_and(pick_row == 0, pick_lane == 0)
    last_pick = jnp.logical_and(pick_row == 1, pick_lane == LANES - 1)
    pick = jnp.where(jnp.logical_or(first_pick, last_pick), 1.0, 0.0).astype(BF16)

    def columns_of(block):
        return lax.dot_general(
            pick, jnp.concatenate(split_two(block), axis=1), (((1,), (1,)), ((), ())),
            preferred_element_type=jnp.float32,
        )

    log_cols[...] = jnp.zeros_like(log_cols)
    for level in range(log_ref.shape[0]):
        found = columns_of(log_ref[level])
        for end in range(2):
            log_cols[end, level : level + 1, :own_rows] = found[end : end + 1, :]
    load_field.wait()

    def take_columns(index, carry):
        for pair in range(unroll):
            mode = 2 * (index * unroll + pair)
            found = columns_of(block_field[pl.ds(mode, 2)].reshape(2 * rows, LANES))
            for half in range(2):
                part = pltpu.roll(found, LANES - rows, 1) if half else found
                for end in range(2):
                    field_cols[end, pl.ds(mode + half, 1), :] = part[end : end + 1, :]
        return carry

    lax.fori_loop(0, pairs // unroll, take_columns, 0)
    log_copies = (
        (not_last, log_ref.at[:, own_rows - 1, :], log_lines.at[1], 0,
         dict(gy=flat_next[0], sa=flat_next[1])),
        (not_first, log_ref.at[:, 0, :], log_lines.at[0], 1,
         dict(gy=flat_last[0], sa=flat_last[1])),
        (x < count_x - 1, log_cols.at[1], log_sides.at[0], 2, dict(gx=x + 1)),
        (x > 0, log_cols.at[0], log_sides.at[1], 3, dict(gx=x - 1)),
    )
    for condition, source, target, slot, place in log_copies:
        start(condition, remote(source, target, log_send.at[slot], log_recv.at[slot], **place))
    for step in range(shares):
        to = peer(step)
        for kind in range(2):
            source = field_cols.at[kind]
            if step:
                start(None, remote(
                    source, sides.at[kind, share], side_send.at[step, kind],
                    side_recv.at[kind, share], sa=to,
                ))
            else:
                pltpu.make_async_copy(
                    source, sides.at[kind, share], side_recv.at[kind, share]
                ).start()
        start(x > 0, remote(
            field_cols.at[0], sides.at[2, share], side_send.at[step, 2],
            side_recv.at[2, share], gx=x - 1, sa=to,
        ))
        start(x < count_x - 1, remote(
            field_cols.at[1], sides.at[3, share], side_send.at[step, 3],
            side_recv.at[3, share], gx=x + 1, sa=to,
        ))

    lax.fori_loop(early, own_rows, send_lines, 0)
    per = traces.shape[0] // 8 // owners
    plane = (count_x, count_y)
    beyond = got.shape[0] - traces.shape[0]
    if beyond:
        got[traces.shape[0] :, :] = jnp.zeros((beyond, LANES), jnp.float32)
    traces[...] = jnp.zeros_like(traces)
    make_tables(
        plane, per, mean_ref[0], lane_ref, column_ref, far_ref,
        inverse, by_row, by_col, col_table, row_table,
    )

    weight_op[...] = jnp.zeros_like(weight_op)
    total[...] = jnp.zeros_like(total)

    nodes_given = node_ref.shape[1]
    picks[...] = jnp.zeros_like(picks)
    picks[:, :nodes_given] = node_ref[...]
    shares_of[...] = jnp.zeros_like(shares_of)
    shares_of[:, :nodes_given] = weight_ref[...]
    degrees[...] = jnp.zeros_like(degrees)
    for start_at in range(0, every, LANES):
        width_at = min(LANES, every - start_at)
        degrees[start_at : start_at + mode_ref.shape[0], :width_at] = mode_ref[
            :, start_at : start_at + width_at
        ].astype(jnp.float32)
        here = slice(start_at, start_at + LANES)
        degrees[here, :] = jnp.transpose(degrees[here, :])

    def make_basis(block, carry):
        lanes = pl.ds(pl.multiple_of(block * LANES, LANES), LANES)
        picked = picks[:, lanes]
        germs = jnp.zeros(picked.shape, jnp.float32)
        for level, point in enumerate(hermite_points):
            germs = jnp.where(picked == level, point, germs)
        square = germs * germs
        second = (square - 1.0) / math.sqrt(2.0)
        third = (square * germs - 3.0 * germs) / math.sqrt(6.0)
        values = jnp.ones((every, LANES), jnp.float32)
        for germ in range(germs.shape[0]):
            degree = jnp.broadcast_to(degrees[:every, germ : germ + 1], (every, LANES))
            at = lambda table: jnp.broadcast_to(table[germ : germ + 1, :], (every, LANES))
            values = values * jnp.where(
                degree == 0, 1.0,
                jnp.where(degree == 1, at(germs), jnp.where(degree == 2, at(second), at(third))),
            )
        high, low = split_two(values)
        wide = lambda a: a.astype(jnp.float32)
        stack = stacked([wide(high), wide(high), wide(low)], basis_op.shape[1])
        basis_op[lanes, :] = jnp.transpose(stack).astype(BF16)
        high, low = split_two(values * (2.0 * shares_of[:, lanes]))
        weight_op[:every, lanes] = high
        weight_op[every:, lanes] = low
        spread = stacked([-jnp.ones((1, LANES), jnp.float32), -germs], LOG_DEPTH)
        high, low = split_two(spread)
        stack = stacked([wide(high), wide(high), wide(low)], LANES)
        germ_op[lanes, :] = jnp.transpose(stack).astype(BF16)
        return carry

    lax.fori_loop(0, basis_op.shape[0] // LANES, make_basis, 0)

    def log_stack(block):
        high, low = split_two(stacked([block], LOG_DEPTH))
        return stacked([high, low, high], LANES)

    def field_stack(block):
        high, low = split_two(block)
        return stacked([high, low, high], line_op.shape[1])

    for condition, _, target, slot, _ in (
        (not_first, None, log_lines.at[1], 0, None), (not_last, None, log_lines.at[0], 1, None),
        (x > 0, None, log_sides.at[0], 2, None), (x < count_x - 1, None, log_sides.at[1], 3, None),
    ):
        @pl.when(condition)
        def _():
            arrived(target, log_recv.at[slot])

    def make_log(row, carry):
        log_op[row] = log_stack(log_ref[:, row, :])
        return carry

    lax.fori_loop(0, own_rows, make_log, 0)
    log_op[below] = log_stack(
        jnp.where(last_y, log_ref[:, own_rows - 1, :], log_lines[0])
    )
    log_op[above] = log_stack(jnp.where(first_y, log_ref[:, 0, :], log_lines[1]))

    def at_nodes(nodes, field, logs):
        return (product(basis_op[nodes, :], field), jnp.exp(product(germ_op[nodes, :], logs)))

    def flux(later, earlier, half_later, half_earlier):
        return (later - earlier) * pl.reciprocal(half_later + half_earlier)

    def project(nodes, applied):
        high = applied.astype(BF16)
        rest = applied - high.astype(jnp.float32)
        middle = rest.astype(BF16)
        low = (rest - middle.astype(jnp.float32)).astype(BF16)
        both = product(weight_op[:, nodes], high) + product(weight_op[:, nodes], middle)
        return both[:every] + both[every:] + product(weight_op[:every, nodes], low)

    node_slice = lambda block: pl.ds(pl.multiple_of(block * NODE_BLOCK, NODE_BLOCK), NODE_BLOCK)

    for kind in range(4):
        condition = (None, None, x < count_x - 1, x > 0)[kind]
        for source in range(shares):
            wait = lambda: arrived(sides.at[kind, source], side_recv.at[kind, source])
            wait() if condition is None else pl.when(condition)(wait)
    flat = lambda ref: ref.reshape(every, LANES)
    turn = lax.rem(LANES - share * own_rows, LANES)
    side = [pltpu.roll(flat(sides[kind]), turn, 1) for kind in range(4)]
    log_first, log_last = log_cols[0], log_cols[1]
    before = jnp.where(x == 0, side[0], side[3])
    after = jnp.where(x == count_x - 1, side[1], side[2])
    log_before = jnp.where(x == 0, log_first, log_sides[0])
    log_after = jnp.where(x == count_x - 1, log_last, log_sides[1])

    def beside(low_part, high_part):
        lane = lax.broadcasted_iota(jnp.int32, low_part.shape, 1)
        return jnp.where(lane < own_rows, low_part, pltpu.roll(high_part, own_rows, 1))

    line_op[0, :, :LANES] = field_stack(beside(before, side[1]))
    line_op[0, :, LANES:] = field_stack(beside(side[0], after))
    log_edge = jnp.concatenate(
        [log_stack(beside(log_before, log_last)), log_stack(beside(log_first, log_after))], axis=1
    )
    edge[...] = jnp.zeros_like(edge)

    def make_edge(block, carry):
        nodes = node_slice(block)
        values, halves = at_nodes(nodes, line_op[0], log_edge)
        edge[...] += project(nodes, flux(
            values[:, LANES:], values[:, :LANES], halves[:, LANES:], halves[:, :LANES]
        ))
        return carry

    lax.fori_loop(0, blocks, make_edge, 0)

    def wait_line(row):
        for source in range(shares):
            arrived(lines.at[row, source], line_recv.at[row, source])

    wait_line(0)
    pl.when(not_first)(lambda: wait_line(above))
    line = flat(lines[0])
    line_op[0, :, :LANES] = field_stack(jnp.where(first_y, line, flat(lines[above])))
    line_op[0, :, LANES:] = field_stack(line)

    def begin(block, carry):
        nodes = node_slice(block)
        logs = jnp.concatenate([log_op[above], log_op[0]], axis=1)
        values, halves = at_nodes(nodes, line_op[0], logs)
        value_prev[nodes, :] = values[:, LANES:]
        half_prev[nodes, :] = halves[:, LANES:]
        flux_prev[nodes, :] = flux(
            values[:, LANES:], values[:, :LANES], halves[:, LANES:], halves[:, :LANES]
        )
        return carry

    lax.fori_loop(0, blocks, begin, 0)

    home_row = lambda row: home.at[pl.ds(row * modes, modes), :]

    def out_copy(row, step):
        to = peer(step)
        return remote(
            total.at[row, to], home_row(share * own_rows + row), out_send.at[row, step],
            out_recv.at[row, share], sa=to,
        )

    def own_copy(row):
        return pltpu.make_async_copy(
            total.at[row, share], home_row(share * own_rows + row), out_recv.at[row, share]
        )

    def take_origin(index, carry):
        for pair in range(unroll):
            one_origin(index * unroll + pair)
        return carry

    def one_origin(pair):
        block = origin[pl.ds(2 * pair, 2)].reshape(2 * rows, LANES)
        block = row_transform(block, pair_ref, rest_ref)
        spectrum[pair] = col_transform(
            jnp.concatenate([block[:rows], block[rows:]], axis=1), all_ref
        )

    groups = own_rows // group

    def take_group(index, carry):
        base = index * group
        for ahead in range(1, group + 1):
            row = base + ahead
            if ahead < group:
                wait_line(row)
            else:
                pl.when(jnp.logical_or(row < own_rows, not_last))(lambda: wait_line(row))
            line = flat(lines[row])
            if ahead == group:
                line = jnp.where(
                    jnp.logical_and(row == own_rows, last_y), flat(lines[row - 1]), line
                )
            place = pl.ds((ahead - 1) % 2 * LANES, LANES)
            line_op[(ahead - 1) // 2, :, place] = field_stack(line)

        def take_nodes(block, carry):
            nodes = node_slice(block)
            value, half, flux_up = value_prev[nodes, :], half_prev[nodes, :], flux_prev[nodes, :]
            inside = lax.broadcasted_iota(jnp.int32, value.shape, 1) < LANES - 1
            for pair in range(group // 2):
                row = base + 2 * pair
                logs = jnp.concatenate([log_op[row + 1], log_op[row + 2]], axis=1)
                values, halves = at_nodes(nodes, line_op[pair], logs)
                applied = []
                for here in range(2):
                    value_next = values[:, here * LANES : (here + 1) * LANES]
                    half_next = halves[:, here * LANES : (here + 1) * LANES]
                    flux_down = flux(value_next, value, half_next, half)
                    across = jnp.where(
                        inside,
                        flux(
                            pltpu.roll(value, LANES - 1, 1), value,
                            pltpu.roll(half, LANES - 1, 1), half,
                        ),
                        0.0,
                    )
                    applied.append(
                        (0.5 * storage_rate) * value
                        - (across - pltpu.roll(across, 1, 1)) - (flux_down - flux_up)
                    )
                    value, half, flux_up = value_next, half_next, flux_down
                sums = project(nodes, jnp.concatenate(applied, axis=1))
                parts = sums.reshape(shares, modes, 2 * LANES)
                total[row] += parts[:, :, :LANES]
                total[row + 1] += parts[:, :, LANES:]
            value_prev[nodes, :] = value
            half_prev[nodes, :] = half
            flux_prev[nodes, :] = flux_up
            return carry

        lax.fori_loop(0, blocks, take_nodes, 0, unroll=True)
        lane = lax.broadcasted_iota(jnp.int32, (every, LANES), 1)
        for step in range(group):
            row = base + step
            left = pltpu.roll(edge[...], lax.rem(LANES - row, LANES), 1)
            right = pltpu.roll(edge[...], LANES - 1 - own_rows - row, 1)
            change = jnp.where(lane == 0, left, 0.0) - jnp.where(lane == LANES - 1, right, 0.0)
            line = row_transform(flat(total[row]) + change, pair_ref, rest_ref)
            total[row] = line.reshape(shares, modes, LANES)
        for step in range(group):
            row = base + step
            for to in range(1, shares):
                out_copy(row, to).start()
            own_copy(row).start()
        return carry

    lax.fori_loop(0, groups, take_group, 0)
    load_origin.wait()
    lax.fori_loop(0, pairs // unroll, take_origin, 0)

    def arrive(row, carry):
        for step in range(1, shares):
            source = peer(step)
            arrived(home_row(source * own_rows + row), out_recv.at[row, source])
        own_copy(row).wait()
        return carry

    lax.fori_loop(0, own_rows, arrive, 0)

    def take_pair(pair, columns):
        line = [home[pl.ds(2 * pair + half, rows, stride=modes), :] for half in range(2)]
        line = col_transform(jnp.concatenate(line, axis=1), all_ref)
        line = spectrum[pair] - line
        spectrum[pair] = line
        alone = line * inverse[...]
        trace = pl.ds(8 * pair, 8)
        lane = lax.broadcasted_iota(jnp.int32, (LANES, LANES), 1)
        result = []
        for end in range(2):
            ends = jnp.broadcast_to(column_ref[:rows, 4 + end : 5 + end], (rows, 2 * LANES))
            result.append(jnp.sum(alone * ends, axis=0, keepdims=True))
            upright = jnp.concatenate([alone[:, :LANES], alone[:, LANES:]], axis=0)
            upright = jnp.sum(upright * lane_ref[end : end + 1, :], axis=1, keepdims=True)
            columns = jnp.where(lane == end * (LANES // 2) + pair, upright, columns)
        blank = jnp.zeros((2, LANES), jnp.float32)
        traces[trace, :] = jnp.concatenate(
            [blank, result[0][:, :LANES], result[0][:, LANES:],
             result[1][:, :LANES], result[1][:, LANES:], blank], axis=0
        )
        return columns

    def take_pairs(index, columns):
        for pair in range(unroll):
            columns = take_pair(index * unroll + pair, columns)
        return columns

    columns = lax.fori_loop(
        0, pairs // unroll, take_pairs, jnp.zeros((LANES, LANES), jnp.float32)
    )
    tall[...] = jnp.transpose(columns)
    for end in range(2):
        traces[pl.ds(end, pairs, stride=8), :] = tall[pl.ds(end * (LANES // 2), pairs), :]
    save = pltpu.make_async_copy(spectrum, spec_ref, spec_sem)
    save.start()

    piece = lambda owner: pl.ds(owner * per * 8, per * 8)

    def trace_copy(step):
        to = other(step)
        return remote(
            traces.at[piece(to), :], got.at[piece(me), :], trace_send.at[step],
            trace_recv.at[me], **at_owner(to),
        )

    def flux_copy(step):
        to = other(step)
        return remote(
            back.at[piece(to), :], flux_ref.at[piece(me), :], flux_send.at[step],
            flux_recv.at[me], **at_owner(to),
        )

    for step in range(1, owners):
        trace_copy(step).start()
    got[piece(me), :] = traces[piece(me), :]
    load_join.wait()
    for step in range(1, owners):
        arrived(got.at[piece(other(step)), :], trace_recv.at[other(step)])
    solve_fluxes(plane, per, got, back, lane_ref, join, by_row, by_col, col_table, row_table)
    for step in range(1, owners):
        flux_copy(step).start()
    own_flux = pltpu.make_async_copy(
        back.at[piece(me), :], flux_ref.at[piece(me), :], flux_recv.at[me]
    )
    own_flux.start()

    def sent(row, carry):
        for step in range(1, shares):
            line_copy(row, step).wait_send()
            out_copy(row, step).wait_send()
        return carry

    lax.fori_loop(0, own_rows, sent, 0)
    for condition, copy in remote_copies:
        if condition is None:
            copy.wait_send()
        else:
            pl.when(condition)(copy.wait_send)
    save.wait()
    own_flux.wait()
    for step in range(1, owners):
        trace_copy(step).wait_send()
        flux_copy(step).wait_send()
        arrived(flux_ref.at[piece(other(step)), :], flux_recv.at[other(step)])


def finish_kernel(
    spec_ref, flux_ref, now_ref, before_ref, mean_ref, lane_ref, column_ref, rows_ref, cols_ref,
    fresh_ref, update_ref, inverse,
):
    rows = spec_ref.shape[1]
    column = lambda k: jnp.broadcast_to(column_ref[:rows, k : k + 1], (rows, LANES))

    @pl.when(pl.program_id(0) == 0)
    def start():
        inverse[...] = 1.0 / (storage_rate + mean_ref[0] * (column(3) + lane_ref[2:3, :]))

    upright = jnp.transpose(flux_ref[...])
    for pair in range(spec_ref.shape[0]):
        parts = []
        for half in range(2):
            beside = lambda kind: jnp.broadcast_to(
                upright[half * rows : (half + 1) * rows, 8 * pair + kind : 8 * pair + kind + 1],
                (rows, LANES),
            )
            over = lambda kind: flux_ref[8 * pair + kind : 8 * pair + kind + 1, :]
            part = spec_ref[pair, :, half * LANES : (half + 1) * LANES]
            part = part + (beside(1) * lane_ref[1:2, :] - beside(0) * lane_ref[0:1, :])
            part = part + (column(5) * over(4 + half) - column(4) * over(2 + half))
            parts.append(part * inverse[...])
        high, low = split_two(jnp.concatenate(parts, axis=1))
        part = product(rows_ref[...], jnp.concatenate([high, low, high], axis=0))
        high, low = split_two(jnp.concatenate([part[:, :LANES], part[:, LANES:]], axis=0))
        part = product(jnp.concatenate([high, low], axis=1), cols_ref[...])
        part = (part[:, :LANES] + part[:, LANES:]).reshape(2, rows, LANES)
        mode = slice(2 * pair, 2 * pair + 2)
        update_ref[mode] = part
        before = before_ref[mode]
        fresh_ref[mode] = before + relax_weight * (now_ref[mode] - before + step_length * part)


def cosine_table(length):
    freq, cells = np.arange(length)[:, None], np.arange(length)[None, :]
    factor = np.where(freq == 0, math.sqrt(1.0 / length), math.sqrt(2.0 / length))
    return factor * np.cos((freq * (2 * cells + 1) % (4 * length)) * (math.pi / (2 * length)))


def pieces(table):
    found, rest = [], table.astype(np.float32)
    for _ in range(3):
        found.append(rest.astype(BF16))
        rest = rest - found[-1].astype(np.float32)
    return found


def constant_tables(count_x, rows, width):
    eigen = lambda count: 2.0 - 2.0 * np.cos(np.arange(count) * (math.pi / count))
    row_table, col_table = cosine_table(rows), cosine_table(width)
    far_table = cosine_table(count_x * width)
    join = np.einsum("kix,lx->kil", far_table.reshape(-1, count_x, width), col_table)
    twice = lambda a: np.concatenate([a, a])
    lanes = [
        col_table[:, 0], col_table[:, -1], eigen(width),
        twice(row_table[:, 0]), twice(row_table[:, -1]), twice(eigen(rows)),
    ]
    columns = [lanes[2], lanes[0], lanes[1], lanes[5], lanes[3], lanes[4]]
    grow = lambda a: np.pad(np.stack(a), ((0, 8 - len(a)), (0, 0))).astype(np.float32)
    high, middle, low = pieces(col_table.T)
    front = pieces(col_table)
    pair = np.block([[high, middle], [high, middle]])
    rest = np.concatenate([high, low])
    back = np.block([[front[0], front[1]], [front[0], np.zeros_like(high)]])
    high, middle, low = pieces(row_table)
    every = np.concatenate([high, high, middle, middle, high, low], axis=1)
    high, low, _ = pieces(row_table.T)
    rows_back = np.concatenate([high, high, low], axis=1)
    return dict(
        pair=pair, rest=rest, every=every, lanes=grow(lanes), columns=grow(columns).T.copy(),
        far=grow([eigen(count_x * width)]), join=join.reshape(len(far_table), -1).astype(np.float32),
        rows=rows_back, cols=back,
    )


def chebyshev_step(
    field, field_before, source, log_fields, weights, mean_perm, node_index, mode_index
):
    modes, rows, width = field.shape
    count_x, count_y, shares = (lax.axis_size(axis) for axis in ("gx", "gy", "sa"))
    padded = round_up(modes, 16)
    grow = lambda a, size, dim: jnp.pad(
        a, [(0, size - a.shape[d] if d == dim else 0) for d in range(a.ndim)]
    )
    field, field_before, source = (grow(a, padded, 0) for a in (field, field_before, source))
    mean = mean_perm.reshape(1)
    tables = constant_tables(count_x, rows, width)
    pairs, owners = padded // 2, count_x * count_y
    per = -(-pairs // owners)
    depth_solve = round_up(count_y * per, 8)
    extra = 8 * (depth_solve - count_y * per)
    own_rows = rows // shares
    nodes = node_index.shape[0]
    all_nodes = round_up(nodes, NODE_BLOCK)
    modes_of = grow(mode_index.reshape(shares, modes, -1), padded, 1).reshape(shares * padded, -1)
    levels = log_fields.shape[0]
    group = math.gcd(own_rows, 8)
    every = shares * padded
    depth = round_up(3 * every, LANES)
    slots = own_rows + 2
    vmem = lambda shape, kind=jnp.float32: pltpu.VMEM(shape, kind)
    dma = lambda *shape: pltpu.SemaphoreType.DMA(shape)
    place = pl.BlockSpec(memory_space=pl.ANY)
    whole = pl.BlockSpec(memory_space=pltpu.VMEM)
    numbers = pl.BlockSpec(memory_space=pltpu.SMEM)
    spectrum, fluxes = pl.pallas_call(
        functools.partial(node_kernel, (count_x, count_y, shares, group)),
        in_specs=[place, whole, whole, whole, whole]
        + [place, numbers] + [whole] * 6 + [place],
        out_specs=[place, place],
        out_shape=[
            jax.ShapeDtypeStruct((pairs, rows, 2 * width), jnp.float32),
            jax.ShapeDtypeStruct((owners * per * 8, LANES), jnp.float32),
        ],
        scratch_shapes=[
            vmem((slots, shares, padded, LANES)),
            vmem((2, levels, LANES)),
            vmem((2, levels, LANES)),
            vmem((4, shares, padded, LANES)),
            vmem((own_rows, shares, padded, LANES)),
            vmem((group // 2, depth, 2 * LANES), BF16),
            vmem((slots, LANES, LANES), BF16),
            vmem((all_nodes, depth), BF16),
            vmem((all_nodes, LANES), BF16),
            vmem((2 * every, all_nodes), BF16),
            vmem((every, LANES)),
            vmem((all_nodes, LANES)),
            vmem((all_nodes, LANES)),
            vmem((all_nodes, LANES)),
            vmem((rows * padded, LANES)),
            vmem((pairs, rows, 2 * LANES)),
            vmem((padded, rows, LANES)),
            vmem((owners * per * 8, LANES)),
            vmem((owners * per * 8 + extra, LANES)),
            vmem((owners * per * 8 + extra, LANES)),
            vmem((LANES, LANES)),
            vmem(tables["join"].shape),
            vmem((rows, 2 * LANES)),
            vmem((LANES, 4 * LANES)),
            vmem((2 * LANES, 2 * LANES)),
            vmem((count_x - 1, round_up(count_x - 1, 8), LANES)),
            vmem((2 * count_y - 3, depth_solve, count_x * width)),
            vmem((padded, rows, LANES)),
            vmem((2, padded, LANES)),
            vmem((2, levels, LANES)),
            vmem((node_index.shape[1], all_nodes), jnp.int32),
            vmem((1, all_nodes)),
            vmem((round_up(every, LANES), LANES)),
            dma(3), pltpu.SemaphoreType.DMA, dma(owners), dma(owners), dma(owners), dma(owners),
            dma(own_rows, shares), dma(slots, shares), dma(2 * shares), dma(shares, 4),
            dma(4, shares), dma(4), dma(4), dma(own_rows, shares), dma(own_rows, shares),
        ],
        compiler_params=pltpu.CompilerParams(
            collective_id=0, has_side_effects=True, vmem_limit_bytes=56 * 1024 * 1024
        ),
    )(
        field, log_fields, node_index.T, modes_of.T, weights[None, :], source, mean,
        *(tables[name] for name in ("pair", "rest", "every", "lanes", "columns", "far", "join")),
    )
    step = math.gcd(pairs, 8)
    block = pl.BlockSpec((2 * step, rows, width), lambda n: (n, 0, 0))
    still = lambda a: pl.BlockSpec(a.shape, lambda n: (0,) * a.ndim)
    shape = jax.ShapeDtypeStruct(field.shape, jnp.float32)
    fresh, update = pl.pallas_call(
        finish_kernel,
        grid=(pairs // step,),
        in_specs=[
            pl.BlockSpec((step, rows, 2 * width), lambda n: (n, 0, 0)),
            pl.BlockSpec((8 * step, LANES), lambda n: (n, 0)),
            block, block, numbers,
        ] + [still(tables[name]) for name in ("lanes", "columns", "rows", "cols")],
        out_specs=[block, block],
        out_shape=[shape, shape],
        scratch_shapes=[vmem((rows, LANES))],
        compiler_params=pltpu.CompilerParams(dimension_semantics=("arbitrary",)),
    )(
        spectrum, fluxes, field, field_before, mean,
        *(tables[name] for name in ("lanes", "columns", "rows", "cols")),
    )
    return (fresh[:modes], update[:modes])


def solution(mesh):
    return jax.shard_map(
        chebyshev_step,
        mesh=mesh,
        in_specs=(
            P("sa", "gy", "gx"),
            P("sa", "gy", "gx"),
            P("sa", "gy", "gx"),
            P(None, ("gy", "sa"), "gx"),
            P(),
            P(),
            P(),
            P(),
        ),
        out_specs=(P("sa", "gy", "gx"), P("sa", "gy", "gx")),
        check_vma=False,
    )
```

```python
import functools
import math

import jax
import jax.numpy as jnp
import numpy as np
from jax import lax
from jax.experimental import pallas as pl
from jax.experimental.pallas import tpu as pltpu
from jax.sharding import PartitionSpec as P


HIGHEST = lax.Precision.HIGHEST
hermite_points = (
    0.0,
    -1.7320508075688772,
    1.7320508075688772,
    -1.355626179974266,
    1.355626179974266,
    -2.8569700138728056,
    2.8569700138728056,
)
storage_rate = 0.0004
relax_weight = 1.6
step_length = 0.3


LANES = 128
NODE_BLOCK = 512
LOG_DEPTH = 16
EARLY = 4
BF16 = jnp.bfloat16


def round_up(value, step):
    return -(-value // step) * step


def product(left, right):
    return jnp.dot(left, right, preferred_element_type=jnp.float32)


def split_two(block):
    high = block.astype(BF16)
    return (high, (block - high.astype(jnp.float32)).astype(BF16))


def split_three(block):
    high = block.astype(BF16)
    rest = block - high.astype(jnp.float32)
    middle = rest.astype(BF16)
    return (high, middle, (rest - middle.astype(jnp.float32)).astype(BF16))


def exact(left, right):
    return jnp.dot(left, right, precision=HIGHEST, preferred_element_type=jnp.float32)


def row_transform(block, pair_ref, rest_ref):
    high, middle, low = split_three(block)
    both = product(jnp.concatenate([high, middle], axis=1), pair_ref[...])
    both = both[:, :LANES] + both[:, LANES:]
    return both + product(jnp.concatenate([low, high], axis=1), rest_ref[...])


def col_transform(block, all_ref):
    high, middle, low = split_three(block)
    stack = jnp.concatenate([high, middle, high, middle, low, high], axis=0)
    return product(all_ref[...], stack)


def make_tables(sizes, per, mean, lane_ref, column_ref, far_ref, inverse, by_row, by_col, col_table, row_table):
    count_x, count_y = sizes
    half = LANES // 2
    column = lambda k, rows=LANES: jnp.broadcast_to(column_ref[:rows, k : k + 1], (rows, LANES))
    lanes = lambda k: lane_ref[k : k + 1, :]
    upright = 1.0 / (storage_rate + mean * (column(0) + lanes(5)))
    flat = 1.0 / (storage_rate + mean * (column(3) + lanes(2)))
    inverse[:, :LANES] = flat[:half]
    inverse[:, LANES:] = flat[:half]
    lane = lax.broadcasted_iota(jnp.int32, (LANES, LANES), 1)
    row = lax.broadcasted_iota(jnp.int32, (LANES, LANES), 0)
    for end in range(2):
        part = upright * column(1 + end)
        by_col[:LANES, end * LANES : (end + 1) * LANES] = jnp.where(lane < half, part, 0.0)
        by_col[LANES:, end * LANES : (end + 1) * LANES] = jnp.where(lane < half, 0.0, part)
        part = flat * column(4 + end)
        by_row[:, 2 * end * LANES : (2 * end + 1) * LANES] = jnp.where(row < half, part, 0.0)
        by_row[:, (2 * end + 1) * LANES : (2 * end + 2) * LANES] = jnp.where(row < half, 0.0, part)

    def tables(count, same, cross):
        shrink = [
            1.0 / (1.0 / mean + 2.0 * same - 2.0 * math.cos(n * math.pi / count) * cross)
            for n in range(1, count)
        ]
        sine = lambda a, b: math.sin(a * b % (2 * count) * math.pi / count)
        return [
            [
                sum((2.0 / count) * sine(n, a) * sine(n, b) * shrink[n - 1] for n in range(1, count))
                for b in range(1, count)
            ]
            for a in range(1, count)
        ]

    total = lambda a: jnp.sum(a, axis=0, keepdims=True)
    ends = column(1), column(2)
    found = tables(
        count_x, total(upright * ends[0] * ends[0]), total(upright * ends[0] * ends[1])
    )
    for a in range(count_x - 1):
        for b in range(count_x - 1):
            col_table[a, b : b + 1, :] = found[a][b]
    far = far_ref[0:1, :]
    wide = lambda k: jnp.broadcast_to(column_ref[:half, k : k + 1], (half, far.shape[1]))
    deep = 1.0 / (storage_rate + mean * (wide(3) + far))
    found = tables(
        count_y, total(deep * wide(4) * wide(4)), total(deep * wide(4) * wide(5))
    )
    depth = row_table.shape[1]
    where_row = lax.broadcasted_iota(jnp.int32, (depth, far.shape[1]), 0) // per
    for shift in range(-(count_y - 2), count_y - 1):
        table = jnp.zeros((depth, far.shape[1]), jnp.float32)
        for a in range(count_y - 1):
            if 0 <= a + shift < count_y - 1:
                table = jnp.where(where_row == a, found[a][a + shift], table)
        row_table[shift + count_y - 2] = table


def solve_fluxes(sizes, per, got, back, lane_ref, join_ref, by_row, by_col, col_table, row_table):
    count_x, count_y = sizes
    depth = row_table.shape[1]
    rows = count_y * per
    lanes = lambda k: lane_ref[k : k + 1, :]
    take = lambda block, kind: got[pl.ds(block * rows * 8 + kind, depth, stride=8), :]
    row = lax.broadcasted_iota(jnp.int32, (depth, LANES), 0)
    up = lambda a, by=1: pltpu.roll(a, (-by * per) % depth, 0)
    down = lambda a: jnp.where(row < per, 0.0, pltpu.roll(a, per, 0))
    blocks, cuts = range(count_x), range(1, count_x)

    def through_cols(first, last):
        jump = [first[cut] - last[cut - 1] for cut in cuts]
        return [
            sum(col_table[a, b : b + 1, :] * jump[b] for b in range(count_x - 1))
            for a in range(count_x - 1)
        ]

    fluxes = through_cols([take(b, 0) for b in blocks], [take(b, 1) for b in blocks])
    spread = [exact(flux, by_row[...]) for flux in fluxes]

    def at_row(block, end, half):
        part = slice((2 * end + half) * LANES, (2 * end + half + 1) * LANES)
        value = take(block, 2 + 2 * end + half)
        if block < count_x - 1:
            value = value + spread[block][:, part] * lanes(1)
        if block > 0:
            value = value - spread[block - 1][:, part] * lanes(0)
        return value

    jump = jnp.concatenate(
        [
            jnp.concatenate([up(at_row(b, 0, half)) - at_row(b, 1, half) for b in blocks], axis=1)
            for half in range(2)
        ],
        axis=0,
    )
    far = lax.dot_general(
        jump, join_ref[...], (((1,), (1,)), ((), ())), precision=HIGHEST,
        preferred_element_type=jnp.float32,
    )
    mixed = []
    for half in range(2):
        part = far[half * depth : (half + 1) * depth]
        mixed.append(sum(
            row_table[shift + count_y - 2] * (up(part, shift) if shift else part)
            for shift in range(-(count_y - 2), count_y - 1)
        ))
    near = exact(jnp.concatenate(mixed, axis=0), join_ref[...])
    through_rows = [
        [near[half * depth : (half + 1) * depth, b * LANES : (b + 1) * LANES] for half in range(2)]
        for b in blocks
    ]
    ends = []
    for b in blocks:
        reach = exact(jnp.concatenate(through_rows[b], axis=1), by_col[...])
        ends.append([
            lanes(4) * reach[:, end * LANES : (end + 1) * LANES]
            - lanes(3) * down(reach[:, end * LANES : (end + 1) * LANES])
            for end in range(2)
        ])
    more = through_cols([end[0] for end in ends], [end[1] for end in ends])
    fluxes = [a + b for a, b in zip(fluxes, more)]
    nothing = jnp.zeros((depth, LANES), jnp.float32)
    for b in blocks:
        left = fluxes[b - 1] if b > 0 else nothing
        right = fluxes[b] if b < count_x - 1 else nothing
        top = [down(part) for part in through_rows[b]]
        for kind, value in enumerate([left, right] + top + through_rows[b]):
            back[pl.ds(b * rows * 8 + kind, depth, stride=8), :] = value


def stacked(parts, depth):
    missing = depth - sum(part.shape[0] for part in parts)
    if missing:
        parts = parts + [jnp.zeros((missing,) + parts[0].shape[1:], parts[0].dtype)]
    return jnp.concatenate(parts, axis=0)


def node_kernel(
    sizes, field_ref, log_ref, node_ref, mode_ref, weight_ref,
    source_ref, mean_ref, pair_ref, rest_ref, all_ref, lane_ref, column_ref, far_ref, join_ref,
    spec_ref, flux_ref,
    lines, log_lines, log_sides, sides, total, line_op, log_op, basis_op, germ_op, weight_op,
    edge, value_prev, half_prev, flux_prev,
    home, spectrum, origin, traces, got, back, tall, join,
    inverse, by_row, by_col, col_table, row_table,
    block_field, field_cols, log_cols, picks, shares_of, degrees,
    load_sem, spec_sem, trace_send, trace_recv, flux_send, flux_recv,
    line_send, line_recv, halo_send, side_send, side_recv, log_send, log_recv, out_send, out_recv,
):
    count_x, count_y, shares, group = sizes
    modes, rows, width = field_ref.shape
    own_rows = rows // shares
    every = shares * modes
    below, above = own_rows, own_rows + 1
    blocks = basis_op.shape[0] // NODE_BLOCK
    x, y, share = (lax.axis_index(axis) for axis in ("gx", "gy", "sa"))
    first_y = jnp.logical_and(y == 0, share == 0)
    last_y = jnp.logical_and(y == count_y - 1, share == shares - 1)
    not_first, not_last = jnp.logical_not(first_y), jnp.logical_not(last_y)
    peer = lambda step: lax.rem(share + step, shares)

    def remote(source, target, send, recv, **place):
        return pltpu.make_async_remote_copy(
            src_ref=source, dst_ref=target, send_sem=send, recv_sem=recv,
            device_id=place, device_id_type=pl.DeviceIdType.MESH,
        )

    def arrived(target, recv):
        pltpu.make_async_copy(target, target, recv).wait()

    load_field = pltpu.make_async_copy(field_ref, block_field, load_sem.at[2])
    load_field.start()
    load_origin = pltpu.make_async_copy(source_ref, origin, load_sem.at[0])
    load_origin.start()
    load_join = pltpu.make_async_copy(join_ref, join, load_sem.at[1])
    load_join.start()

    barrier = pltpu.get_barrier_semaphore()
    greet = lambda **place: pl.semaphore_signal(
        barrier, inc=1, device_id=place, device_id_type=pl.DeviceIdType.MESH
    )
    for step in range(1, shares):
        greet(sa=peer(step))
    owners = count_x * count_y
    me = x * count_y + y
    other = lambda step: lax.rem(me + step, owners)
    at_owner = lambda owner: dict(gx=lax.div(owner, count_y), gy=lax.rem(owner, count_y))
    for step in range(1, owners):
        greet(**at_owner(other(step)))
    conditions = (
        (x > 0, dict(gx=x - 1)), (x < count_x - 1, dict(gx=x + 1)),
        (y > 0, dict(gy=y - 1)), (y < count_y - 1, dict(gy=y + 1)),
    )
    for condition, place in conditions:
        @pl.when(condition)
        def _():
            for step in range(1, shares):
                greet(sa=peer(step), **place)
    sides_met = sum(condition.astype(jnp.int32) for condition, _ in conditions)
    pl.semaphore_wait(barrier, owners - 1 + (shares - 1) * (1 + sides_met))

    remote_copies = []

    def start(condition, copy):
        remote_copies.append((condition, copy))
        if condition is None:
            copy.start()
        else:
            pl.when(condition)(copy.start)

    row_of = lambda row: field_ref.at[:, row, :]
    flat_next = jnp.where(share == shares - 1, y + 1, y), lax.rem(share + 1, shares)
    flat_last = jnp.where(share == 0, y - 1, y), lax.rem(share + shares - 1, shares)
    start(y > 0, remote(
        row_of(0), lines.at[below, share], halo_send.at[0], line_recv.at[below, share],
        gy=y - 1, sa=jnp.int32(shares - 1),
    ))
    start(y < count_y - 1, remote(
        row_of(rows - 1), lines.at[above, share], halo_send.at[1], line_recv.at[above, share],
        gy=y + 1, sa=jnp.int32(0),
    ))
    for step in range(1, shares):
        to = peer(step)
        start(to > 0, remote(
            row_of(jnp.maximum(to * own_rows - 1, 0)), lines.at[above, share],
            halo_send.at[2 * step], line_recv.at[above, share], sa=to,
        ))
        start(to < shares - 1, remote(
            row_of(jnp.minimum((to + 1) * own_rows, rows - 1)), lines.at[below, share],
            halo_send.at[2 * step + 1], line_recv.at[below, share], sa=to,
        ))
    own_above = pltpu.make_async_copy(
        row_of(jnp.maximum(share * own_rows - 1, 0)), lines.at[above, share],
        line_recv.at[above, share],
    )
    own_below = pltpu.make_async_copy(
        row_of(jnp.minimum((share + 1) * own_rows, rows - 1)), lines.at[below, share],
        line_recv.at[below, share],
    )
    pl.when(share > 0)(own_above.start)
    pl.when(share < shares - 1)(own_below.start)
    def line_copy(row, step):
        to = peer(step)
        return remote(
            row_of(to * own_rows + row), lines.at[row, share], line_send.at[row, step],
            line_recv.at[row, share], sa=to,
        )

    def send_lines(row, carry):
        for step in range(1, shares):
            line_copy(row, step).start()
        pltpu.make_async_copy(
            row_of(share * own_rows + row), lines.at[row, share], line_recv.at[row, share]
        ).start()
        return carry

    early = min(EARLY, own_rows)
    lax.fori_loop(0, early, send_lines, 0)
    pairs = modes // 2
    unroll = max(n for n in range(1, 11) if pairs % n == 0)
    pick_row = lax.broadcasted_iota(jnp.int32, (16, 2 * LANES), 0)
    pick_lane = lax.broadcasted_iota(jnp.int32, (16, 2 * LANES), 1) % LANES
    first_pick = jnp.logical_and(pick_row == 0, pick_lane == 0)
    last_pick = jnp.logical_and(pick_row == 1, pick_lane == LANES - 1)
    pick = jnp.where(jnp.logical_or(first_pick, last_pick), 1.0, 0.0).astype(BF16)

    def columns_of(block):
        return lax.dot_general(
            pick, jnp.concatenate(split_two(block), axis=1), (((1,), (1,)), ((), ())),
            preferred_element_type=jnp.float32,
        )

    log_cols[...] = jnp.zeros_like(log_cols)
    for level in range(log_ref.shape[0]):
        found = columns_of(log_ref[level])
        for end in range(2):
            log_cols[end, level : level + 1, :own_rows] = found[end : end + 1, :]
    load_field.wait()

    def take_columns(index, carry):
        for pair in range(unroll):
            mode = 2 * (index * unroll + pair)
            found = columns_of(block_field[pl.ds(mode, 2)].reshape(2 * rows, LANES))
            for half in range(2):
                part = pltpu.roll(found, LANES - rows, 1) if half else found
                for end in range(2):
                    field_cols[end, pl.ds(mode + half, 1), :] = part[end : end + 1, :]
        return carry

    lax.fori_loop(0, pairs // unroll, take_columns, 0)
    log_copies = (
        (not_last, log_ref.at[:, own_rows - 1, :], log_lines.at[1], 0,
         dict(gy=flat_next[0], sa=flat_next[1])),
        (not_first, log_ref.at[:, 0, :], log_lines.at[0], 1,
         dict(gy=flat_last[0], sa=flat_last[1])),
        (x < count_x - 1, log_cols.at[1], log_sides.at[0], 2, dict(gx=x + 1)),
        (x > 0, log_cols.at[0], log_sides.at[1], 3, dict(gx=x - 1)),
    )
    for condition, source, target, slot, place in log_copies:
        start(condition, remote(source, target, log_send.at[slot], log_recv.at[slot], **place))
    for step in range(shares):
        to = peer(step)
        for kind in range(2):
            source = field_cols.at[kind]
            if step:
                start(None, remote(
                    source, sides.at[kind, share], side_send.at[step, kind],
                    side_recv.at[kind, share], sa=to,
                ))
            else:
                pltpu.make_async_copy(
                    source, sides.at[kind, share], side_recv.at[kind, share]
                ).start()
        start(x > 0, remote(
            field_cols.at[0], sides.at[2, share], side_send.at[step, 2],
            side_recv.at[2, share], gx=x - 1, sa=to,
        ))
        start(x < count_x - 1, remote(
            field_cols.at[1], sides.at[3, share], side_send.at[step, 3],
            side_recv.at[3, share], gx=x + 1, sa=to,
        ))

    lax.fori_loop(early, own_rows, send_lines, 0)
    per = traces.shape[0] // 8 // owners
    plane = (count_x, count_y)
    beyond = got.shape[0] - traces.shape[0]
    if beyond:
        got[traces.shape[0] :, :] = jnp.zeros((beyond, LANES), jnp.float32)
    traces[...] = jnp.zeros_like(traces)
    make_tables(
        plane, per, mean_ref[0], lane_ref, column_ref, far_ref,
        inverse, by_row, by_col, col_table, row_table,
    )

    weight_op[...] = jnp.zeros_like(weight_op)
    total[...] = jnp.zeros_like(total)

    nodes_given = node_ref.shape[1]
    picks[...] = jnp.zeros_like(picks)
    picks[:, :nodes_given] = node_ref[...]
    shares_of[...] = jnp.zeros_like(shares_of)
    shares_of[:, :nodes_given] = weight_ref[...]
    degrees[...] = jnp.zeros_like(degrees)
    for start_at in range(0, every, LANES):
        width_at = min(LANES, every - start_at)
        degrees[start_at : start_at + mode_ref.shape[0], :width_at] = mode_ref[
            :, start_at : start_at + width_at
        ].astype(jnp.float32)
        here = slice(start_at, start_at + LANES)
        degrees[here, :] = jnp.transpose(degrees[here, :])

    def make_basis(block, carry):
        lanes = pl.ds(pl.multiple_of(block * LANES, LANES), LANES)
        picked = picks[:, lanes]
        germs = jnp.zeros(picked.shape, jnp.float32)
        for level, point in enumerate(hermite_points):
            germs = jnp.where(picked == level, point, germs)
        square = germs * germs
        second = (square - 1.0) / math.sqrt(2.0)
        third = (square * germs - 3.0 * germs) / math.sqrt(6.0)
        values = jnp.ones((every, LANES), jnp.float32)
        for germ in range(germs.shape[0]):
            degree = jnp.broadcast_to(degrees[:every, germ : germ + 1], (every, LANES))
            at = lambda table: jnp.broadcast_to(table[germ : germ + 1, :], (every, LANES))
            values = values * jnp.where(
                degree == 0, 1.0,
                jnp.where(degree == 1, at(germs), jnp.where(degree == 2, at(second), at(third))),
            )
        high, low = split_two(values)
        wide = lambda a: a.astype(jnp.float32)
        stack = stacked([wide(high), wide(high), wide(low)], basis_op.shape[1])
        basis_op[lanes, :] = jnp.transpose(stack).astype(BF16)
        high, low = split_two(values * (2.0 * shares_of[:, lanes]))
        weight_op[:every, lanes] = high
        weight_op[every:, lanes] = low
        spread = stacked([-jnp.ones((1, LANES), jnp.float32), -germs], LOG_DEPTH)
        high, low = split_two(spread)
        stack = stacked([wide(high), wide(high), wide(low)], LANES)
        germ_op[lanes, :] = jnp.transpose(stack).astype(BF16)
        return carry

    lax.fori_loop(0, basis_op.shape[0] // LANES, make_basis, 0)

    def log_stack(block):
        high, low = split_two(stacked([block], LOG_DEPTH))
        return stacked([high, low, high], LANES)

    def field_stack(block):
        high, low = split_two(block)
        return stacked([high, low, high], line_op.shape[1])

    for condition, _, target, slot, _ in (
        (not_first, None, log_lines.at[1], 0, None), (not_last, None, log_lines.at[0], 1, None),
        (x > 0, None, log_sides.at[0], 2, None), (x < count_x - 1, None, log_sides.at[1], 3, None),
    ):
        @pl.when(condition)
        def _():
            arrived(target, log_recv.at[slot])

    def make_log(row, carry):
        log_op[row] = log_stack(log_ref[:, row, :])
        return carry

    lax.fori_loop(0, own_rows, make_log, 0)
    log_op[below] = log_stack(
        jnp.where(last_y, log_ref[:, own_rows - 1, :], log_lines[0])
    )
    log_op[above] = log_stack(jnp.where(first_y, log_ref[:, 0, :], log_lines[1]))

    def at_nodes(nodes, field, logs):
        return (product(basis_op[nodes, :], field), jnp.exp(product(germ_op[nodes, :], logs)))

    def flux(later, earlier, half_later, half_earlier):
        return (later - earlier) * pl.reciprocal(half_later + half_earlier)

    def project(nodes, applied):
        high = applied.astype(BF16)
        rest = applied - high.astype(jnp.float32)
        middle = rest.astype(BF16)
        low = (rest - middle.astype(jnp.float32)).astype(BF16)
        both = product(weight_op[:, nodes], high) + product(weight_op[:, nodes], middle)
        return both[:every] + both[every:] + product(weight_op[:every, nodes], low)

    node_slice = lambda block: pl.ds(pl.multiple_of(block * NODE_BLOCK, NODE_BLOCK), NODE_BLOCK)

    for kind in range(4):
        condition = (None, None, x < count_x - 1, x > 0)[kind]
        for source in range(shares):
            wait = lambda: arrived(sides.at[kind, source], side_recv.at[kind, source])
            wait() if condition is None else pl.when(condition)(wait)
    flat = lambda ref: ref.reshape(every, LANES)
    turn = lax.rem(LANES - share * own_rows, LANES)
    side = [pltpu.roll(flat(sides[kind]), turn, 1) for kind in range(4)]
    log_first, log_last = log_cols[0], log_cols[1]
    before = jnp.where(x == 0, side[0], side[3])
    after = jnp.where(x == count_x - 1, side[1], side[2])
    log_before = jnp.where(x == 0, log_first, log_sides[0])
    log_after = jnp.where(x == count_x - 1, log_last, log_sides[1])

    def beside(low_part, high_part):
        lane = lax.broadcasted_iota(jnp.int32, low_part.shape, 1)
        return jnp.where(lane < own_rows, low_part, pltpu.roll(high_part, own_rows, 1))

    line_op[0, :, :LANES] = field_stack(beside(before, side[1]))
    line_op[0, :, LANES:] = field_stack(beside(side[0], after))
    log_edge = jnp.concatenate(
        [log_stack(beside(log_before, log_last)), log_stack(beside(log_first, log_after))], axis=1
    )
    edge[...] = jnp.zeros_like(edge)

    def make_edge(block, carry):
        nodes = node_slice(block)
        values, halves = at_nodes(nodes, line_op[0], log_edge)
        edge[...] += project(nodes, flux(
            values[:, LANES:], values[:, :LANES], halves[:, LANES:], halves[:, :LANES]
        ))
        return carry

    lax.fori_loop(0, blocks, make_edge, 0)

    def wait_line(row):
        for source in range(shares):
            arrived(lines.at[row, source], line_recv.at[row, source])

    wait_line(0)
    pl.when(not_first)(lambda: wait_line(above))
    line = flat(lines[0])
    line_op[0, :, :LANES] = field_stack(jnp.where(first_y, line, flat(lines[above])))
    line_op[0, :, LANES:] = field_stack(line)

    def begin(block, carry):
        nodes = node_slice(block)
        logs = jnp.concatenate([log_op[above], log_op[0]], axis=1)
        values, halves = at_nodes(nodes, line_op[0], logs)
        value_prev[nodes, :] = values[:, LANES:]
        half_prev[nodes, :] = halves[:, LANES:]
        flux_prev[nodes, :] = flux(
            values[:, LANES:], values[:, :LANES], halves[:, LANES:], halves[:, :LANES]
        )
        return carry

    lax.fori_loop(0, blocks, begin, 0)

    home_row = lambda row: home.at[pl.ds(row * modes, modes), :]

    def out_copy(row, step):
        to = peer(step)
        return remote(
            total.at[row, to], home_row(share * own_rows + row), out_send.at[row, step],
            out_recv.at[row, share], sa=to,
        )

    def own_copy(row):
        return pltpu.make_async_copy(
            total.at[row, share], home_row(share * own_rows + row), out_recv.at[row, share]
        )

    def take_origin(index, carry):
        for pair in range(unroll):
            one_origin(index * unroll + pair)
        return carry

    def one_origin(pair):
        block = origin[pl.ds(2 * pair, 2)].reshape(2 * rows, LANES)
        block = row_transform(block, pair_ref, rest_ref)
        spectrum[pair] = col_transform(
            jnp.concatenate([block[:rows], block[rows:]], axis=1), all_ref
        )

    groups = own_rows // group

    def take_group(index, carry):
        base = index * group
        for ahead in range(1, group + 1):
            row = base + ahead
            if ahead < group:
                wait_line(row)
            else:
                pl.when(jnp.logical_or(row < own_rows, not_last))(lambda: wait_line(row))
            line = flat(lines[row])
            if ahead == group:
                line = jnp.where(
                    jnp.logical_and(row == own_rows, last_y), flat(lines[row - 1]), line
                )
            place = pl.ds((ahead - 1) % 2 * LANES, LANES)
            line_op[(ahead - 1) // 2, :, place] = field_stack(line)

        def take_nodes(block, carry):
            nodes = node_slice(block)
            value, half, flux_up = value_prev[nodes, :], half_prev[nodes, :], flux_prev[nodes, :]
            inside = lax.broadcasted_iota(jnp.int32, value.shape, 1) < LANES - 1
            for pair in range(group // 2):
                row = base + 2 * pair
                logs = jnp.concatenate([log_op[row + 1], log_op[row + 2]], axis=1)
                values, halves = at_nodes(nodes, line_op[pair], logs)
                applied = []
                for here in range(2):
                    value_next = values[:, here * LANES : (here + 1) * LANES]
                    half_next = halves[:, here * LANES : (here + 1) * LANES]
                    flux_down = flux(value_next, value, half_next, half)
                    across = jnp.where(
                        inside,
                        flux(
                            pltpu.roll(value, LANES - 1, 1), value,
                            pltpu.roll(half, LANES - 1, 1), half,
                        ),
                        0.0,
                    )
                    applied.append(
                        (0.5 * storage_rate) * value
                        - (across - pltpu.roll(across, 1, 1)) - (flux_down - flux_up)
                    )
                    value, half, flux_up = value_next, half_next, flux_down
                sums = project(nodes, jnp.concatenate(applied, axis=1))
                parts = sums.reshape(shares, modes, 2 * LANES)
                total[row] += parts[:, :, :LANES]
                total[row + 1] += parts[:, :, LANES:]
            value_prev[nodes, :] = value
            half_prev[nodes, :] = half
            flux_prev[nodes, :] = flux_up
            return carry

        lax.fori_loop(0, blocks, take_nodes, 0, unroll=True)
        lane = lax.broadcasted_iota(jnp.int32, (every, LANES), 1)
        for step in range(group):
            row = base + step
            left = pltpu.roll(edge[...], lax.rem(LANES - row, LANES), 1)
            right = pltpu.roll(edge[...], LANES - 1 - own_rows - row, 1)
            change = jnp.where(lane == 0, left, 0.0) - jnp.where(lane == LANES - 1, right, 0.0)
            line = row_transform(flat(total[row]) + change, pair_ref, rest_ref)
            total[row] = line.reshape(shares, modes, LANES)
        for step in range(group):
            row = base + step
            for to in range(1, shares):
                out_copy(row, to).start()
            own_copy(row).start()
        return carry

    lax.fori_loop(0, groups, take_group, 0)
    load_origin.wait()
    lax.fori_loop(0, pairs // unroll, take_origin, 0)

    def arrive(row, carry):
        for step in range(1, shares):
            source = peer(step)
            arrived(home_row(source * own_rows + row), out_recv.at[row, source])
        own_copy(row).wait()
        return carry

    lax.fori_loop(0, own_rows, arrive, 0)

    def take_pair(pair, columns):
        line = [home[pl.ds(2 * pair + half, rows, stride=modes), :] for half in range(2)]
        line = col_transform(jnp.concatenate(line, axis=1), all_ref)
        line = spectrum[pair] - line
        spectrum[pair] = line
        alone = line * inverse[...]
        trace = pl.ds(8 * pair, 8)
        lane = lax.broadcasted_iota(jnp.int32, (LANES, LANES), 1)
        result = []
        for end in range(2):
            ends = jnp.broadcast_to(column_ref[:rows, 4 + end : 5 + end], (rows, 2 * LANES))
            result.append(jnp.sum(alone * ends, axis=0, keepdims=True))
            upright = jnp.concatenate([alone[:, :LANES], alone[:, LANES:]], axis=0)
            upright = jnp.sum(upright * lane_ref[end : end + 1, :], axis=1, keepdims=True)
            columns = jnp.where(lane == end * (LANES // 2) + pair, upright, columns)
        blank = jnp.zeros((2, LANES), jnp.float32)
        traces[trace, :] = jnp.concatenate(
            [blank, result[0][:, :LANES], result[0][:, LANES:],
             result[1][:, :LANES], result[1][:, LANES:], blank], axis=0
        )
        return columns

    def take_pairs(index, columns):
        for pair in range(unroll):
            columns = take_pair(index * unroll + pair, columns)
        return columns

    columns = lax.fori_loop(
        0, pairs // unroll, take_pairs, jnp.zeros((LANES, LANES), jnp.float32)
    )
    tall[...] = jnp.transpose(columns)
    for end in range(2):
        traces[pl.ds(end, pairs, stride=8), :] = tall[pl.ds(end * (LANES // 2), pairs), :]
    save = pltpu.make_async_copy(spectrum, spec_ref, spec_sem)
    save.start()

    piece = lambda owner: pl.ds(owner * per * 8, per * 8)

    def trace_copy(step):
        to = other(step)
        return remote(
            traces.at[piece(to), :], got.at[piece(me), :], trace_send.at[step],
            trace_recv.at[me], **at_owner(to),
        )

    def flux_copy(step):
        to = other(step)
        return remote(
            back.at[piece(to), :], flux_ref.at[piece(me), :], flux_send.at[step],
            flux_recv.at[me], **at_owner(to),
        )

    used = lambda owner: owner * per < pairs
    for step in range(1, owners):
        pl.when(used(other(step)))(trace_copy(step).start)
    got[piece(me), :] = traces[piece(me), :]
    load_join.wait()
    for step in range(1, owners):
        @pl.when(used(me))
        def _():
            arrived(got.at[piece(other(step)), :], trace_recv.at[other(step)])
    solve_fluxes(plane, per, got, back, lane_ref, join, by_row, by_col, col_table, row_table)
    for step in range(1, owners):
        pl.when(used(me))(flux_copy(step).start)
    own_flux = pltpu.make_async_copy(
        back.at[piece(me), :], flux_ref.at[piece(me), :], flux_recv.at[me]
    )
    own_flux.start()

    def sent(row, carry):
        for step in range(1, shares):
            line_copy(row, step).wait_send()
            out_copy(row, step).wait_send()
        return carry

    lax.fori_loop(0, own_rows, sent, 0)
    for condition, copy in remote_copies:
        if condition is None:
            copy.wait_send()
        else:
            pl.when(condition)(copy.wait_send)
    save.wait()
    own_flux.wait()
    for step in range(1, owners):
        pl.when(used(other(step)))(trace_copy(step).wait_send)
        pl.when(used(me))(flux_copy(step).wait_send)

        @pl.when(used(other(step)))
        def _():
            arrived(flux_ref.at[piece(other(step)), :], flux_recv.at[other(step)])


def finish_kernel(
    spec_ref, flux_ref, now_ref, before_ref, mean_ref, lane_ref, column_ref, rows_ref, cols_ref,
    fresh_ref, update_ref, inverse,
):
    rows = spec_ref.shape[1]
    column = lambda k: jnp.broadcast_to(column_ref[:rows, k : k + 1], (rows, LANES))

    @pl.when(pl.program_id(0) == 0)
    def start():
        inverse[...] = 1.0 / (storage_rate + mean_ref[0] * (column(3) + lane_ref[2:3, :]))

    upright = jnp.transpose(flux_ref[...])
    for pair in range(spec_ref.shape[0]):
        parts = []
        for half in range(2):
            beside = lambda kind: jnp.broadcast_to(
                upright[half * rows : (half + 1) * rows, 8 * pair + kind : 8 * pair + kind + 1],
                (rows, LANES),
            )
            over = lambda kind: flux_ref[8 * pair + kind : 8 * pair + kind + 1, :]
            part = spec_ref[pair, :, half * LANES : (half + 1) * LANES]
            part = part + (beside(1) * lane_ref[1:2, :] - beside(0) * lane_ref[0:1, :])
            part = part + (column(5) * over(4 + half) - column(4) * over(2 + half))
            parts.append(part * inverse[...])
        high, low = split_two(jnp.concatenate(parts, axis=1))
        part = product(rows_ref[...], jnp.concatenate([high, low, high], axis=0))
        high, low = split_two(jnp.concatenate([part[:, :LANES], part[:, LANES:]], axis=0))
        part = product(jnp.concatenate([high, low], axis=1), cols_ref[...])
        part = (part[:, :LANES] + part[:, LANES:]).reshape(2, rows, LANES)
        mode = slice(2 * pair, 2 * pair + 2)
        update_ref[mode] = part
        before = before_ref[mode]
        fresh_ref[mode] = before + relax_weight * (now_ref[mode] - before + step_length * part)


def cosine_table(length):
    freq, cells = np.arange(length)[:, None], np.arange(length)[None, :]
    factor = np.where(freq == 0, math.sqrt(1.0 / length), math.sqrt(2.0 / length))
    return factor * np.cos((freq * (2 * cells + 1) % (4 * length)) * (math.pi / (2 * length)))


def pieces(table):
    found, rest = [], table.astype(np.float32)
    for _ in range(3):
        found.append(rest.astype(BF16))
        rest = rest - found[-1].astype(np.float32)
    return found


def constant_tables(count_x, rows, width):
    eigen = lambda count: 2.0 - 2.0 * np.cos(np.arange(count) * (math.pi / count))
    row_table, col_table = cosine_table(rows), cosine_table(width)
    far_table = cosine_table(count_x * width)
    join = np.einsum("kix,lx->kil", far_table.reshape(-1, count_x, width), col_table)
    twice = lambda a: np.concatenate([a, a])
    lanes = [
        col_table[:, 0], col_table[:, -1], eigen(width),
        twice(row_table[:, 0]), twice(row_table[:, -1]), twice(eigen(rows)),
    ]
    columns = [lanes[2], lanes[0], lanes[1], lanes[5], lanes[3], lanes[4]]
    grow = lambda a: np.pad(np.stack(a), ((0, 8 - len(a)), (0, 0))).astype(np.float32)
    high, middle, low = pieces(col_table.T)
    front = pieces(col_table)
    pair = np.block([[high, middle], [high, middle]])
    rest = np.concatenate([high, low])
    back = np.block([[front[0], front[1]], [front[0], np.zeros_like(high)]])
    high, middle, low = pieces(row_table)
    every = np.concatenate([high, high, middle, middle, high, low], axis=1)
    high, low, _ = pieces(row_table.T)
    rows_back = np.concatenate([high, high, low], axis=1)
    return dict(
        pair=pair, rest=rest, every=every, lanes=grow(lanes), columns=grow(columns).T.copy(),
        far=grow([eigen(count_x * width)]), join=join.reshape(len(far_table), -1).astype(np.float32),
        rows=rows_back, cols=back,
    )


def chebyshev_step(
    field, field_before, source, log_fields, weights, mean_perm, node_index, mode_index
):
    modes, rows, width = field.shape
    count_x, count_y, shares = (lax.axis_size(axis) for axis in ("gx", "gy", "sa"))
    padded = round_up(modes, 16)
    grow = lambda a, size, dim: jnp.pad(
        a, [(0, size - a.shape[d] if d == dim else 0) for d in range(a.ndim)]
    )
    field, field_before, source = (grow(a, padded, 0) for a in (field, field_before, source))
    mean = mean_perm.reshape(1)
    tables = constant_tables(count_x, rows, width)
    pairs, owners = padded // 2, count_x * count_y
    per = -(-pairs // owners)
    depth_solve = round_up(count_y * per, 8)
    extra = 8 * (depth_solve - count_y * per)
    own_rows = rows // shares
    nodes = node_index.shape[0]
    all_nodes = round_up(nodes, NODE_BLOCK)
    modes_of = grow(mode_index.reshape(shares, modes, -1), padded, 1).reshape(shares * padded, -1)
    levels = log_fields.shape[0]
    group = math.gcd(own_rows, 8)
    every = shares * padded
    depth = round_up(3 * every, LANES)
    slots = own_rows + 2
    vmem = lambda shape, kind=jnp.float32: pltpu.VMEM(shape, kind)
    dma = lambda *shape: pltpu.SemaphoreType.DMA(shape)
    place = pl.BlockSpec(memory_space=pl.ANY)
    whole = pl.BlockSpec(memory_space=pltpu.VMEM)
    numbers = pl.BlockSpec(memory_space=pltpu.SMEM)
    spectrum, fluxes = pl.pallas_call(
        functools.partial(node_kernel, (count_x, count_y, shares, group)),
        in_specs=[place, whole, whole, whole, whole]
        + [place, numbers] + [whole] * 6 + [place],
        out_specs=[place, place],
        out_shape=[
            jax.ShapeDtypeStruct((pairs, rows, 2 * width), jnp.float32),
            jax.ShapeDtypeStruct((owners * per * 8, LANES), jnp.float32),
        ],
        scratch_shapes=[
            vmem((slots, shares, padded, LANES)),
            vmem((2, levels, LANES)),
            vmem((2, levels, LANES)),
            vmem((4, shares, padded, LANES)),
            vmem((own_rows, shares, padded, LANES)),
            vmem((group // 2, depth, 2 * LANES), BF16),
            vmem((slots, LANES, LANES), BF16),
            vmem((all_nodes, depth), BF16),
            vmem((all_nodes, LANES), BF16),
            vmem((2 * every, all_nodes), BF16),
            vmem((every, LANES)),
            vmem((all_nodes, LANES)),
            vmem((all_nodes, LANES)),
            vmem((all_nodes, LANES)),
            vmem((rows * padded, LANES)),
            vmem((pairs, rows, 2 * LANES)),
            vmem((padded, rows, LANES)),
            vmem((owners * per * 8, LANES)),
            vmem((owners * per * 8 + extra, LANES)),
            vmem((owners * per * 8 + extra, LANES)),
            vmem((LANES, LANES)),
            vmem(tables["join"].shape),
            vmem((rows, 2 * LANES)),
            vmem((LANES, 4 * LANES)),
            vmem((2 * LANES, 2 * LANES)),
            vmem((count_x - 1, round_up(count_x - 1, 8), LANES)),
            vmem((2 * count_y - 3, depth_solve, count_x * width)),
            vmem((padded, rows, LANES)),
            vmem((2, padded, LANES)),
            vmem((2, levels, LANES)),
            vmem((node_index.shape[1], all_nodes), jnp.int32),
            vmem((1, all_nodes)),
            vmem((round_up(every, LANES), LANES)),
            dma(3), pltpu.SemaphoreType.DMA, dma(owners), dma(owners), dma(owners), dma(owners),
            dma(own_rows, shares), dma(slots, shares), dma(2 * shares), dma(shares, 4),
            dma(4, shares), dma(4), dma(4), dma(own_rows, shares), dma(own_rows, shares),
        ],
        compiler_params=pltpu.CompilerParams(
            collective_id=0, has_side_effects=True, vmem_limit_bytes=56 * 1024 * 1024
        ),
    )(
        field, log_fields, node_index.T, modes_of.T, weights.reshape(1, -1), source, mean,
        *(tables[name] for name in ("pair", "rest", "every", "lanes", "columns", "far", "join")),
    )
    step = math.gcd(pairs, 20)
    block = pl.BlockSpec((2 * step, rows, width), lambda n: (n, 0, 0))
    still = lambda a: pl.BlockSpec(a.shape, lambda n: (0,) * a.ndim)
    shape = jax.ShapeDtypeStruct(field.shape, jnp.float32)
    fresh, update = pl.pallas_call(
        finish_kernel,
        grid=(pairs // step,),
        in_specs=[
            pl.BlockSpec((step, rows, 2 * width), lambda n: (n, 0, 0)),
            pl.BlockSpec((8 * step, LANES), lambda n: (n, 0)),
            block, block, numbers,
        ] + [still(tables[name]) for name in ("lanes", "columns", "rows", "cols")],
        out_specs=[block, block],
        out_shape=[shape, shape],
        scratch_shapes=[vmem((rows, LANES))],
        compiler_params=pltpu.CompilerParams(dimension_semantics=("arbitrary",)),
    )(
        spectrum, fluxes, field, field_before, mean,
        *(tables[name] for name in ("lanes", "columns", "rows", "cols")),
    )
    return (fresh[:modes], update[:modes])


def solution(mesh):
    return jax.shard_map(
        chebyshev_step,
        mesh=mesh,
        in_specs=(
            P("sa", "gy", "gx"),
            P("sa", "gy", "gx"),
            P("sa", "gy", "gx"),
            P(None, ("gy", "sa"), "gx"),
            P(),
            P(),
            P(),
            P(),
        ),
        out_specs=(P("sa", "gy", "gx"), P("sa", "gy", "gx")),
        check_vma=False,
    )
```

```python
import functools
import math

import jax
import jax.numpy as jnp
import numpy as np
from jax import lax
from jax.experimental import pallas as pl
from jax.experimental.pallas import tpu as pltpu
from jax.sharding import PartitionSpec as P


HIGHEST = lax.Precision.HIGHEST
hermite_points = (
    0.0,
    -1.7320508075688772,
    1.7320508075688772,
    -1.355626179974266,
    1.355626179974266,
    -2.8569700138728056,
    2.8569700138728056,
)
storage_rate = 0.0004
relax_weight = 1.6
step_length = 0.3


LANES = 128
NODE_BLOCK = 512
LOG_DEPTH = 16
EARLY = 4
BF16 = jnp.bfloat16


def round_up(value, step):
    return -(-value // step) * step


def product(left, right):
    return jnp.dot(left, right, preferred_element_type=jnp.float32)


def split_two(block):
    high = block.astype(BF16)
    return (high, (block - high.astype(jnp.float32)).astype(BF16))


def split_three(block):
    high = block.astype(BF16)
    rest = block - high.astype(jnp.float32)
    middle = rest.astype(BF16)
    return (high, middle, (rest - middle.astype(jnp.float32)).astype(BF16))


def exact(left, right):
    return jnp.dot(left, right, precision=HIGHEST, preferred_element_type=jnp.float32)


def row_transform(block, pair_ref, rest_ref):
    high, middle, low = split_three(block)
    both = product(jnp.concatenate([high, middle], axis=1), pair_ref[...])
    both = both[:, :LANES] + both[:, LANES:]
    return both + product(jnp.concatenate([low, high], axis=1), rest_ref[...])


def col_transform(block, all_ref):
    high, middle, low = split_three(block)
    stack = jnp.concatenate([high, middle, high, middle, low, high], axis=0)
    return product(all_ref[...], stack)


def make_tables(sizes, per, mean, lane_ref, column_ref, far_ref, inverse, by_row, by_col, col_table, row_table):
    count_x, count_y = sizes
    half = LANES // 2
    column = lambda k, rows=LANES: jnp.broadcast_to(column_ref[:rows, k : k + 1], (rows, LANES))
    lanes = lambda k: lane_ref[k : k + 1, :]
    upright = 1.0 / (storage_rate + mean * (column(0) + lanes(5)))
    flat = 1.0 / (storage_rate + mean * (column(3) + lanes(2)))
    inverse[:, :LANES] = flat[:half]
    inverse[:, LANES:] = flat[:half]
    lane = lax.broadcasted_iota(jnp.int32, (LANES, LANES), 1)
    row = lax.broadcasted_iota(jnp.int32, (LANES, LANES), 0)
    for end in range(2):
        part = upright * column(1 + end)
        by_col[:LANES, end * LANES : (end + 1) * LANES] = jnp.where(lane < half, part, 0.0)
        by_col[LANES:, end * LANES : (end + 1) * LANES] = jnp.where(lane < half, 0.0, part)
        part = flat * column(4 + end)
        by_row[:, 2 * end * LANES : (2 * end + 1) * LANES] = jnp.where(row < half, part, 0.0)
        by_row[:, (2 * end + 1) * LANES : (2 * end + 2) * LANES] = jnp.where(row < half, 0.0, part)

    def tables(count, same, cross):
        shrink = [
            1.0 / (1.0 / mean + 2.0 * same - 2.0 * math.cos(n * math.pi / count) * cross)
            for n in range(1, count)
        ]
        sine = lambda a, b: math.sin(a * b % (2 * count) * math.pi / count)
        return [
            [
                sum((2.0 / count) * sine(n, a) * sine(n, b) * shrink[n - 1] for n in range(1, count))
                for b in range(1, count)
            ]
            for a in range(1, count)
        ]

    total = lambda a: jnp.sum(a, axis=0, keepdims=True)
    ends = column(1), column(2)
    found = tables(
        count_x, total(upright * ends[0] * ends[0]), total(upright * ends[0] * ends[1])
    )
    for a in range(count_x - 1):
        for b in range(count_x - 1):
            col_table[a, b : b + 1, :] = found[a][b]
    far = far_ref[0:1, :]
    wide = lambda k: jnp.broadcast_to(column_ref[:half, k : k + 1], (half, far.shape[1]))
    deep = 1.0 / (storage_rate + mean * (wide(3) + far))
    found = tables(
        count_y, total(deep * wide(4) * wide(4)), total(deep * wide(4) * wide(5))
    )
    depth = row_table.shape[1]
    where_row = lax.broadcasted_iota(jnp.int32, (depth, far.shape[1]), 0) // per
    for shift in range(-(count_y - 2), count_y - 1):
        table = jnp.zeros((depth, far.shape[1]), jnp.float32)
        for a in range(count_y - 1):
            if 0 <= a + shift < count_y - 1:
                table = jnp.where(where_row == a, found[a][a + shift], table)
        row_table[shift + count_y - 2] = table


def solve_fluxes(sizes, per, got, back, lane_ref, join_ref, by_row, by_col, col_table, row_table):
    count_x, count_y = sizes
    depth = row_table.shape[1]
    rows = count_y * per
    lanes = lambda k: lane_ref[k : k + 1, :]
    take = lambda block, kind: got[pl.ds(block * rows * 8 + kind, depth, stride=8), :]
    row = lax.broadcasted_iota(jnp.int32, (depth, LANES), 0)
    up = lambda a, by=1: pltpu.roll(a, (-by * per) % depth, 0)
    down = lambda a: jnp.where(row < per, 0.0, pltpu.roll(a, per, 0))
    blocks, cuts = range(count_x), range(1, count_x)

    def through_cols(first, last):
        jump = [first[cut] - last[cut - 1] for cut in cuts]
        return [
            sum(col_table[a, b : b + 1, :] * jump[b] for b in range(count_x - 1))
            for a in range(count_x - 1)
        ]

    fluxes = through_cols([take(b, 0) for b in blocks], [take(b, 1) for b in blocks])
    spread = [exact(flux, by_row[...]) for flux in fluxes]

    def at_row(block, end, half):
        part = slice((2 * end + half) * LANES, (2 * end + half + 1) * LANES)
        value = take(block, 2 + 2 * end + half)
        if block < count_x - 1:
            value = value + spread[block][:, part] * lanes(1)
        if block > 0:
            value = value - spread[block - 1][:, part] * lanes(0)
        return value

    jump = jnp.concatenate(
        [
            jnp.concatenate([up(at_row(b, 0, half)) - at_row(b, 1, half) for b in blocks], axis=1)
            for half in range(2)
        ],
        axis=0,
    )
    far = lax.dot_general(
        jump, join_ref[...], (((1,), (1,)), ((), ())), precision=HIGHEST,
        preferred_element_type=jnp.float32,
    )
    mixed = []
    for half in range(2):
        part = far[half * depth : (half + 1) * depth]
        mixed.append(sum(
            row_table[shift + count_y - 2] * (up(part, shift) if shift else part)
            for shift in range(-(count_y - 2), count_y - 1)
        ))
    near = exact(jnp.concatenate(mixed, axis=0), join_ref[...])
    through_rows = [
        [near[half * depth : (half + 1) * depth, b * LANES : (b + 1) * LANES] for half in range(2)]
        for b in blocks
    ]
    ends = []
    for b in blocks:
        reach = exact(jnp.concatenate(through_rows[b], axis=1), by_col[...])
        ends.append([
            lanes(4) * reach[:, end * LANES : (end + 1) * LANES]
            - lanes(3) * down(reach[:, end * LANES : (end + 1) * LANES])
            for end in range(2)
        ])
    more = through_cols([end[0] for end in ends], [end[1] for end in ends])
    fluxes = [a + b for a, b in zip(fluxes, more)]
    nothing = jnp.zeros((depth, LANES), jnp.float32)
    for b in blocks:
        left = fluxes[b - 1] if b > 0 else nothing
        right = fluxes[b] if b < count_x - 1 else nothing
        top = [down(part) for part in through_rows[b]]
        for kind, value in enumerate([left, right] + top + through_rows[b]):
            back[pl.ds(b * rows * 8 + kind, depth, stride=8), :] = value


def stacked(parts, depth):
    missing = depth - sum(part.shape[0] for part in parts)
    if missing:
        parts = parts + [jnp.zeros((missing,) + parts[0].shape[1:], parts[0].dtype)]
    return jnp.concatenate(parts, axis=0)


def node_kernel(
    sizes, field_ref, log_ref, node_ref, mode_ref, weight_ref,
    source_ref, mean_ref, pair_ref, rest_ref, all_ref, lane_ref, column_ref, far_ref, join_ref,
    spec_ref, flux_ref,
    lines, log_lines, log_sides, sides, total, line_op, log_op, basis_op, germ_op, weight_op,
    edge, value_prev, half_prev, flux_prev,
    home, spectrum, origin, traces, got, back, tall, join,
    inverse, by_row, by_col, col_table, row_table,
    block_field, field_cols, log_cols, picks, shares_of, degrees,
    load_sem, spec_sem, trace_send, trace_recv, flux_send, flux_recv,
    line_send, line_recv, halo_send, side_send, side_recv, log_send, log_recv, out_send, out_recv,
):
    count_x, count_y, shares, group = sizes
    modes, rows, width = field_ref.shape
    own_rows = rows // shares
    every = shares * modes
    below, above = own_rows, own_rows + 1
    blocks = basis_op.shape[0] // NODE_BLOCK
    x, y, share = (lax.axis_index(axis) for axis in ("gx", "gy", "sa"))
    first_y = jnp.logical_and(y == 0, share == 0)
    last_y = jnp.logical_and(y == count_y - 1, share == shares - 1)
    not_first, not_last = jnp.logical_not(first_y), jnp.logical_not(last_y)
    peer = lambda step: lax.rem(share + step, shares)

    def remote(source, target, send, recv, **place):
        return pltpu.make_async_remote_copy(
            src_ref=source, dst_ref=target, send_sem=send, recv_sem=recv,
            device_id=place, device_id_type=pl.DeviceIdType.MESH,
        )

    def arrived(target, recv):
        pltpu.make_async_copy(target, target, recv).wait()

    load_field = pltpu.make_async_copy(field_ref, block_field, load_sem.at[2])
    load_field.start()
    load_origin = pltpu.make_async_copy(source_ref, origin, load_sem.at[0])
    load_origin.start()
    load_join = pltpu.make_async_copy(join_ref, join, load_sem.at[1])
    load_join.start()

    barrier = pltpu.get_barrier_semaphore()
    greet = lambda **place: pl.semaphore_signal(
        barrier, inc=1, device_id=place, device_id_type=pl.DeviceIdType.MESH
    )
    for step in range(1, shares):
        greet(sa=peer(step))
    owners = count_x * count_y
    me = x * count_y + y
    other = lambda step: lax.rem(me + step, owners)
    at_owner = lambda owner: dict(gx=lax.div(owner, count_y), gy=lax.rem(owner, count_y))
    for step in range(1, owners):
        greet(**at_owner(other(step)))
    conditions = (
        (x > 0, dict(gx=x - 1)), (x < count_x - 1, dict(gx=x + 1)),
        (y > 0, dict(gy=y - 1)), (y < count_y - 1, dict(gy=y + 1)),
    )
    for condition, place in conditions:
        @pl.when(condition)
        def _():
            for step in range(1, shares):
                greet(sa=peer(step), **place)
    per = traces.shape[0] // 8 // owners
    plane = (count_x, count_y)
    beyond = got.shape[0] - traces.shape[0]
    if beyond:
        got[traces.shape[0] :, :] = jnp.zeros((beyond, LANES), jnp.float32)
    traces[...] = jnp.zeros_like(traces)
    make_tables(
        plane, per, mean_ref[0], lane_ref, column_ref, far_ref,
        inverse, by_row, by_col, col_table, row_table,
    )

    total[...] = jnp.zeros_like(total)

    nodes_given = node_ref.shape[1]
    picks[...] = jnp.zeros_like(picks)
    picks[:, :nodes_given] = node_ref[...]
    shares_of[...] = jnp.zeros_like(shares_of)
    shares_of[:, :nodes_given] = weight_ref[...].reshape(1, nodes_given)
    degrees[...] = jnp.zeros_like(degrees)
    for start_at in range(0, every, LANES):
        width_at = min(LANES, every - start_at)
        degrees[start_at : start_at + mode_ref.shape[0], :width_at] = mode_ref[
            :, start_at : start_at + width_at
        ].astype(jnp.float32)
        here = slice(start_at, start_at + LANES)
        degrees[here, :] = jnp.transpose(degrees[here, :])

    sides_met = sum(condition.astype(jnp.int32) for condition, _ in conditions)
    pl.semaphore_wait(barrier, owners - 1 + (shares - 1) * (1 + sides_met))

    remote_copies = []

    def start(condition, copy):
        remote_copies.append((condition, copy))
        if condition is None:
            copy.start()
        else:
            pl.when(condition)(copy.start)

    row_of = lambda row: field_ref.at[:, row, :]
    flat_next = jnp.where(share == shares - 1, y + 1, y), lax.rem(share + 1, shares)
    flat_last = jnp.where(share == 0, y - 1, y), lax.rem(share + shares - 1, shares)
    start(y > 0, remote(
        row_of(0), lines.at[below, share], halo_send.at[0], line_recv.at[below, share],
        gy=y - 1, sa=jnp.int32(shares - 1),
    ))
    start(y < count_y - 1, remote(
        row_of(rows - 1), lines.at[above, share], halo_send.at[1], line_recv.at[above, share],
        gy=y + 1, sa=jnp.int32(0),
    ))
    for step in range(1, shares):
        to = peer(step)
        start(to > 0, remote(
            row_of(jnp.maximum(to * own_rows - 1, 0)), lines.at[above, share],
            halo_send.at[2 * step], line_recv.at[above, share], sa=to,
        ))
        start(to < shares - 1, remote(
            row_of(jnp.minimum((to + 1) * own_rows, rows - 1)), lines.at[below, share],
            halo_send.at[2 * step + 1], line_recv.at[below, share], sa=to,
        ))
    own_above = pltpu.make_async_copy(
        row_of(jnp.maximum(share * own_rows - 1, 0)), lines.at[above, share],
        line_recv.at[above, share],
    )
    own_below = pltpu.make_async_copy(
        row_of(jnp.minimum((share + 1) * own_rows, rows - 1)), lines.at[below, share],
        line_recv.at[below, share],
    )
    pl.when(share > 0)(own_above.start)
    pl.when(share < shares - 1)(own_below.start)
    def line_copy(row, step):
        to = peer(step)
        return remote(
            row_of(to * own_rows + row), lines.at[row, share], line_send.at[row, step],
            line_recv.at[row, share], sa=to,
        )

    def send_lines(row, carry):
        for step in range(1, shares):
            line_copy(row, step).start()
        pltpu.make_async_copy(
            row_of(share * own_rows + row), lines.at[row, share], line_recv.at[row, share]
        ).start()
        return carry

    early = min(EARLY, own_rows)
    lax.fori_loop(0, early, send_lines, 0)
    pairs = modes // 2
    unroll = max(n for n in range(1, 11) if pairs % n == 0)
    pick_row = lax.broadcasted_iota(jnp.int32, (16, 2 * LANES), 0)
    pick_lane = lax.broadcasted_iota(jnp.int32, (16, 2 * LANES), 1) % LANES
    first_pick = jnp.logical_and(pick_row == 0, pick_lane == 0)
    last_pick = jnp.logical_and(pick_row == 1, pick_lane == LANES - 1)
    pick = jnp.where(jnp.logical_or(first_pick, last_pick), 1.0, 0.0).astype(BF16)

    def columns_of(block):
        return lax.dot_general(
            pick, jnp.concatenate(split_two(block), axis=1), (((1,), (1,)), ((), ())),
            preferred_element_type=jnp.float32,
        )

    log_cols[...] = jnp.zeros_like(log_cols)
    for level in range(log_ref.shape[0]):
        found = columns_of(log_ref[level])
        for end in range(2):
            log_cols[end, level : level + 1, :own_rows] = found[end : end + 1, :]
    load_field.wait()

    left_lanes = lax.broadcasted_iota(jnp.int32, (1, LANES), 1) < rows

    def take_columns(index, carry):
        for pair in range(unroll):
            mode = 2 * (index * unroll + pair)
            found = columns_of(block_field[pl.ds(mode, 2)].reshape(2 * rows, LANES))
            for half in range(2):
                part = pltpu.roll(found, LANES - rows, 1) if half else found
                for end in range(2):
                    field_cols[end, pl.ds(mode + half, 1), :] = part[end : end + 1, :]
                both = jnp.where(left_lanes, part[0:1, :], pltpu.roll(part, rows, 1)[1:2, :])
                field_cols[2, pl.ds(mode + half, 1), :] = both
        return carry

    lax.fori_loop(0, pairs // unroll, take_columns, 0)
    log_copies = (
        (not_last, log_ref.at[:, own_rows - 1, :], log_lines.at[1], 0,
         dict(gy=flat_next[0], sa=flat_next[1])),
        (not_first, log_ref.at[:, 0, :], log_lines.at[0], 1,
         dict(gy=flat_last[0], sa=flat_last[1])),
        (x < count_x - 1, log_cols.at[1], log_sides.at[0], 2, dict(gx=x + 1)),
        (x > 0, log_cols.at[0], log_sides.at[1], 3, dict(gx=x - 1)),
    )
    for condition, source, target, slot, place in log_copies:
        start(condition, remote(source, target, log_send.at[slot], log_recv.at[slot], **place))
    for step in range(shares):
        to = peer(step)
        if step:
            start(None, remote(
                field_cols.at[2], sides.at[0, share], side_send.at[step, 0],
                side_recv.at[0, share], sa=to,
            ))
        else:
            pltpu.make_async_copy(
                field_cols.at[2], sides.at[0, share], side_recv.at[0, share]
            ).start()
        start(x > 0, remote(
            field_cols.at[0], sides.at[2, share], side_send.at[step, 2],
            side_recv.at[2, share], gx=x - 1, sa=to,
        ))
        start(x < count_x - 1, remote(
            field_cols.at[1], sides.at[3, share], side_send.at[step, 3],
            side_recv.at[3, share], gx=x + 1, sa=to,
        ))

    lax.fori_loop(early, own_rows, send_lines, 0)
    def make_basis(block, carry):
        lanes = pl.ds(pl.multiple_of(block * LANES, LANES), LANES)
        picked = picks[:, lanes]
        germs = jnp.zeros(picked.shape, jnp.float32)
        for level, point in enumerate(hermite_points):
            germs = jnp.where(picked == level, point, germs)
        square = germs * germs
        second = (square - 1.0) / math.sqrt(2.0)
        third = (square * germs - 3.0 * germs) / math.sqrt(6.0)
        values = jnp.ones((every, LANES), jnp.float32)
        for germ in range(germs.shape[0]):
            degree = jnp.broadcast_to(degrees[:every, germ : germ + 1], (every, LANES))
            at = lambda table: jnp.broadcast_to(table[germ : germ + 1, :], (every, LANES))
            values = values * jnp.where(
                degree == 0, 1.0,
                jnp.where(degree == 1, at(germs), jnp.where(degree == 2, at(second), at(third))),
            )
        high, low = split_two(values)
        wide = lambda a: a.astype(jnp.float32)
        stack = stacked([wide(high), wide(high), wide(low)], basis_op.shape[1])
        basis_op[lanes, :] = jnp.transpose(stack).astype(BF16)
        high, low = split_two(values * (2.0 * shares_of[:, lanes]))
        weight_op[:every, lanes] = high
        weight_op[every:, lanes] = low
        spread = stacked([-jnp.ones((1, LANES), jnp.float32), -germs], LOG_DEPTH)
        high, low = split_two(spread)
        stack = stacked([wide(high), wide(high), wide(low)], LANES)
        germ_op[lanes, :] = jnp.transpose(stack).astype(BF16)
        return carry

    lax.fori_loop(0, basis_op.shape[0] // LANES, make_basis, 0)

    def log_stack(block):
        high, low = split_two(stacked([block], LOG_DEPTH))
        return stacked([high, low, high], LANES)

    def field_stack(block):
        high, low = split_two(block)
        return stacked([high, low, high], line_op.shape[1])

    for condition, _, target, slot, _ in (
        (not_first, None, log_lines.at[1], 0, None), (not_last, None, log_lines.at[0], 1, None),
        (x > 0, None, log_sides.at[0], 2, None), (x < count_x - 1, None, log_sides.at[1], 3, None),
    ):
        @pl.when(condition)
        def _():
            arrived(target, log_recv.at[slot])

    def make_log(row, carry):
        log_op[row] = log_stack(log_ref[:, row, :])
        return carry

    lax.fori_loop(0, own_rows, make_log, 0)
    log_op[below] = log_stack(
        jnp.where(last_y, log_ref[:, own_rows - 1, :], log_lines[0])
    )
    log_op[above] = log_stack(jnp.where(first_y, log_ref[:, 0, :], log_lines[1]))

    def at_nodes(nodes, field, logs):
        return (product(basis_op[nodes, :], field), jnp.exp(product(germ_op[nodes, :], logs)))

    def flux(later, earlier, half_later, half_earlier):
        return (later - earlier) * pl.reciprocal(half_later + half_earlier)

    def project(nodes, applied):
        high = applied.astype(BF16)
        rest = applied - high.astype(jnp.float32)
        middle = rest.astype(BF16)
        low = (rest - middle.astype(jnp.float32)).astype(BF16)
        both = product(weight_op[:, nodes], high) + product(weight_op[:, nodes], middle)
        return both[:every] + both[every:] + product(weight_op[:every, nodes], low)

    node_slice = lambda block: pl.ds(pl.multiple_of(block * NODE_BLOCK, NODE_BLOCK), NODE_BLOCK)

    for kind, condition in ((0, None), (2, x < count_x - 1), (3, x > 0)):
        for source in range(shares):
            wait = lambda: arrived(sides.at[kind, source], side_recv.at[kind, source])
            wait() if condition is None else pl.when(condition)(wait)
    flat = lambda ref: ref.reshape(every, LANES)
    turn = lax.rem(LANES - share * own_rows, LANES)
    side = [pltpu.roll(flat(sides[kind]), turn, 1) for kind in (0, 0, 2, 3)]
    side[1] = pltpu.roll(side[1], LANES - rows, 1)
    log_first, log_last = log_cols[0], log_cols[1]
    before = jnp.where(x == 0, side[0], side[3])
    after = jnp.where(x == count_x - 1, side[1], side[2])
    log_before = jnp.where(x == 0, log_first, log_sides[0])
    log_after = jnp.where(x == count_x - 1, log_last, log_sides[1])

    def beside(low_part, high_part):
        lane = lax.broadcasted_iota(jnp.int32, low_part.shape, 1)
        return jnp.where(lane < own_rows, low_part, pltpu.roll(high_part, own_rows, 1))

    line_op[0, :, :LANES] = field_stack(beside(before, side[1]))
    line_op[0, :, LANES:] = field_stack(beside(side[0], after))
    log_edge = jnp.concatenate(
        [log_stack(beside(log_before, log_last)), log_stack(beside(log_first, log_after))], axis=1
    )
    edge[...] = jnp.zeros_like(edge)

    def make_edge(block, carry):
        nodes = node_slice(block)
        values, halves = at_nodes(nodes, line_op[0], log_edge)
        edge[...] += project(nodes, flux(
            values[:, LANES:], values[:, :LANES], halves[:, LANES:], halves[:, :LANES]
        ))
        return carry

    lax.fori_loop(0, blocks, make_edge, 0)

    def wait_line(row):
        for source in range(shares):
            arrived(lines.at[row, source], line_recv.at[row, source])

    wait_line(0)
    pl.when(not_first)(lambda: wait_line(above))
    line = flat(lines[0])
    line_op[0, :, :LANES] = field_stack(jnp.where(first_y, line, flat(lines[above])))
    line_op[0, :, LANES:] = field_stack(line)

    def begin(block, carry):
        nodes = node_slice(block)
        logs = jnp.concatenate([log_op[above], log_op[0]], axis=1)
        values, halves = at_nodes(nodes, line_op[0], logs)
        value_prev[nodes, :] = values[:, LANES:]
        half_prev[nodes, :] = halves[:, LANES:]
        flux_prev[nodes, :] = flux(
            values[:, LANES:], values[:, :LANES], halves[:, LANES:], halves[:, :LANES]
        )
        return carry

    lax.fori_loop(0, blocks, begin, 0)

    home_row = lambda row: home.at[pl.ds(row * modes, modes), :]

    def out_copy(row, step):
        to = peer(step)
        return remote(
            total.at[row, to], home_row(share * own_rows + row), out_send.at[row, step],
            out_recv.at[row, share], sa=to,
        )

    def own_copy(row):
        return pltpu.make_async_copy(
            total.at[row, share], home_row(share * own_rows + row), out_recv.at[row, share]
        )

    def take_origin(index, carry):
        for pair in range(unroll):
            one_origin(index * unroll + pair)
        return carry

    def one_origin(pair):
        block = origin[pl.ds(2 * pair, 2)].reshape(2 * rows, LANES)
        block = row_transform(block, pair_ref, rest_ref)
        spectrum[pair] = col_transform(
            jnp.concatenate([block[:rows], block[rows:]], axis=1), all_ref
        )

    groups = own_rows // group

    def take_group(index, carry):
        base = index * group
        for ahead in range(1, group + 1):
            row = base + ahead
            if ahead < group:
                wait_line(row)
            else:
                pl.when(jnp.logical_or(row < own_rows, not_last))(lambda: wait_line(row))
            line = flat(lines[row])
            if ahead == group:
                line = jnp.where(
                    jnp.logical_and(row == own_rows, last_y), flat(lines[row - 1]), line
                )
            place = pl.ds((ahead - 1) % 2 * LANES, LANES)
            line_op[(ahead - 1) // 2, :, place] = field_stack(line)

        def take_nodes(block, carry):
            nodes = node_slice(block)
            value, half, flux_up = value_prev[nodes, :], half_prev[nodes, :], flux_prev[nodes, :]
            inside = lax.broadcasted_iota(jnp.int32, value.shape, 1) < LANES - 1
            for pair in range(group // 2):
                row = base + 2 * pair
                logs = jnp.concatenate([log_op[row + 1], log_op[row + 2]], axis=1)
                values, halves = at_nodes(nodes, line_op[pair], logs)
                applied = []
                for here in range(2):
                    value_next = values[:, here * LANES : (here + 1) * LANES]
                    half_next = halves[:, here * LANES : (here + 1) * LANES]
                    flux_down = flux(value_next, value, half_next, half)
                    across = jnp.where(
                        inside,
                        flux(
                            pltpu.roll(value, LANES - 1, 1), value,
                            pltpu.roll(half, LANES - 1, 1), half,
                        ),
                        0.0,
                    )
                    applied.append(
                        (0.5 * storage_rate) * value
                        - (across - pltpu.roll(across, 1, 1)) - (flux_down - flux_up)
                    )
                    value, half, flux_up = value_next, half_next, flux_down
                sums = project(nodes, jnp.concatenate(applied, axis=1))
                parts = sums.reshape(shares, modes, 2 * LANES)
                total[row] += parts[:, :, :LANES]
                total[row + 1] += parts[:, :, LANES:]
            value_prev[nodes, :] = value
            half_prev[nodes, :] = half
            flux_prev[nodes, :] = flux_up
            return carry

        lax.fori_loop(0, blocks, take_nodes, 0, unroll=True)
        lane = lax.broadcasted_iota(jnp.int32, (every, LANES), 1)
        for step in range(group):
            row = base + step
            left = pltpu.roll(edge[...], lax.rem(LANES - row, LANES), 1)
            right = pltpu.roll(edge[...], LANES - 1 - own_rows - row, 1)
            change = jnp.where(lane == 0, left, 0.0) - jnp.where(lane == LANES - 1, right, 0.0)
            line = row_transform(flat(total[row]) + change, pair_ref, rest_ref)
            total[row] = line.reshape(shares, modes, LANES)
        for step in range(group):
            row = base + step
            for to in range(1, shares):
                out_copy(row, to).start()
            own_copy(row).start()
        return carry

    lax.fori_loop(0, groups, take_group, 0)
    load_origin.wait()
    lax.fori_loop(0, pairs // unroll, take_origin, 0)

    def arrive(row, carry):
        for step in range(1, shares):
            source = peer(step)
            arrived(home_row(source * own_rows + row), out_recv.at[row, source])
        own_copy(row).wait()
        return carry

    lax.fori_loop(0, own_rows, arrive, 0)

    def take_pair(pair, columns):
        line = [home[pl.ds(2 * pair + half, rows, stride=modes), :] for half in range(2)]
        line = col_transform(jnp.concatenate(line, axis=1), all_ref)
        line = spectrum[pair] - line
        spectrum[pair] = line
        alone = line * inverse[...]
        trace = pl.ds(8 * pair, 8)
        lane = lax.broadcasted_iota(jnp.int32, (LANES, LANES), 1)
        result = []
        for end in range(2):
            ends = jnp.broadcast_to(column_ref[:rows, 4 + end : 5 + end], (rows, 2 * LANES))
            result.append(jnp.sum(alone * ends, axis=0, keepdims=True))
            upright = jnp.concatenate([alone[:, :LANES], alone[:, LANES:]], axis=0)
            upright = jnp.sum(upright * lane_ref[end : end + 1, :], axis=1, keepdims=True)
            columns = jnp.where(lane == end * (LANES // 2) + pair, upright, columns)
        blank = jnp.zeros((2, LANES), jnp.float32)
        traces[trace, :] = jnp.concatenate(
            [blank, result[0][:, :LANES], result[0][:, LANES:],
             result[1][:, :LANES], result[1][:, LANES:], blank], axis=0
        )
        return columns

    def take_pairs(index, columns):
        for pair in range(unroll):
            columns = take_pair(index * unroll + pair, columns)
        return columns

    columns = lax.fori_loop(
        0, pairs // unroll, take_pairs, jnp.zeros((LANES, LANES), jnp.float32)
    )
    tall[...] = jnp.transpose(columns)
    for end in range(2):
        traces[pl.ds(end, pairs, stride=8), :] = tall[pl.ds(end * (LANES // 2), pairs), :]
    save = pltpu.make_async_copy(spectrum, spec_ref, spec_sem)
    save.start()

    piece = lambda owner: pl.ds(owner * per * 8, per * 8)

    def trace_copy(step):
        to = other(step)
        return remote(
            traces.at[piece(to), :], got.at[piece(me), :], trace_send.at[step],
            trace_recv.at[me], **at_owner(to),
        )

    def flux_copy(step):
        to = other(step)
        return remote(
            back.at[piece(to), :], flux_ref.at[piece(me), :], flux_send.at[step],
            flux_recv.at[me], **at_owner(to),
        )

    used = lambda owner: owner * per < pairs
    for step in range(1, owners):
        pl.when(used(other(step)))(trace_copy(step).start)
    got[piece(me), :] = traces[piece(me), :]
    load_join.wait()
    for step in range(1, owners):
        @pl.when(used(me))
        def _():
            arrived(got.at[piece(other(step)), :], trace_recv.at[other(step)])
    solve_fluxes(plane, per, got, back, lane_ref, join, by_row, by_col, col_table, row_table)
    for step in range(1, owners):
        pl.when(used(me))(flux_copy(step).start)
    own_flux = pltpu.make_async_copy(
        back.at[piece(me), :], flux_ref.at[piece(me), :], flux_recv.at[me]
    )
    own_flux.start()

    def sent(row, carry):
        for step in range(1, shares):
            line_copy(row, step).wait_send()
            out_copy(row, step).wait_send()
        return carry

    lax.fori_loop(0, own_rows, sent, 0)
    for condition, copy in remote_copies:
        if condition is None:
            copy.wait_send()
        else:
            pl.when(condition)(copy.wait_send)
    save.wait()
    own_flux.wait()
    for step in range(1, owners):
        pl.when(used(other(step)))(trace_copy(step).wait_send)
        pl.when(used(me))(flux_copy(step).wait_send)

        @pl.when(used(other(step)))
        def _():
            arrived(flux_ref.at[piece(other(step)), :], flux_recv.at[other(step)])


def finish_kernel(
    spec_ref, flux_ref, now_ref, before_ref, mean_ref, lane_ref, column_ref, rows_ref, cols_ref,
    fresh_ref, update_ref, inverse,
):
    rows = spec_ref.shape[1]
    column = lambda k: jnp.broadcast_to(column_ref[:rows, k : k + 1], (rows, LANES))

    @pl.when(pl.program_id(0) == 0)
    def start():
        inverse[...] = 1.0 / (storage_rate + mean_ref[0] * (column(3) + lane_ref[2:3, :]))

    upright = jnp.transpose(flux_ref[...])
    for pair in range(spec_ref.shape[0]):
        parts = []
        for half in range(2):
            beside = lambda kind: jnp.broadcast_to(
                upright[half * rows : (half + 1) * rows, 8 * pair + kind : 8 * pair + kind + 1],
                (rows, LANES),
            )
            over = lambda kind: flux_ref[8 * pair + kind : 8 * pair + kind + 1, :]
            part = spec_ref[pair, :, half * LANES : (half + 1) * LANES]
            part = part + (beside(1) * lane_ref[1:2, :] - beside(0) * lane_ref[0:1, :])
            part = part + (column(5) * over(4 + half) - column(4) * over(2 + half))
            parts.append(part * inverse[...])
        high, low = split_two(jnp.concatenate(parts, axis=1))
        part = product(rows_ref[...], jnp.concatenate([high, low, high], axis=0))
        high, low = split_two(jnp.concatenate([part[:, :LANES], part[:, LANES:]], axis=0))
        part = product(jnp.concatenate([high, low], axis=1), cols_ref[...])
        part = (part[:, :LANES] + part[:, LANES:]).reshape(2, rows, LANES)
        mode = slice(2 * pair, 2 * pair + 2)
        update_ref[mode] = part
        before = before_ref[mode]
        fresh_ref[mode] = before + relax_weight * (now_ref[mode] - before + step_length * part)


def cosine_table(length):
    freq, cells = np.arange(length)[:, None], np.arange(length)[None, :]
    factor = np.where(freq == 0, math.sqrt(1.0 / length), math.sqrt(2.0 / length))
    return factor * np.cos((freq * (2 * cells + 1) % (4 * length)) * (math.pi / (2 * length)))


def pieces(table):
    found, rest = [], table.astype(np.float32)
    for _ in range(3):
        found.append(rest.astype(BF16))
        rest = rest - found[-1].astype(np.float32)
    return found


def constant_tables(count_x, rows, width):
    eigen = lambda count: 2.0 - 2.0 * np.cos(np.arange(count) * (math.pi / count))
    row_table, col_table = cosine_table(rows), cosine_table(width)
    far_table = cosine_table(count_x * width)
    join = np.einsum("kix,lx->kil", far_table.reshape(-1, count_x, width), col_table)
    twice = lambda a: np.concatenate([a, a])
    lanes = [
        col_table[:, 0], col_table[:, -1], eigen(width),
        twice(row_table[:, 0]), twice(row_table[:, -1]), twice(eigen(rows)),
    ]
    columns = [lanes[2], lanes[0], lanes[1], lanes[5], lanes[3], lanes[4]]
    grow = lambda a: np.pad(np.stack(a), ((0, 8 - len(a)), (0, 0))).astype(np.float32)
    high, middle, low = pieces(col_table.T)
    front = pieces(col_table)
    pair = np.block([[high, middle], [high, middle]])
    rest = np.concatenate([high, low])
    back = np.block([[front[0], front[1]], [front[0], np.zeros_like(high)]])
    high, middle, low = pieces(row_table)
    every = np.concatenate([high, high, middle, middle, high, low], axis=1)
    high, low, _ = pieces(row_table.T)
    rows_back = np.concatenate([high, high, low], axis=1)
    return dict(
        pair=pair, rest=rest, every=every, lanes=grow(lanes), columns=grow(columns).T.copy(),
        far=grow([eigen(count_x * width)]), join=join.reshape(len(far_table), -1).astype(np.float32),
        rows=rows_back, cols=back,
    )


def chebyshev_step(
    field, field_before, source, log_fields, weights, mean_perm, node_index, mode_index
):
    modes, rows, width = field.shape
    count_x, count_y, shares = (lax.axis_size(axis) for axis in ("gx", "gy", "sa"))
    padded = round_up(modes, 16)
    grow = lambda a, size, dim: jnp.pad(
        a, [(0, size - a.shape[d] if d == dim else 0) for d in range(a.ndim)]
    )
    field, field_before, source = (grow(a, padded, 0) for a in (field, field_before, source))
    mean = mean_perm.reshape(1)
    tables = constant_tables(count_x, rows, width)
    pairs, owners = padded // 2, count_x * count_y
    per = -(-pairs // owners)
    depth_solve = round_up(count_y * per, 8)
    extra = 8 * (depth_solve - count_y * per)
    own_rows = rows // shares
    nodes = node_index.shape[0]
    all_nodes = round_up(nodes, NODE_BLOCK)
    modes_of = grow(mode_index.reshape(shares, modes, -1), padded, 1).reshape(shares * padded, -1)
    levels = log_fields.shape[0]
    group = math.gcd(own_rows, 8)
    every = shares * padded
    depth = round_up(3 * every, LANES)
    slots = own_rows + 2
    vmem = lambda shape, kind=jnp.float32: pltpu.VMEM(shape, kind)
    dma = lambda *shape: pltpu.SemaphoreType.DMA(shape)
    place = pl.BlockSpec(memory_space=pl.ANY)
    whole = pl.BlockSpec(memory_space=pltpu.VMEM)
    numbers = pl.BlockSpec(memory_space=pltpu.SMEM)
    spectrum, fluxes = pl.pallas_call(
        functools.partial(node_kernel, (count_x, count_y, shares, group)),
        in_specs=[place, whole, whole, whole, whole]
        + [place, numbers] + [whole] * 6 + [place],
        out_specs=[place, place],
        out_shape=[
            jax.ShapeDtypeStruct((pairs, rows, 2 * width), jnp.float32),
            jax.ShapeDtypeStruct((owners * per * 8, LANES), jnp.float32),
        ],
        scratch_shapes=[
            vmem((slots, shares, padded, LANES)),
            vmem((2, levels, LANES)),
            vmem((2, levels, LANES)),
            vmem((4, shares, padded, LANES)),
            vmem((own_rows, shares, padded, LANES)),
            vmem((group // 2, depth, 2 * LANES), BF16),
            vmem((slots, LANES, LANES), BF16),
            vmem((all_nodes, depth), BF16),
            vmem((all_nodes, LANES), BF16),
            vmem((2 * every, all_nodes), BF16),
            vmem((every, LANES)),
            vmem((all_nodes, LANES)),
            vmem((all_nodes, LANES)),
            vmem((all_nodes, LANES)),
            vmem((rows * padded, LANES)),
            vmem((pairs, rows, 2 * LANES)),
            vmem((padded, rows, LANES)),
            vmem((owners * per * 8, LANES)),
            vmem((owners * per * 8 + extra, LANES)),
            vmem((owners * per * 8 + extra, LANES)),
            vmem((LANES, LANES)),
            vmem(tables["join"].shape),
            vmem((rows, 2 * LANES)),
            vmem((LANES, 4 * LANES)),
            vmem((2 * LANES, 2 * LANES)),
            vmem((count_x - 1, round_up(count_x - 1, 8), LANES)),
            vmem((2 * count_y - 3, depth_solve, count_x * width)),
            vmem((padded, rows, LANES)),
            vmem((3, padded, LANES)),
            vmem((2, levels, LANES)),
            vmem((node_index.shape[1], all_nodes), jnp.int32),
            vmem((1, all_nodes)),
            vmem((round_up(every, LANES), LANES)),
            dma(3), pltpu.SemaphoreType.DMA, dma(owners), dma(owners), dma(owners), dma(owners),
            dma(own_rows, shares), dma(slots, shares), dma(2 * shares), dma(shares, 4),
            dma(4, shares), dma(4), dma(4), dma(own_rows, shares), dma(own_rows, shares),
        ],
        compiler_params=pltpu.CompilerParams(
            collective_id=0, has_side_effects=True, vmem_limit_bytes=56 * 1024 * 1024
        ),
    )(
        field, log_fields, node_index.T, modes_of.T, weights, source, mean,
        *(tables[name] for name in ("pair", "rest", "every", "lanes", "columns", "far", "join")),
    )
    step = math.gcd(pairs, 20)
    block = pl.BlockSpec((2 * step, rows, width), lambda n: (n, 0, 0))
    still = lambda a: pl.BlockSpec(a.shape, lambda n: (0,) * a.ndim)
    shape = jax.ShapeDtypeStruct(field.shape, jnp.float32)
    fresh, update = pl.pallas_call(
        finish_kernel,
        grid=(pairs // step,),
        in_specs=[
            pl.BlockSpec((step, rows, 2 * width), lambda n: (n, 0, 0)),
            pl.BlockSpec((8 * step, LANES), lambda n: (n, 0)),
            block, block, numbers,
        ] + [still(tables[name]) for name in ("lanes", "columns", "rows", "cols")],
        out_specs=[block, block],
        out_shape=[shape, shape],
        scratch_shapes=[vmem((rows, LANES))],
        compiler_params=pltpu.CompilerParams(dimension_semantics=("arbitrary",)),
    )(
        spectrum, fluxes, field, field_before, mean,
        *(tables[name] for name in ("lanes", "columns", "rows", "cols")),
    )
    return (fresh[:modes], update[:modes])


def solution(mesh):
    return jax.shard_map(
        chebyshev_step,
        mesh=mesh,
        in_specs=(
            P("sa", "gy", "gx"),
            P("sa", "gy", "gx"),
            P("sa", "gy", "gx"),
            P(None, ("gy", "sa"), "gx"),
            P(),
            P(),
            P(),
            P(),
        ),
        out_specs=(P("sa", "gy", "gx"), P("sa", "gy", "gx")),
        check_vma=False,
    )
```

```python
import functools
import math

import jax
import jax.numpy as jnp
import numpy as np
from jax import lax
from jax.experimental import pallas as pl
from jax.experimental.pallas import tpu as pltpu
from jax.sharding import PartitionSpec as P


HIGHEST = lax.Precision.HIGHEST
hermite_points = (
    0.0,
    -1.7320508075688772,
    1.7320508075688772,
    -1.355626179974266,
    1.355626179974266,
    -2.8569700138728056,
    2.8569700138728056,
)
storage_rate = 0.0004
relax_weight = 1.6
step_length = 0.3


LANES = 128
NODE_BLOCK = 768
LOG_DEPTH = 16
EARLY = 4
BF16 = jnp.bfloat16


def round_up(value, step):
    return -(-value // step) * step


def product(left, right):
    return jnp.dot(left, right, preferred_element_type=jnp.float32)


def split_two(block):
    high = block.astype(BF16)
    return (high, (block - high.astype(jnp.float32)).astype(BF16))


def split_three(block):
    high = block.astype(BF16)
    rest = block - high.astype(jnp.float32)
    middle = rest.astype(BF16)
    return (high, middle, (rest - middle.astype(jnp.float32)).astype(BF16))


def exact(left, right):
    return jnp.dot(left, right, precision=HIGHEST, preferred_element_type=jnp.float32)


def row_transform(block, pair_ref, rest_ref):
    high, middle, low = split_three(block)
    both = product(jnp.concatenate([high, middle], axis=1), pair_ref[...])
    both = both[:, :LANES] + both[:, LANES:]
    return both + product(jnp.concatenate([low, high], axis=1), rest_ref[...])


def col_transform(block, all_ref):
    high, middle, low = split_three(block)
    stack = jnp.concatenate([high, middle, high, middle, low, high], axis=0)
    return product(all_ref[...], stack)


def make_tables(sizes, per, mean, lane_ref, column_ref, far_ref, inverse, by_row, by_col, col_table, row_table):
    count_x, count_y = sizes
    half = LANES // 2
    column = lambda k, rows=LANES: jnp.broadcast_to(column_ref[:rows, k : k + 1], (rows, LANES))
    lanes = lambda k: lane_ref[k : k + 1, :]
    upright = 1.0 / (storage_rate + mean * (column(0) + lanes(5)))
    flat = 1.0 / (storage_rate + mean * (column(3) + lanes(2)))
    inverse[:, :LANES] = flat[:half]
    inverse[:, LANES:] = flat[:half]
    lane = lax.broadcasted_iota(jnp.int32, (LANES, LANES), 1)
    row = lax.broadcasted_iota(jnp.int32, (LANES, LANES), 0)
    for end in range(2):
        part = upright * column(1 + end)
        by_col[:LANES, end * LANES : (end + 1) * LANES] = jnp.where(lane < half, part, 0.0)
        by_col[LANES:, end * LANES : (end + 1) * LANES] = jnp.where(lane < half, 0.0, part)
        part = flat * column(4 + end)
        by_row[:, 2 * end * LANES : (2 * end + 1) * LANES] = jnp.where(row < half, part, 0.0)
        by_row[:, (2 * end + 1) * LANES : (2 * end + 2) * LANES] = jnp.where(row < half, 0.0, part)

    def tables(count, same, cross):
        shrink = [
            1.0 / (1.0 / mean + 2.0 * same - 2.0 * math.cos(n * math.pi / count) * cross)
            for n in range(1, count)
        ]
        sine = lambda a, b: math.sin(a * b % (2 * count) * math.pi / count)
        return [
            [
                sum((2.0 / count) * sine(n, a) * sine(n, b) * shrink[n - 1] for n in range(1, count))
                for b in range(1, count)
            ]
            for a in range(1, count)
        ]

    total = lambda a: jnp.sum(a, axis=0, keepdims=True)
    ends = column(1), column(2)
    found = tables(
        count_x, total(upright * ends[0] * ends[0]), total(upright * ends[0] * ends[1])
    )
    for a in range(count_x - 1):
        for b in range(count_x - 1):
            col_table[a, b : b + 1, :] = found[a][b]
    far = far_ref[0:1, :]
    wide = lambda k: jnp.broadcast_to(column_ref[:half, k : k + 1], (half, far.shape[1]))
    deep = 1.0 / (storage_rate + mean * (wide(3) + far))
    found = tables(
        count_y, total(deep * wide(4) * wide(4)), total(deep * wide(4) * wide(5))
    )
    depth = row_table.shape[1]
    where_row = lax.broadcasted_iota(jnp.int32, (depth, far.shape[1]), 0) // per
    for shift in range(-(count_y - 2), count_y - 1):
        table = jnp.zeros((depth, far.shape[1]), jnp.float32)
        for a in range(count_y - 1):
            if 0 <= a + shift < count_y - 1:
                table = jnp.where(where_row == a, found[a][a + shift], table)
        row_table[shift + count_y - 2] = table


def solve_fluxes(sizes, per, got, back, lane_ref, join_ref, by_row, by_col, col_table, row_table):
    count_x, count_y = sizes
    depth = row_table.shape[1]
    rows = count_y * per
    lanes = lambda k: lane_ref[k : k + 1, :]
    take = lambda block, kind: got[pl.ds(block * rows * 8 + kind, depth, stride=8), :]
    row = lax.broadcasted_iota(jnp.int32, (depth, LANES), 0)
    up = lambda a, by=1: pltpu.roll(a, (-by * per) % depth, 0)
    down = lambda a: jnp.where(row < per, 0.0, pltpu.roll(a, per, 0))
    blocks, cuts = range(count_x), range(1, count_x)

    def through_cols(first, last):
        jump = [first[cut] - last[cut - 1] for cut in cuts]
        return [
            sum(col_table[a, b : b + 1, :] * jump[b] for b in range(count_x - 1))
            for a in range(count_x - 1)
        ]

    fluxes = through_cols([take(b, 0) for b in blocks], [take(b, 1) for b in blocks])
    spread = [exact(flux, by_row[...]) for flux in fluxes]

    def at_row(block, end, half):
        part = slice((2 * end + half) * LANES, (2 * end + half + 1) * LANES)
        value = take(block, 2 + 2 * end + half)
        if block < count_x - 1:
            value = value + spread[block][:, part] * lanes(1)
        if block > 0:
            value = value - spread[block - 1][:, part] * lanes(0)
        return value

    jump = jnp.concatenate(
        [
            jnp.concatenate([up(at_row(b, 0, half)) - at_row(b, 1, half) for b in blocks], axis=1)
            for half in range(2)
        ],
        axis=0,
    )
    far = lax.dot_general(
        jump, join_ref[...], (((1,), (1,)), ((), ())), precision=HIGHEST,
        preferred_element_type=jnp.float32,
    )
    mixed = []
    for half in range(2):
        part = far[half * depth : (half + 1) * depth]
        mixed.append(sum(
            row_table[shift + count_y - 2] * (up(part, shift) if shift else part)
            for shift in range(-(count_y - 2), count_y - 1)
        ))
    near = exact(jnp.concatenate(mixed, axis=0), join_ref[...])
    through_rows = [
        [near[half * depth : (half + 1) * depth, b * LANES : (b + 1) * LANES] for half in range(2)]
        for b in blocks
    ]
    ends = []
    for b in blocks:
        reach = exact(jnp.concatenate(through_rows[b], axis=1), by_col[...])
        ends.append([
            lanes(4) * reach[:, end * LANES : (end + 1) * LANES]
            - lanes(3) * down(reach[:, end * LANES : (end + 1) * LANES])
            for end in range(2)
        ])
    more = through_cols([end[0] for end in ends], [end[1] for end in ends])
    fluxes = [a + b for a, b in zip(fluxes, more)]
    nothing = jnp.zeros((depth, LANES), jnp.float32)
    for b in blocks:
        left = fluxes[b - 1] if b > 0 else nothing
        right = fluxes[b] if b < count_x - 1 else nothing
        top = [down(part) for part in through_rows[b]]
        for kind, value in enumerate([left, right] + top + through_rows[b]):
            back[pl.ds(b * rows * 8 + kind, depth, stride=8), :] = value


def stacked(parts, depth):
    missing = depth - sum(part.shape[0] for part in parts)
    if missing:
        parts = parts + [jnp.zeros((missing,) + parts[0].shape[1:], parts[0].dtype)]
    return jnp.concatenate(parts, axis=0)


def node_kernel(
    sizes, field_ref, log_ref, node_ref, mode_ref, weight_ref,
    source_ref, mean_ref, pair_ref, rest_ref, all_ref, lane_ref, column_ref, far_ref, join_ref,
    spec_ref, flux_ref,
    lines, log_lines, log_sides, sides, total, line_op, log_op, basis_op, germ_op, weight_op,
    edge, value_prev, half_prev, flux_prev,
    home, spectrum, origin, traces, got, back, tall, join,
    inverse, by_row, by_col, col_table, row_table,
    block_field, field_cols, log_cols, picks, shares_of, degrees,
    load_sem, spec_sem, trace_send, trace_recv, flux_send, flux_recv,
    line_send, line_recv, halo_send, side_send, side_recv, log_send, log_recv, out_send, out_recv,
):
    count_x, count_y, shares, group = sizes
    modes, rows, width = field_ref.shape
    own_rows = rows // shares
    every = shares * modes
    below, above = own_rows, own_rows + 1
    blocks = basis_op.shape[0] // NODE_BLOCK
    x, y, share = (lax.axis_index(axis) for axis in ("gx", "gy", "sa"))
    first_y = jnp.logical_and(y == 0, share == 0)
    last_y = jnp.logical_and(y == count_y - 1, share == shares - 1)
    not_first, not_last = jnp.logical_not(first_y), jnp.logical_not(last_y)
    peer = lambda step: lax.rem(share + step, shares)

    def remote(source, target, send, recv, **place):
        return pltpu.make_async_remote_copy(
            src_ref=source, dst_ref=target, send_sem=send, recv_sem=recv,
            device_id=place, device_id_type=pl.DeviceIdType.MESH,
        )

    def arrived(target, recv):
        pltpu.make_async_copy(target, target, recv).wait()

    load_field = pltpu.make_async_copy(field_ref, block_field, load_sem.at[2])
    load_field.start()
    load_origin = pltpu.make_async_copy(source_ref, origin, load_sem.at[0])
    load_origin.start()
    load_join = pltpu.make_async_copy(join_ref, join, load_sem.at[1])
    load_join.start()

    barrier = pltpu.get_barrier_semaphore()
    greet = lambda **place: pl.semaphore_signal(
        barrier, inc=1, device_id=place, device_id_type=pl.DeviceIdType.MESH
    )
    for step in range(1, shares):
        greet(sa=peer(step))
    owners = count_x * count_y
    me = x * count_y + y
    other = lambda step: lax.rem(me + step, owners)
    at_owner = lambda owner: dict(gx=lax.div(owner, count_y), gy=lax.rem(owner, count_y))
    for step in range(1, owners):
        greet(**at_owner(other(step)))
    conditions = (
        (x > 0, dict(gx=x - 1)), (x < count_x - 1, dict(gx=x + 1)),
        (y > 0, dict(gy=y - 1)), (y < count_y - 1, dict(gy=y + 1)),
    )
    for condition, place in conditions:
        @pl.when(condition)
        def _():
            for step in range(1, shares):
                greet(sa=peer(step), **place)
    per = traces.shape[0] // 8 // owners
    plane = (count_x, count_y)
    beyond = got.shape[0] - traces.shape[0]
    if beyond:
        got[traces.shape[0] :, :] = jnp.zeros((beyond, LANES), jnp.float32)
    traces[...] = jnp.zeros_like(traces)

    total[...] = jnp.zeros_like(total)

    nodes_given = node_ref.shape[1]
    picks[...] = jnp.zeros_like(picks)
    picks[:, :nodes_given] = node_ref[...]
    shares_of[...] = jnp.zeros_like(shares_of)
    shares_of[:, :nodes_given] = weight_ref[...].reshape(1, nodes_given)
    degrees[...] = jnp.zeros_like(degrees)
    for start_at in range(0, every, LANES):
        width_at = min(LANES, every - start_at)
        degrees[start_at : start_at + mode_ref.shape[0], :width_at] = mode_ref[
            :, start_at : start_at + width_at
        ].astype(jnp.float32)
        here = slice(start_at, start_at + LANES)
        degrees[here, :] = jnp.transpose(degrees[here, :])

    sides_met = sum(condition.astype(jnp.int32) for condition, _ in conditions)
    pl.semaphore_wait(barrier, owners - 1 + (shares - 1) * (1 + sides_met))

    remote_copies = []

    def start(condition, copy):
        remote_copies.append((condition, copy))
        if condition is None:
            copy.start()
        else:
            pl.when(condition)(copy.start)

    row_of = lambda row: field_ref.at[:, row, :]
    flat_next = jnp.where(share == shares - 1, y + 1, y), lax.rem(share + 1, shares)
    flat_last = jnp.where(share == 0, y - 1, y), lax.rem(share + shares - 1, shares)
    start(y > 0, remote(
        row_of(0), lines.at[below, share], halo_send.at[0], line_recv.at[below, share],
        gy=y - 1, sa=jnp.int32(shares - 1),
    ))
    start(y < count_y - 1, remote(
        row_of(rows - 1), lines.at[above, share], halo_send.at[1], line_recv.at[above, share],
        gy=y + 1, sa=jnp.int32(0),
    ))
    for step in range(1, shares):
        to = peer(step)
        start(to > 0, remote(
            row_of(jnp.maximum(to * own_rows - 1, 0)), lines.at[above, share],
            halo_send.at[2 * step], line_recv.at[above, share], sa=to,
        ))
        start(to < shares - 1, remote(
            row_of(jnp.minimum((to + 1) * own_rows, rows - 1)), lines.at[below, share],
            halo_send.at[2 * step + 1], line_recv.at[below, share], sa=to,
        ))
    own_above = pltpu.make_async_copy(
        row_of(jnp.maximum(share * own_rows - 1, 0)), lines.at[above, share],
        line_recv.at[above, share],
    )
    own_below = pltpu.make_async_copy(
        row_of(jnp.minimum((share + 1) * own_rows, rows - 1)), lines.at[below, share],
        line_recv.at[below, share],
    )
    pl.when(share > 0)(own_above.start)
    pl.when(share < shares - 1)(own_below.start)
    def line_copy(row, step):
        to = peer(step)
        return remote(
            row_of(to * own_rows + row), lines.at[row, share], line_send.at[row, step],
            line_recv.at[row, share], sa=to,
        )

    def send_lines(row, carry):
        for step in range(1, shares):
            line_copy(row, step).start()
        pltpu.make_async_copy(
            row_of(share * own_rows + row), lines.at[row, share], line_recv.at[row, share]
        ).start()
        return carry

    early = min(EARLY, own_rows)
    lax.fori_loop(0, early, send_lines, 0)
    pairs = modes // 2
    unroll = max(n for n in range(1, 21) if pairs % n == 0)
    pick_row = lax.broadcasted_iota(jnp.int32, (16, 2 * LANES), 0)
    pick_lane = lax.broadcasted_iota(jnp.int32, (16, 2 * LANES), 1) % LANES
    first_pick = jnp.logical_and(pick_row == 0, pick_lane == 0)
    last_pick = jnp.logical_and(pick_row == 1, pick_lane == LANES - 1)
    pick = jnp.where(jnp.logical_or(first_pick, last_pick), 1.0, 0.0).astype(BF16)

    def columns_of(block):
        return lax.dot_general(
            pick, jnp.concatenate(split_two(block), axis=1), (((1,), (1,)), ((), ())),
            preferred_element_type=jnp.float32,
        )

    log_cols[...] = jnp.zeros_like(log_cols)
    for level in range(log_ref.shape[0]):
        found = columns_of(log_ref[level])
        for end in range(2):
            log_cols[end, level : level + 1, :own_rows] = found[end : end + 1, :]
    load_field.wait()

    left_lanes = lax.broadcasted_iota(jnp.int32, (1, LANES), 1) < rows

    def take_columns(index, carry):
        for pair in range(unroll):
            mode = 2 * (index * unroll + pair)
            found = columns_of(block_field[pl.ds(mode, 2)].reshape(2 * rows, LANES))
            for half in range(2):
                part = pltpu.roll(found, LANES - rows, 1) if half else found
                for end in range(2):
                    field_cols[end, pl.ds(mode + half, 1), :] = part[end : end + 1, :]
                both = jnp.where(left_lanes, part[0:1, :], pltpu.roll(part, rows, 1)[1:2, :])
                field_cols[2, pl.ds(mode + half, 1), :] = both
        return carry

    lax.fori_loop(0, pairs // unroll, take_columns, 0)
    log_copies = (
        (not_last, log_ref.at[:, own_rows - 1, :], log_lines.at[1], 0,
         dict(gy=flat_next[0], sa=flat_next[1])),
        (not_first, log_ref.at[:, 0, :], log_lines.at[0], 1,
         dict(gy=flat_last[0], sa=flat_last[1])),
        (x < count_x - 1, log_cols.at[1], log_sides.at[0], 2, dict(gx=x + 1)),
        (x > 0, log_cols.at[0], log_sides.at[1], 3, dict(gx=x - 1)),
    )
    for condition, source, target, slot, place in log_copies:
        start(condition, remote(source, target, log_send.at[slot], log_recv.at[slot], **place))
    for step in range(shares):
        to = peer(step)
        if step:
            start(None, remote(
                field_cols.at[2], sides.at[0, share], side_send.at[step, 0],
                side_recv.at[0, share], sa=to,
            ))
        else:
            pltpu.make_async_copy(
                field_cols.at[2], sides.at[0, share], side_recv.at[0, share]
            ).start()
        start(x > 0, remote(
            field_cols.at[0], sides.at[2, share], side_send.at[step, 2],
            side_recv.at[2, share], gx=x - 1, sa=to,
        ))
        start(x < count_x - 1, remote(
            field_cols.at[1], sides.at[3, share], side_send.at[step, 3],
            side_recv.at[3, share], gx=x + 1, sa=to,
        ))

    lax.fori_loop(early, own_rows, send_lines, 0)
    def make_basis(block, carry):
        lanes = pl.ds(pl.multiple_of(block * LANES, LANES), LANES)
        picked = picks[:, lanes]
        germs = jnp.zeros(picked.shape, jnp.float32)
        for level, point in enumerate(hermite_points):
            germs = jnp.where(picked == level, point, germs)
        square = germs * germs
        second = (square - 1.0) / math.sqrt(2.0)
        third = (square * germs - 3.0 * germs) / math.sqrt(6.0)
        values = jnp.ones((every, LANES), jnp.float32)
        for germ in range(germs.shape[0]):
            degree = jnp.broadcast_to(degrees[:every, germ : germ + 1], (every, LANES))
            at = lambda table: jnp.broadcast_to(table[germ : germ + 1, :], (every, LANES))
            values = values * jnp.where(
                degree == 0, 1.0,
                jnp.where(degree == 1, at(germs), jnp.where(degree == 2, at(second), at(third))),
            )
        high, low = split_two(values)
        wide = lambda a: a.astype(jnp.float32)
        stack = stacked([wide(high), wide(high), wide(low)], basis_op.shape[1])
        basis_op[lanes, :] = jnp.transpose(stack).astype(BF16)
        high, low = split_two(values * (2.0 * shares_of[:, lanes]))
        weight_op[:every, lanes] = high
        weight_op[every:, lanes] = low
        spread = stacked([-jnp.ones((1, LANES), jnp.float32), -germs], LOG_DEPTH)
        high, low = split_two(spread)
        stack = stacked([wide(high), wide(high), wide(low)], LANES)
        germ_op[lanes, :] = jnp.transpose(stack).astype(BF16)
        return carry

    lax.fori_loop(0, basis_op.shape[0] // LANES, make_basis, 0)

    def log_stack(block):
        high, low = split_two(stacked([block], LOG_DEPTH))
        return stacked([high, low, high], LANES)

    def field_stack(block):
        high, low = split_two(block)
        return stacked([high, low, high], line_op.shape[1])

    for condition, _, target, slot, _ in (
        (not_first, None, log_lines.at[1], 0, None), (not_last, None, log_lines.at[0], 1, None),
        (x > 0, None, log_sides.at[0], 2, None), (x < count_x - 1, None, log_sides.at[1], 3, None),
    ):
        @pl.when(condition)
        def _():
            arrived(target, log_recv.at[slot])

    def make_log(row, carry):
        log_op[row] = log_stack(log_ref[:, row, :])
        return carry

    lax.fori_loop(0, own_rows, make_log, 0)
    log_op[below] = log_stack(
        jnp.where(last_y, log_ref[:, own_rows - 1, :], log_lines[0])
    )
    log_op[above] = log_stack(jnp.where(first_y, log_ref[:, 0, :], log_lines[1]))

    def at_nodes(nodes, field, logs):
        return (product(basis_op[nodes, :], field), jnp.exp(product(germ_op[nodes, :], logs)))

    def flux(later, earlier, half_later, half_earlier):
        return (later - earlier) * pl.reciprocal(half_later + half_earlier)

    def project(nodes, applied):
        high = applied.astype(BF16)
        rest = applied - high.astype(jnp.float32)
        middle = rest.astype(BF16)
        low = (rest - middle.astype(jnp.float32)).astype(BF16)
        both = product(weight_op[:, nodes], high) + product(weight_op[:, nodes], middle)
        return both[:every] + both[every:] + product(weight_op[:every, nodes], low)

    node_slice = lambda block: pl.ds(pl.multiple_of(block * NODE_BLOCK, NODE_BLOCK), NODE_BLOCK)

    for kind, condition in ((0, None), (2, x < count_x - 1), (3, x > 0)):
        for source in range(shares):
            wait = lambda: arrived(sides.at[kind, source], side_recv.at[kind, source])
            wait() if condition is None else pl.when(condition)(wait)
    flat = lambda ref: ref.reshape(every, LANES)
    turn = lax.rem(LANES - share * own_rows, LANES)
    side = [pltpu.roll(flat(sides[kind]), turn, 1) for kind in (0, 0, 2, 3)]
    side[1] = pltpu.roll(side[1], LANES - rows, 1)
    log_first, log_last = log_cols[0], log_cols[1]
    before = jnp.where(x == 0, side[0], side[3])
    after = jnp.where(x == count_x - 1, side[1], side[2])
    log_before = jnp.where(x == 0, log_first, log_sides[0])
    log_after = jnp.where(x == count_x - 1, log_last, log_sides[1])

    def beside(low_part, high_part):
        lane = lax.broadcasted_iota(jnp.int32, low_part.shape, 1)
        return jnp.where(lane < own_rows, low_part, pltpu.roll(high_part, own_rows, 1))

    line_op[0, :, :LANES] = field_stack(beside(before, side[1]))
    line_op[0, :, LANES:] = field_stack(beside(side[0], after))
    log_edge = jnp.concatenate(
        [log_stack(beside(log_before, log_last)), log_stack(beside(log_first, log_after))], axis=1
    )
    edge[...] = jnp.zeros_like(edge)

    def make_edge(block, carry):
        nodes = node_slice(block)
        values, halves = at_nodes(nodes, line_op[0], log_edge)
        edge[...] += project(nodes, flux(
            values[:, LANES:], values[:, :LANES], halves[:, LANES:], halves[:, :LANES]
        ))
        return carry

    lax.fori_loop(0, blocks, make_edge, 0)

    def wait_line(row):
        for source in range(shares):
            arrived(lines.at[row, source], line_recv.at[row, source])

    wait_line(0)
    pl.when(not_first)(lambda: wait_line(above))
    line = flat(lines[0])
    line_op[0, :, :LANES] = field_stack(jnp.where(first_y, line, flat(lines[above])))
    line_op[0, :, LANES:] = field_stack(line)

    def begin(block, carry):
        nodes = node_slice(block)
        logs = jnp.concatenate([log_op[above], log_op[0]], axis=1)
        values, halves = at_nodes(nodes, line_op[0], logs)
        value_prev[nodes, :] = values[:, LANES:]
        half_prev[nodes, :] = halves[:, LANES:]
        flux_prev[nodes, :] = flux(
            values[:, LANES:], values[:, :LANES], halves[:, LANES:], halves[:, :LANES]
        )
        return carry

    lax.fori_loop(0, blocks, begin, 0)

    home_row = lambda row: home.at[pl.ds(row * modes, modes), :]

    def out_copy(row, step):
        to = peer(step)
        return remote(
            total.at[row, to], home_row(share * own_rows + row), out_send.at[row, step],
            out_recv.at[row, share], sa=to,
        )

    def own_copy(row):
        return pltpu.make_async_copy(
            total.at[row, share], home_row(share * own_rows + row), out_recv.at[row, share]
        )

    def take_origin(index, carry):
        for pair in range(unroll):
            one_origin(index * unroll + pair)
        return carry

    def one_origin(pair):
        block = origin[pl.ds(2 * pair, 2)].reshape(2 * rows, LANES)
        block = row_transform(block, pair_ref, rest_ref)
        spectrum[pair] = col_transform(
            jnp.concatenate([block[:rows], block[rows:]], axis=1), all_ref
        )

    groups = own_rows // group

    def take_group(index, carry):
        base = index * group
        for ahead in range(1, group + 1):
            row = base + ahead
            if ahead < group:
                wait_line(row)
            else:
                pl.when(jnp.logical_or(row < own_rows, not_last))(lambda: wait_line(row))
            line = flat(lines[row])
            if ahead == group:
                line = jnp.where(
                    jnp.logical_and(row == own_rows, last_y), flat(lines[row - 1]), line
                )
            place = pl.ds((ahead - 1) % 2 * LANES, LANES)
            line_op[(ahead - 1) // 2, :, place] = field_stack(line)

        def take_nodes(block, carry):
            nodes = node_slice(block)
            value, half, flux_up = value_prev[nodes, :], half_prev[nodes, :], flux_prev[nodes, :]
            inside = lax.broadcasted_iota(jnp.int32, value.shape, 1) < LANES - 1
            for pair in range(group // 2):
                row = base + 2 * pair
                logs = jnp.concatenate([log_op[row + 1], log_op[row + 2]], axis=1)
                values, halves = at_nodes(nodes, line_op[pair], logs)
                applied = []
                for here in range(2):
                    value_next = values[:, here * LANES : (here + 1) * LANES]
                    half_next = halves[:, here * LANES : (here + 1) * LANES]
                    flux_down = flux(value_next, value, half_next, half)
                    across = jnp.where(
                        inside,
                        flux(
                            pltpu.roll(value, LANES - 1, 1), value,
                            pltpu.roll(half, LANES - 1, 1), half,
                        ),
                        0.0,
                    )
                    applied.append(
                        (0.5 * storage_rate) * value
                        - (across - pltpu.roll(across, 1, 1)) - (flux_down - flux_up)
                    )
                    value, half, flux_up = value_next, half_next, flux_down
                sums = project(nodes, jnp.concatenate(applied, axis=1))
                parts = sums.reshape(shares, modes, 2 * LANES)
                total[row] += parts[:, :, :LANES]
                total[row + 1] += parts[:, :, LANES:]
            value_prev[nodes, :] = value
            half_prev[nodes, :] = half
            flux_prev[nodes, :] = flux_up
            return carry

        lax.fori_loop(0, blocks, take_nodes, 0, unroll=True)
        lane = lax.broadcasted_iota(jnp.int32, (every, LANES), 1)
        for step in range(group):
            row = base + step
            left = pltpu.roll(edge[...], lax.rem(LANES - row, LANES), 1)
            right = pltpu.roll(edge[...], LANES - 1 - own_rows - row, 1)
            change = jnp.where(lane == 0, left, 0.0) - jnp.where(lane == LANES - 1, right, 0.0)
            line = row_transform(flat(total[row]) + change, pair_ref, rest_ref)
            total[row] = line.reshape(shares, modes, LANES)
        for step in range(group):
            row = base + step
            for to in range(1, shares):
                out_copy(row, to).start()
            own_copy(row).start()
        return carry

    lax.fori_loop(0, groups, take_group, 0)
    make_tables(
        plane, per, mean_ref[0], lane_ref, column_ref, far_ref,
        inverse, by_row, by_col, col_table, row_table,
    )
    load_origin.wait()
    lax.fori_loop(0, pairs // unroll, take_origin, 0)

    def arrive(row, carry):
        for step in range(1, shares):
            source = peer(step)
            arrived(home_row(source * own_rows + row), out_recv.at[row, source])
        own_copy(row).wait()
        return carry

    lax.fori_loop(0, own_rows, arrive, 0)

    def take_pair(pair, columns):
        line = [home[pl.ds(2 * pair + half, rows, stride=modes), :] for half in range(2)]
        line = col_transform(jnp.concatenate(line, axis=1), all_ref)
        line = spectrum[pair] - line
        spectrum[pair] = line
        alone = line * inverse[...]
        trace = pl.ds(8 * pair, 8)
        lane = lax.broadcasted_iota(jnp.int32, (LANES, LANES), 1)
        result = []
        for end in range(2):
            ends = jnp.broadcast_to(column_ref[:rows, 4 + end : 5 + end], (rows, 2 * LANES))
            result.append(jnp.sum(alone * ends, axis=0, keepdims=True))
            upright = jnp.concatenate([alone[:, :LANES], alone[:, LANES:]], axis=0)
            upright = jnp.sum(upright * lane_ref[end : end + 1, :], axis=1, keepdims=True)
            columns = jnp.where(lane == end * (LANES // 2) + pair, upright, columns)
        blank = jnp.zeros((2, LANES), jnp.float32)
        traces[trace, :] = jnp.concatenate(
            [blank, result[0][:, :LANES], result[0][:, LANES:],
             result[1][:, :LANES], result[1][:, LANES:], blank], axis=0
        )
        return columns

    def take_pairs(index, columns):
        for pair in range(unroll):
            columns = take_pair(index * unroll + pair, columns)
        return columns

    columns = lax.fori_loop(
        0, pairs // unroll, take_pairs, jnp.zeros((LANES, LANES), jnp.float32)
    )
    tall[...] = jnp.transpose(columns)
    for end in range(2):
        traces[pl.ds(end, pairs, stride=8), :] = tall[pl.ds(end * (LANES // 2), pairs), :]
    save = pltpu.make_async_copy(spectrum, spec_ref, spec_sem)
    save.start()

    piece = lambda owner: pl.ds(owner * per * 8, per * 8)

    def trace_copy(step):
        to = other(step)
        return remote(
            traces.at[piece(to), :], got.at[piece(me), :], trace_send.at[step],
            trace_recv.at[me], **at_owner(to),
        )

    def flux_copy(step):
        to = other(step)
        return remote(
            back.at[piece(to), :], flux_ref.at[piece(me), :], flux_send.at[step],
            flux_recv.at[me], **at_owner(to),
        )

    used = lambda owner: owner * per < pairs
    for step in range(1, owners):
        pl.when(used(other(step)))(trace_copy(step).start)
    got[piece(me), :] = traces[piece(me), :]
    load_join.wait()
    for step in range(1, owners):
        @pl.when(used(me))
        def _():
            arrived(got.at[piece(other(step)), :], trace_recv.at[other(step)])
    solve_fluxes(plane, per, got, back, lane_ref, join, by_row, by_col, col_table, row_table)
    for step in range(1, owners):
        pl.when(used(me))(flux_copy(step).start)
    own_flux = pltpu.make_async_copy(
        back.at[piece(me), :], flux_ref.at[piece(me), :], flux_recv.at[me]
    )
    own_flux.start()

    def sent(row, carry):
        for step in range(1, shares):
            line_copy(row, step).wait_send()
            out_copy(row, step).wait_send()
        return carry

    lax.fori_loop(0, own_rows, sent, 0)
    for condition, copy in remote_copies:
        if condition is None:
            copy.wait_send()
        else:
            pl.when(condition)(copy.wait_send)
    save.wait()
    own_flux.wait()
    for step in range(1, owners):
        pl.when(used(other(step)))(trace_copy(step).wait_send)
        pl.when(used(me))(flux_copy(step).wait_send)

        @pl.when(used(other(step)))
        def _():
            arrived(flux_ref.at[piece(other(step)), :], flux_recv.at[other(step)])


def finish_kernel(
    spec_ref, flux_ref, now_ref, before_ref, mean_ref, lane_ref, column_ref, rows_ref, cols_ref,
    fresh_ref, update_ref, inverse,
):
    rows = spec_ref.shape[1]
    column = lambda k: jnp.broadcast_to(column_ref[:rows, k : k + 1], (rows, LANES))

    @pl.when(pl.program_id(0) == 0)
    def start():
        inverse[...] = 1.0 / (storage_rate + mean_ref[0] * (column(3) + lane_ref[2:3, :]))

    upright = jnp.transpose(flux_ref[...])
    for pair in range(spec_ref.shape[0]):
        parts = []
        for half in range(2):
            beside = lambda kind: jnp.broadcast_to(
                upright[half * rows : (half + 1) * rows, 8 * pair + kind : 8 * pair + kind + 1],
                (rows, LANES),
            )
            over = lambda kind: flux_ref[8 * pair + kind : 8 * pair + kind + 1, :]
            part = spec_ref[pair, :, half * LANES : (half + 1) * LANES]
            part = part + (beside(1) * lane_ref[1:2, :] - beside(0) * lane_ref[0:1, :])
            part = part + (column(5) * over(4 + half) - column(4) * over(2 + half))
            parts.append(part * inverse[...])
        high, low = split_two(jnp.concatenate(parts, axis=1))
        part = product(rows_ref[...], jnp.concatenate([high, low, high], axis=0))
        high, low = split_two(jnp.concatenate([part[:, :LANES], part[:, LANES:]], axis=0))
        part = product(jnp.concatenate([high, low], axis=1), cols_ref[...])
        part = (part[:, :LANES] + part[:, LANES:]).reshape(2, rows, LANES)
        mode = slice(2 * pair, 2 * pair + 2)
        update_ref[mode] = part
        before = before_ref[mode]
        fresh_ref[mode] = before + relax_weight * (now_ref[mode] - before + step_length * part)


def cosine_table(length):
    freq, cells = np.arange(length)[:, None], np.arange(length)[None, :]
    factor = np.where(freq == 0, math.sqrt(1.0 / length), math.sqrt(2.0 / length))
    return factor * np.cos((freq * (2 * cells + 1) % (4 * length)) * (math.pi / (2 * length)))


def pieces(table):
    found, rest = [], table.astype(np.float32)
    for _ in range(3):
        found.append(rest.astype(BF16))
        rest = rest - found[-1].astype(np.float32)
    return found


def constant_tables(count_x, rows, width):
    eigen = lambda count: 2.0 - 2.0 * np.cos(np.arange(count) * (math.pi / count))
    row_table, col_table = cosine_table(rows), cosine_table(width)
    far_table = cosine_table(count_x * width)
    join = np.einsum("kix,lx->kil", far_table.reshape(-1, count_x, width), col_table)
    twice = lambda a: np.concatenate([a, a])
    lanes = [
        col_table[:, 0], col_table[:, -1], eigen(width),
        twice(row_table[:, 0]), twice(row_table[:, -1]), twice(eigen(rows)),
    ]
    columns = [lanes[2], lanes[0], lanes[1], lanes[5], lanes[3], lanes[4]]
    grow = lambda a: np.pad(np.stack(a), ((0, 8 - len(a)), (0, 0))).astype(np.float32)
    high, middle, low = pieces(col_table.T)
    front = pieces(col_table)
    pair = np.block([[high, middle], [high, middle]])
    rest = np.concatenate([high, low])
    back = np.block([[front[0], front[1]], [front[0], np.zeros_like(high)]])
    high, middle, low = pieces(row_table)
    every = np.concatenate([high, high, middle, middle, high, low], axis=1)
    high, low, _ = pieces(row_table.T)
    rows_back = np.concatenate([high, high, low], axis=1)
    return dict(
        pair=pair, rest=rest, every=every, lanes=grow(lanes), columns=grow(columns).T.copy(),
        far=grow([eigen(count_x * width)]), join=join.reshape(len(far_table), -1).astype(np.float32),
        rows=rows_back, cols=back,
    )


def chebyshev_step(
    field, field_before, source, log_fields, weights, mean_perm, node_index, mode_index
):
    modes, rows, width = field.shape
    count_x, count_y, shares = (lax.axis_size(axis) for axis in ("gx", "gy", "sa"))
    padded = round_up(modes, 16)
    grow = lambda a, size, dim: jnp.pad(
        a, [(0, size - a.shape[d] if d == dim else 0) for d in range(a.ndim)]
    )
    field, field_before, source = (grow(a, padded, 0) for a in (field, field_before, source))
    mean = mean_perm.reshape(1)
    tables = constant_tables(count_x, rows, width)
    pairs, owners = padded // 2, count_x * count_y
    per = -(-pairs // owners)
    depth_solve = round_up(count_y * per, 8)
    extra = 8 * (depth_solve - count_y * per)
    own_rows = rows // shares
    nodes = node_index.shape[0]
    all_nodes = round_up(nodes, NODE_BLOCK)
    modes_of = grow(mode_index.reshape(shares, modes, -1), padded, 1).reshape(shares * padded, -1)
    levels = log_fields.shape[0]
    group = math.gcd(own_rows, 8)
    every = shares * padded
    depth = round_up(3 * every, LANES)
    slots = own_rows + 2
    vmem = lambda shape, kind=jnp.float32: pltpu.VMEM(shape, kind)
    dma = lambda *shape: pltpu.SemaphoreType.DMA(shape)
    place = pl.BlockSpec(memory_space=pl.ANY)
    whole = pl.BlockSpec(memory_space=pltpu.VMEM)
    numbers = pl.BlockSpec(memory_space=pltpu.SMEM)
    spectrum, fluxes = pl.pallas_call(
        functools.partial(node_kernel, (count_x, count_y, shares, group)),
        in_specs=[place, whole, whole, whole, whole]
        + [place, numbers] + [whole] * 6 + [place],
        out_specs=[place, place],
        out_shape=[
            jax.ShapeDtypeStruct((pairs, rows, 2 * width), jnp.float32),
            jax.ShapeDtypeStruct((owners * per * 8, LANES), jnp.float32),
        ],
        scratch_shapes=[
            vmem((slots, shares, padded, LANES)),
            vmem((2, levels, LANES)),
            vmem((2, levels, LANES)),
            vmem((4, shares, padded, LANES)),
            vmem((own_rows, shares, padded, LANES)),
            vmem((group // 2, depth, 2 * LANES), BF16),
            vmem((slots, LANES, LANES), BF16),
            vmem((all_nodes, depth), BF16),
            vmem((all_nodes, LANES), BF16),
            vmem((2 * every, all_nodes), BF16),
            vmem((every, LANES)),
            vmem((all_nodes, LANES)),
            vmem((all_nodes, LANES)),
            vmem((all_nodes, LANES)),
            vmem((rows * padded, LANES)),
            vmem((pairs, rows, 2 * LANES)),
            vmem((padded, rows, LANES)),
            vmem((owners * per * 8, LANES)),
            vmem((owners * per * 8 + extra, LANES)),
            vmem((owners * per * 8 + extra, LANES)),
            vmem((LANES, LANES)),
            vmem(tables["join"].shape),
            vmem((rows, 2 * LANES)),
            vmem((LANES, 4 * LANES)),
            vmem((2 * LANES, 2 * LANES)),
            vmem((count_x - 1, round_up(count_x - 1, 8), LANES)),
            vmem((2 * count_y - 3, depth_solve, count_x * width)),
            vmem((padded, rows, LANES)),
            vmem((3, padded, LANES)),
            vmem((2, levels, LANES)),
            vmem((node_index.shape[1], all_nodes), jnp.int32),
            vmem((1, all_nodes)),
            vmem((round_up(every, LANES), LANES)),
            dma(3), pltpu.SemaphoreType.DMA, dma(owners), dma(owners), dma(owners), dma(owners),
            dma(own_rows, shares), dma(slots, shares), dma(2 * shares), dma(shares, 4),
            dma(4, shares), dma(4), dma(4), dma(own_rows, shares), dma(own_rows, shares),
        ],
        compiler_params=pltpu.CompilerParams(
            collective_id=0, has_side_effects=True, vmem_limit_bytes=56 * 1024 * 1024
        ),
    )(
        field, log_fields, node_index.T, modes_of.T, weights, source, mean,
        *(tables[name] for name in ("pair", "rest", "every", "lanes", "columns", "far", "join")),
    )
    step = math.gcd(pairs, 20)
    block = pl.BlockSpec((2 * step, rows, width), lambda n: (n, 0, 0))
    still = lambda a: pl.BlockSpec(a.shape, lambda n: (0,) * a.ndim)
    shape = jax.ShapeDtypeStruct(field.shape, jnp.float32)
    fresh, update = pl.pallas_call(
        finish_kernel,
        grid=(pairs // step,),
        in_specs=[
            pl.BlockSpec((step, rows, 2 * width), lambda n: (n, 0, 0)),
            pl.BlockSpec((8 * step, LANES), lambda n: (n, 0)),
            block, block, numbers,
        ] + [still(tables[name]) for name in ("lanes", "columns", "rows", "cols")],
        out_specs=[block, block],
        out_shape=[shape, shape],
        scratch_shapes=[vmem((rows, LANES))],
        compiler_params=pltpu.CompilerParams(dimension_semantics=("arbitrary",)),
    )(
        spectrum, fluxes, field, field_before, mean,
        *(tables[name] for name in ("lanes", "columns", "rows", "cols")),
    )
    return (fresh[:modes], update[:modes])


def solution(mesh):
    return jax.shard_map(
        chebyshev_step,
        mesh=mesh,
        in_specs=(
            P("sa", "gy", "gx"),
            P("sa", "gy", "gx"),
            P("sa", "gy", "gx"),
            P(None, ("gy", "sa"), "gx"),
            P(),
            P(),
            P(),
            P(),
        ),
        out_specs=(P("sa", "gy", "gx"), P("sa", "gy", "gx")),
        check_vma=False,
    )
```
